32 devices in a mesh: dp: 2 (over y), ctx: 4 (over x, core), tp: 4 (over z).
Axes of the slice: x: 2, y: 2, z: 4, core: 2. Of those that a mesh axis runs over, the one named last changes fastest.
Arguments:
- tokens: bfloat16 [2, 2048, 1024], P('dp', ('ctx', 'tp')), may hold values from -6 to 6
- attention_gain: float32 [1024], replicated, may hold values from 0.5 to 1.5
- query_weight: bfloat16 [1024, 1024], P(('dp', 'ctx'), 'tp'), may hold values from -0.1875 to 0.1875
- key_value_weight: bfloat16 [1024, 1024], P(('dp', 'ctx'), 'tp'), may hold values from -0.1875 to 0.1875
- query_gain: float32 [64], replicated, may hold values from 0.5 to 2.5, as said below
- key_gain: float32 [64], replicated, may hold values from 0.5 to 2.5, as said below
- output_weight: bfloat16 [1024, 1024], P('tp', ('dp', 'ctx')), may hold values from -3 to 3
- ffn_gain: float32 [1024], replicated, may hold values from 0.5 to 1.5
- gate_weight: bfloat16 [1024, 4608], P(('dp', 'ctx'), 'tp'), may hold values from -0.1875 to 0.1875
- up_weight: bfloat16 [1024, 4608], P(('dp', 'ctx'), 'tp'), may hold values from -0.1875 to 0.1875
- down_weight: bfloat16 [4608, 1024], P('tp', ('dp', 'ctx')), may hold values from -0.09375 to 0.09375
- cotangent: bfloat16 [2, 2048, 1024], P('dp', ('ctx', 'tp')), may hold values from -6 to 6
Outputs:
- block_out: bfloat16 [2, 2048, 1024], P('dp', ('ctx', 'tp'))
- grad_tokens: float32 [2, 2048, 1024], P('dp', ('ctx', 'tp'))
- softmax_logsumexp: float32 [2, 16, 2048], P('dp', 'tp', 'ctx')
- grad_attention_gain: float32 [1024], replicated
- grad_query_weight: float32 [1024, 1024], P(('dp', 'ctx'), 'tp')
- grad_keyval_weight: float32 [1024, 1024], P(('dp', 'ctx'), 'tp')
- grad_query_gain: float32 [64], replicated
- grad_key_gain: float32 [64], replicated
- grad_output_weight: float32 [1024, 1024], P('tp', ('dp', 'ctx'))
- grad_ffn_gain: float32 [1024], replicated
- grad_gate_weight: float32 [1024, 4608], P(('dp', 'ctx'), 'tp')
- grad_up_weight: float32 [1024, 4608], P(('dp', 'ctx'), 'tp')
- grad_down_weight: float32 [4608, 1024], P('tp', ('dp', 'ctx'))
The draws below stay inside these ranges and needn't reach their ends.
Inputs may be any that keep to these rules, and one draw needn't show every extreme that they name: `query_gain`: positive scales of the 64 channels of a normalized query. `key_gain`: positive scales of the 64 channels of a normalized key.
All inputs are finite; a program needn't handle non-finite values.
Results may differ from the reference program's by a relative error of at most 0.015.
The reference program's roundings to bfloat16 on the way count: a program that leaves them out, or rounds other values in their place, can miss the bound.
Values may be sent and summed in bfloat16 or wider, within the bound.
No kernel may reach another device: no remote copies, remote signals or barrier semaphores. Data moves between devices by JAX's collectives and lax.ppermute only.
A program may use at most 128 MiB of HBM per device.

```python
import math
import jax
import jax.numpy as jnp
from jax import lax

MODEL_WIDTH = 1024
QUERY_HEADS = 16
KEY_VALUE_HEADS = 8
HEAD_SIZE = 64
FF = 4608
TOKENS_PER_SHARD = 512
SEQS = 2
SEQUENCE_LENGTH = 2048


def channel_scales(key):
    uniform_vals = jax.random.uniform(key, (HEAD_SIZE,), jnp.float32)
    return jnp.exp(math.log(0.5) + uniform_vals * math.log(4.0))


def draw_query_gain(key, part):
    return channel_scales(jax.random.fold_in(key, 101))


def draw_key_gain(key, part):
    return channel_scales(jax.random.fold_in(key, 202))


def shard_levels(rng, shape, cuts, low, high):
    level = 1.0
    for position, blocks in cuts:
        draws = jax.random.uniform(jax.random.fold_in(jax.random.fold_in(rng, 6), position), (blocks,), jnp.float32, low / len(cuts), high / len(cuts))
        level = level * jnp.repeat(jnp.exp(draws), shape[position] // blocks).reshape((-1,) + (1,) * (len(shape) - 1 - position))
    return level


def normal_values(own_key, dims, spread, bound, pieces=(), kind=jnp.bfloat16):
    values = spread * jax.random.normal(own_key, dims, jnp.float32)
    if pieces:
        values = values * shard_levels(own_key, dims, pieces, -0.22, 0.18)
    return jnp.clip(values, -bound, bound).astype(kind)


def setup_inputs(seed: int = 0) -> dict:
    splits = jax.random.split(jax.random.key(seed), 13)
    return {
        "tokens": normal_values(splits[0], (SEQS, SEQUENCE_LENGTH, MODEL_WIDTH), 1.0, 6.0, ((0, 2), (1, 16))),
        "attention_gain": jnp.clip(1.0 + 0.1 * jax.random.normal(splits[1], (MODEL_WIDTH,), jnp.float32), 0.5, 1.5),
        "query_weight": normal_values(splits[2], (MODEL_WIDTH, QUERY_HEADS * HEAD_SIZE), MODEL_WIDTH ** -0.5, 0.1875, ((0, 8), (1, 4))),
        "key_value_weight": normal_values(splits[3], (MODEL_WIDTH, KEY_VALUE_HEADS * 2 * HEAD_SIZE), MODEL_WIDTH ** -0.5, 0.1875, ((0, 8), (1, 4))),
        "query_gain": draw_query_gain(jax.random.fold_in(splits[12], 71), 0),
        "key_gain": draw_key_gain(jax.random.fold_in(splits[12], 71), 0),
        "output_weight": normal_values(splits[6], (QUERY_HEADS * HEAD_SIZE, MODEL_WIDTH), 4 ** -0.5, 3.0, ((0, 4), (1, 8))),
        "ffn_gain": jnp.clip(1.0 + 0.1 * jax.random.normal(splits[7], (MODEL_WIDTH,), jnp.float32), 0.5, 1.5),
        "gate_weight": normal_values(splits[8], (MODEL_WIDTH, FF), MODEL_WIDTH ** -0.5, 0.1875, ((0, 8), (1, 4))),
        "up_weight": normal_values(splits[9], (MODEL_WIDTH, FF), MODEL_WIDTH ** -0.5, 0.1875, ((0, 8), (1, 4))),
        "down_weight": normal_values(splits[10], (FF, MODEL_WIDTH), FF ** -0.5, 0.09375, ((0, 4), (1, 8))),
        "cotangent": normal_values(splits[11], (SEQS, SEQUENCE_LENGTH, MODEL_WIDTH), 1.0, 6.0, ((0, 2), (1, 16))),
    }


epsilon = 1e-05
rope_base = 1000000.0
masked_score = -1e+30

def norm_rows(values, gain):
    inverse = lax.rsqrt(lax.optimization_barrier(jnp.mean(values * values, axis=-1, keepdims=True)) + epsilon)
    normal = values * inverse
    return (normal * gain, normal, inverse)

def norm_back(grad_out, normal, inverse, gain):
    scaled = grad_out * gain
    grad_in = inverse * (scaled - normal * lax.optimization_barrier(jnp.mean(scaled * normal, axis=-1, keepdims=True)))
    return (grad_in, lax.optimization_barrier(jnp.sum(grad_out * normal, axis=tuple(range(grad_out.ndim - 1)))))

def rope_tables(positions, head_width):
    half_width = head_width // 2
    freq = jnp.exp(jnp.arange(half_width, dtype=jnp.float32) * (-2.0 * math.log(rope_base) / head_width))
    angle = positions.astype(jnp.float32)[:, None] * freq[None, :]
    cosine = jnp.cos(angle)
    sine_vals = jnp.sin(angle)
    return (jnp.concatenate([cosine, cosine], -1), jnp.concatenate([sine_vals, sine_vals], -1))

def rotate(values, cosine, sine_vals):
    half_width = values.shape[-1] // 2
    turned = jnp.concatenate([-values[..., half_width:], values[..., :half_width]], -1)
    return values * cosine + turned * sine_vals

def unrotate(grads, cosine, sine_vals):
    half_width = grads.shape[-1] // 2
    scaled = grads * sine_vals
    return grads * cosine + jnp.concatenate([scaled[..., half_width:], -scaled[..., :half_width]], -1)

def barrier_wide(values):
    return lax.optimization_barrier(values.astype(jnp.bfloat16)).astype(jnp.float32)

def one_sequence(seq_tokens, seq_cot, attention_gain, query_weight, key_value_weight, query_gain, key_gain, output_weight, ffn_gain, gate_weight, up_weight, down_weight):
    query_group_count = QUERY_HEADS // KEY_VALUE_HEADS
    score_scale = 1.0 / math.sqrt(HEAD_SIZE)
    block_count = SEQUENCE_LENGTH // TOKENS_PER_SHARD
    resid_in = seq_tokens.astype(jnp.float32)
    normed_wide, hat_first, inv_first = norm_rows(resid_in, attention_gain)
    attention_normed = normed_wide.astype(jnp.bfloat16)
    queries = jnp.dot(attention_normed, query_weight, preferred_element_type=jnp.float32).reshape(SEQUENCE_LENGTH, QUERY_HEADS, HEAD_SIZE).transpose(1, 0, 2)
    key_value_pairs = jnp.dot(attention_normed, key_value_weight, preferred_element_type=jnp.float32).reshape(SEQUENCE_LENGTH, KEY_VALUE_HEADS, 2, HEAD_SIZE)
    key_raw = key_value_pairs[:, :, 0].transpose(1, 0, 2)
    value_raw = key_value_pairs[:, :, 1].transpose(1, 0, 2)
    qnorm, q_hat, q_inv = norm_rows(queries, query_gain)
    knorm, k_hat, k_inv = norm_rows(key_raw, key_gain)
    positions = jnp.arange(SEQUENCE_LENGTH, dtype=jnp.int32)
    cosine, sine_vals = rope_tables(positions, HEAD_SIZE)
    rotary_query = rotate(qnorm, cosine, sine_vals).astype(jnp.bfloat16)
    rot_k = rotate(knorm, cosine, sine_vals).astype(jnp.bfloat16)
    vals = value_raw.astype(jnp.bfloat16)
    keys_wide = rot_k.astype(jnp.float32)
    vals_wide = vals.astype(jnp.float32)

    def forward_block(index):
        start_offset = index * TOKENS_PER_SHARD
        query_slice = lax.dynamic_slice_in_dim(rotary_query, start_offset, TOKENS_PER_SHARD, 1).astype(jnp.float32).reshape(KEY_VALUE_HEADS, query_group_count, TOKENS_PER_SHARD, HEAD_SIZE)
        score = jnp.einsum('hgqd,hkd->hgqk', query_slice, keys_wide) * score_scale
        valid = positions[None, :] <= (start_offset + jnp.arange(TOKENS_PER_SHARD, dtype=jnp.int32))[:, None]
        score = jnp.where(valid, score, masked_score)
        top_score = lax.optimization_barrier(jnp.max(score, axis=-1, keepdims=True))
        weight = jnp.where(valid, jnp.exp(score - top_score), 0.0)
        total = lax.optimization_barrier(jnp.sum(weight, axis=-1, keepdims=True))
        weight16 = barrier_wide(weight)
        mixed = jnp.einsum('hgqk,hkd->hgqd', weight16, vals_wide, precision=lax.Precision.HIGHEST) / total
        return (mixed.reshape(QUERY_HEADS, TOKENS_PER_SHARD, HEAD_SIZE), (top_score + jnp.log(total))[..., 0].reshape(QUERY_HEADS, TOKENS_PER_SHARD))
    mixed_all, stats = lax.map(forward_block, jnp.arange(block_count, dtype=jnp.int32))
    attended_heads = mixed_all.transpose(1, 0, 2, 3).reshape(QUERY_HEADS, SEQUENCE_LENGTH, HEAD_SIZE).astype(jnp.bfloat16)
    attended = attended_heads.transpose(1, 0, 2).reshape(SEQUENCE_LENGTH, QUERY_HEADS * HEAD_SIZE)
    softmax_logsumexp = stats.transpose(1, 0, 2).reshape(QUERY_HEADS, SEQUENCE_LENGTH)
    resid = resid_in + jnp.dot(attended, output_weight, preferred_element_type=jnp.float32)
    normed_fw, hat_second, inv_second = norm_rows(resid, ffn_gain)
    normed_f = normed_fw.astype(jnp.bfloat16)
    gate = jnp.dot(normed_f, gate_weight, preferred_element_type=jnp.float32)
    up_vals = jnp.dot(normed_f, up_weight, preferred_element_type=jnp.float32)
    sigma = jax.nn.sigmoid(gate)
    mid = (gate * sigma * up_vals).astype(jnp.bfloat16)
    block_out = (resid + jnp.dot(mid, down_weight, preferred_element_type=jnp.float32)).astype(jnp.bfloat16)
    grad_down = jnp.dot(mid.T, seq_cot, preferred_element_type=jnp.float32)
    grad_mid = jnp.dot(seq_cot, down_weight.T, preferred_element_type=jnp.float32)
    dgate = (grad_mid * up_vals * sigma * (1.0 + gate * (1.0 - sigma))).astype(jnp.bfloat16)
    dup_vals = (grad_mid * gate * sigma).astype(jnp.bfloat16)
    grad_gate = jnp.dot(normed_f.T, dgate, preferred_element_type=jnp.float32)
    grad_up = jnp.dot(normed_f.T, dup_vals, preferred_element_type=jnp.float32)
    grad_normed_f = jnp.dot(dgate, gate_weight.T, preferred_element_type=jnp.float32) + jnp.dot(dup_vals, up_weight.T, preferred_element_type=jnp.float32)
    through_norm, grad_ffn_gain = norm_back(grad_normed_f, hat_second, inv_second, ffn_gain)
    grad_resid = seq_cot.astype(jnp.float32) + through_norm
    resid_grad16 = grad_resid.astype(jnp.bfloat16)
    grad_output = jnp.dot(attended.T, resid_grad16, preferred_element_type=jnp.float32)
    grad_attended = jnp.dot(resid_grad16, output_weight.T, preferred_element_type=jnp.float32).astype(jnp.bfloat16)
    head_gradient = grad_attended.reshape(SEQUENCE_LENGTH, QUERY_HEADS, HEAD_SIZE).transpose(1, 0, 2)
    delta_rows = lax.optimization_barrier(jnp.sum(head_gradient.astype(jnp.float32) * attended_heads.astype(jnp.float32), axis=-1))

    def backward_block(carry, index):
        key_acc, value_acc = carry
        start_offset = index * TOKENS_PER_SHARD
        query_slice = lax.dynamic_slice_in_dim(rotary_query, start_offset, TOKENS_PER_SHARD, 1).astype(jnp.float32).reshape(KEY_VALUE_HEADS, query_group_count, TOKENS_PER_SHARD, HEAD_SIZE)
        gradient_slice = lax.dynamic_slice_in_dim(head_gradient, start_offset, TOKENS_PER_SHARD, 1).astype(jnp.float32).reshape(KEY_VALUE_HEADS, query_group_count, TOKENS_PER_SHARD, HEAD_SIZE)
        logsumexp_slice = lax.dynamic_slice_in_dim(softmax_logsumexp, start_offset, TOKENS_PER_SHARD, 1).reshape(KEY_VALUE_HEADS, query_group_count, TOKENS_PER_SHARD)
        delta_slice = lax.dynamic_slice_in_dim(delta_rows, start_offset, TOKENS_PER_SHARD, 1).reshape(KEY_VALUE_HEADS, query_group_count, TOKENS_PER_SHARD)
        score = jnp.einsum('hgqd,hkd->hgqk', query_slice, keys_wide) * score_scale
        valid = positions[None, :] <= (start_offset + jnp.arange(TOKENS_PER_SHARD, dtype=jnp.int32))[:, None]
        prob = jnp.where(valid, jnp.exp(score - logsumexp_slice[..., None]), 0.0)
        dprob = jnp.einsum('hgqd,hkd->hgqk', gradient_slice, vals_wide)
        dscore = barrier_wide(prob * (dprob - delta_slice[..., None]) * score_scale)
        prob16 = barrier_wide(prob)
        query_grad = jnp.einsum('hgqk,hkd->hgqd', dscore, keys_wide)
        key_acc = key_acc + jnp.einsum('hgqk,hgqd->hkd', dscore, query_slice)
        value_acc = value_acc + jnp.einsum('hgqk,hgqd->hkd', prob16, gradient_slice)
        return ((key_acc, value_acc), query_grad.reshape(QUERY_HEADS, TOKENS_PER_SHARD, HEAD_SIZE))
    empty_key_rows = jnp.zeros((KEY_VALUE_HEADS, SEQUENCE_LENGTH, HEAD_SIZE), jnp.float32)
    (grad_rot_k, value_gradient), query_blocks = lax.scan(backward_block, (empty_key_rows, empty_key_rows), jnp.arange(block_count, dtype=jnp.int32))
    grad_rot_q = query_blocks.transpose(1, 0, 2, 3).reshape(QUERY_HEADS, SEQUENCE_LENGTH, HEAD_SIZE)
    grad_query_raw, grad_query_gain = norm_back(unrotate(grad_rot_q, cosine, sine_vals), q_hat, q_inv, query_gain)
    raw_key_gradient, grad_key_gain = norm_back(unrotate(grad_rot_k, cosine, sine_vals), k_hat, k_inv, key_gain)
    grad_q16 = grad_query_raw.transpose(1, 0, 2).reshape(SEQUENCE_LENGTH, QUERY_HEADS * HEAD_SIZE).astype(jnp.bfloat16)
    pair_gradient16 = jnp.stack([raw_key_gradient, value_gradient], axis=1).transpose(2, 0, 1, 3).reshape(SEQUENCE_LENGTH, KEY_VALUE_HEADS * 2 * HEAD_SIZE).astype(jnp.bfloat16)
    grad_query_w = jnp.dot(attention_normed.T, grad_q16, preferred_element_type=jnp.float32)
    grad_keyval_w = jnp.dot(attention_normed.T, pair_gradient16, preferred_element_type=jnp.float32)
    grad_normed_a = jnp.dot(grad_q16, query_weight.T, preferred_element_type=jnp.float32) + jnp.dot(pair_gradient16, key_value_weight.T, preferred_element_type=jnp.float32)
    through_first, grad_attention_gain = norm_back(grad_normed_a, hat_first, inv_first, attention_gain)
    grad_tokens = grad_resid + through_first
    grads = (grad_attention_gain, grad_query_w, grad_keyval_w, grad_query_gain, grad_key_gain, grad_output, grad_ffn_gain, grad_gate, grad_up, grad_down)
    return (block_out, grad_tokens, softmax_logsumexp, grads)

def reference(tokens, attention_gain, query_weight, key_value_weight, query_gain, key_gain, output_weight, ffn_gain, gate_weight, up_weight, down_weight, cotangent):
    outputs = []
    input_grads = []
    stats_all = []
    totals = None
    for seq_index in range(SEQS):
        block_out, grad_tokens, softmax_logsumexp, grads = one_sequence(tokens[seq_index], cotangent[seq_index], attention_gain, query_weight, key_value_weight, query_gain, key_gain, output_weight, ffn_gain, gate_weight, up_weight, down_weight)
        outputs.append(block_out)
        input_grads.append(grad_tokens)
        stats_all.append(softmax_logsumexp)
        if totals is None:
            totals = grads
        else:
            totals = tuple((left + right for left, right in zip(totals, grads)))
    return (jnp.stack(outputs), jnp.stack(input_grads), jnp.stack(stats_all), totals[0], totals[1], totals[2], totals[3], totals[4], totals[5], totals[6], totals[7], totals[8], totals[9])
```

```python
import math

import jax
import jax.numpy as jnp
from jax import lax
from jax.experimental import pallas as pl
from jax.experimental.pallas import tpu as pltpu
from jax.sharding import PartitionSpec as P

epsilon = 1e-05
rope_base = 1000000.0
f32 = jnp.float32
bf16 = jnp.bfloat16
exact = lax.Precision.HIGHEST
log2e = math.log2(math.e)


def mm(a, b):
    return lax.dot_general(a, b, (((1,), (0,)), ((), ())), preferred_element_type=f32)


def mm_nt(a, b):
    return lax.dot_general(a, b, (((1,), (1,)), ((), ())), preferred_element_type=f32)


def lanes(shape):
    return lax.broadcasted_iota(jnp.int32, shape, len(shape) - 1)


def rows_of(shape):
    return lax.broadcasted_iota(jnp.int32, shape, 0)


def sds(shape, dtype):
    return jax.ShapeDtypeStruct(shape, dtype)


VM = pl.BlockSpec(memory_space=pltpu.VMEM)
SM = pl.BlockSpec(memory_space=pltpu.SMEM)


def whole_call(body, outs, args, flops, name, scratch=(), scalars=True):
    moved = sum(math.prod(a.shape) * a.dtype.itemsize for a in list(args) + list(outs))
    specs = [VM] * len(args)
    if scalars:
        specs[0] = SM
    return pl.pallas_call(
        body,
        out_shape=list(outs),
        in_specs=specs,
        out_specs=[VM] * len(outs),
        scratch_shapes=list(scratch),
        cost_estimate=pl.CostEstimate(flops=int(flops), bytes_accessed=int(moved), transcendentals=0),
        name=name,
    )(*args)


def on_device(
    tokens,
    attention_gain,
    query_weight,
    key_value_weight,
    query_gain,
    key_gain,
    output_weight,
    ffn_gain,
    gate_weight,
    up_weight,
    down_weight,
    cotangent,
):
    hw = query_gain.shape[0]
    pw = 2 * hw
    R = tokens.shape[1]
    W = tokens.shape[2]
    NT = lax.axis_size("tp")
    NC = lax.axis_size("ctx")
    N = lax.axis_size("dp") * NC
    B = R * NT
    C = query_weight.shape[1]
    F = gate_weight.shape[1]
    QH = C // hw
    KH = key_value_weight.shape[1] // pw
    assert QH == 2 * KH
    H = W // 2
    blk = W // N
    scale = 1.0 / math.sqrt(hw)
    c2 = scale * log2e
    masks = list(range(0, N, 2)) + list(range(1, N, 2))
    me = lax.axis_index("dp") * NC + lax.axis_index("ctx")
    ctx = lax.axis_index("ctx")
    z = lax.axis_index("tp")
    where = jnp.stack([me, ctx, z]).astype(jnp.int32)
    aligned = blk % 128 == 0
    row_aligned = R % 128 == 0

    def plane(v, mask):
        return lax.ppermute(v, ("dp", "ctx"), [(i, i ^ mask) for i in range(N)])

    def column(v, mask):
        return lax.ppermute(v, "tp", [(i, i ^ mask) for i in range(NT)])

    def along(v, mask, keep):
        pairs = [(i, i ^ mask) for i in range(NC) if keep(i, i ^ mask)]
        return lax.ppermute(v, "ctx", pairs)

    def after(v, *deps):
        return lax.optimization_barrier((v,) + deps)[0]

    def gather_plane(own):
        if N == 8:
            half = own.shape[1] // 2
            fx, fy = plane(own, 2), plane(own, 4)
            top, low = plane(fx[:, :half], 4), plane(fy[:, half:], 2)
            mine = jnp.concatenate([own, fx, fy, top, low], axis=1)
        else:
            mine = jnp.concatenate([own] + [plane(own, r) for r in range(2, N, 2)], axis=1)
        return mine, plane(mine, 1)

    def scatter_plane(mine, other):
        got = plane(other, 1)
        m = mine.shape[1] * 2 // N
        parts = [
            mine[:, i * m : (i + 1) * m].astype(f32) + got[:, i * m : (i + 1) * m].astype(f32)
            for i in range(N // 2)
        ]
        if N == 8:
            half = m // 2
            far = parts[3].astype(bf16)
            tx, ty = plane(far[:, :half], 2), plane(far[:, half:], 4)
            ysend = jnp.concatenate(
                [parts[2][:, :half] + tx.astype(f32), parts[2][:, half:]], axis=1
            ).astype(bf16)
            xsend = jnp.concatenate(
                [parts[1][:, :half], parts[1][:, half:] + ty.astype(f32)], axis=1
            ).astype(bf16)
            return parts[0] + plane(xsend, 2).astype(f32) + plane(ysend, 4).astype(f32)
        total = parts[0]
        for i in range(1, N // 2):
            total = total + plane(parts[i].astype(bf16), 2 * i).astype(f32)
        return total

    def gather_column(own):
        return [own] + [column(own, k) for k in range(1, NT)]

    def spread_column(full):
        return [full[:R]] + [column(full[k * R : (k + 1) * R], k) for k in range(1, NT)]

    def slots(ref_rows, fallback):
        return fallback

    def take_cols(v, index, size, order):
        picks = index ^ jnp.array(order, jnp.int32)
        return jnp.take(v.reshape(v.shape[0], -1, size), picks, axis=1).reshape(v.shape)

    own_qkv = jnp.stack([query_weight, key_value_weight])
    own_out = output_weight.T

    def pre_body(s_ref, t_ref, c_ref, g_ref, n_ref, t_out, c_out, g_out):
        index = s_ref[0]
        for s, mask in enumerate(masks):
            if aligned:
                src = pl.ds(pl.multiple_of((index ^ mask) * blk, blk), blk)
            else:
                src = slice(s * blk, (s + 1) * blk)
            dst = slice(s * blk, (s + 1) * blk)
            t_out[:, dst] = t_ref[:, src]
            c_out[:, dst] = c_ref[:, src]
            g_out[:, dst] = g_ref[:, src]
        x = t_out[...].astype(f32)
        inv = lax.rsqrt(jnp.mean(x * x, axis=-1, keepdims=True) + epsilon)
        n_ref[...] = (x * inv * g_out[0:1, :]).astype(bf16)

    gains = jnp.stack([attention_gain, ffn_gain])
    t_in, c_in, g_in = tokens[0], cotangent[0], gains
    if not aligned:
        t_in, c_in, g_in = (take_cols(v, me, blk, masks) for v in (t_in, c_in, g_in))
    normed, tok, cot, gain2 = whole_call(
        pre_body,
        [sds((R, W), bf16), sds((R, W), bf16), sds((R, W), bf16), sds((2, W), f32)],
        (where, t_in, c_in, g_in),
        R * W * 8,
        "pre",
    )
    first_pieces = gather_column(normed)
    qkv_m, qkv_o = gather_plane(own_qkv)
    rows_first = jnp.concatenate(first_pieces, axis=0)

    out_cols = jnp.concatenate(gather_column(own_out), axis=1)
    out_m, out_o = gather_plane(after(out_cols, qkv_o)[None])
    own_ffn = jnp.stack([gate_weight, up_weight, down_weight.T])
    ffn_m, ffn_o = gather_plane(after(own_ffn, qkv_o))

    cot_rows = jnp.concatenate(gather_column(after(cot, rows_first)), axis=0)

    half_width = hw // 2
    freq = jnp.exp(jnp.arange(half_width, dtype=f32) * (-2.0 * math.log(rope_base) / hw))
    positions = ctx * B + (jnp.arange(B, dtype=jnp.int32) ^ (z * R))
    angle = positions.astype(f32)[:, None] * freq[None, :]
    cos_h, sin_h = jnp.cos(angle), jnp.sin(angle)
    cosine = jnp.tile(cos_h, (1, 2 * QH))
    sine = jnp.tile(jnp.concatenate([-sin_h, sin_h], -1), (1, QH))
    qg = jnp.tile(query_gain, QH)[None]
    kg = jnp.tile(jnp.concatenate([key_gain, jnp.ones_like(key_gain)]), KH)[None]

    def head_mean(x):
        n = x.shape[1]
        same = rows_of((n, n)) // hw == lanes((n, n)) // hw
        ones = jnp.where(same, 1.0 / hw, 0.0).astype(f32)
        return jnp.dot(x, ones, precision=exact, preferred_element_type=f32)

    def swap_halves(x):
        first = lanes(x.shape) % hw < half_width
        return jnp.where(
            first, pltpu.roll(x, x.shape[1] - half_width, 1), pltpu.roll(x, half_width, 1)
        )

    def qkv_body(r_ref, wm, wo, cs, sn, qg_ref, kg_ref, rq, pr, q_raw, p_raw):
        left, right = r_ref[:, :H], r_ref[:, H:]
        q = mm(left, wm[0]) + mm(right, wo[0])
        p = mm(left, wm[1]) + mm(right, wo[1])
        q_raw[...] = q
        p_raw[...] = p
        qn = q * lax.rsqrt(head_mean(q * q) + epsilon) * qg_ref[...]
        rq[...] = (qn * cs[...] + swap_halves(qn) * sn[...]).astype(bf16)
        kn = p * lax.rsqrt(head_mean(p * p) + epsilon) * kg_ref[...]
        kr = kn * cs[...] + swap_halves(kn) * sn[...]
        pr[...] = jnp.where(lanes(p.shape) % pw < hw, kr, p).astype(bf16)

    rot_q, pair, q_raw, p_raw = whole_call(
        qkv_body,
        [sds((B, C), bf16), sds((B, C), bf16), sds((B, C), f32), sds((B, C), f32)],
        (rows_first, qkv_m, qkv_o, cosine, sine, qg, kg),
        4 * B * W * C,
        "qkv",
        scalars=False,
    )

    earlier = lambda i, j: i < j
    kv_even = [pair] + [along(pair, r, earlier) for r in range(2, NC, 2)]
    kv_odd = [along(pair, 1, earlier)]
    for r in range(2, NC, 2):
        kv_odd.append(along(kv_even[r // 2], 1, lambda i, j: (i ^ 1 ^ j) == 0 and (i ^ r) < i))
    kv_all = jnp.stack([v for pq in zip(kv_even, kv_odd) for v in pq])

    def widen(x, part):
        moved = x if part == 0 else pltpu.roll(x, hw, 1)
        return jnp.where(lanes(x.shape) < hw, moved, 0.0)

    def widen_high(x, part):
        moved = x if part == 1 else pltpu.roll(x, hw, 1)
        return jnp.where(lanes(x.shape) >= hw, moved, 0.0)

    def causal(zz):
        key = rows_of((B, B)) ^ zz
        qry = lanes((B, B)) ^ zz
        return key <= qry

    def fwd_body(s_ref, q_ref, kv_ref, att_ref, lse_ref, qz, acc, tot):
        r, h = pl.program_id(0), pl.program_id(1)
        here = s_ref[1]

        @pl.when((r == 0) & (h == 0))
        def _():
            for hd in range(QH):
                x = q_ref[:, (hd // 2) * pw : (hd // 2 + 1) * pw].astype(f32)
                qz[hd] = widen(x, hd % 2).astype(bf16)

        def step(masked):
            kv = kv_ref[0]
            kvt = kv.astype(f32).T.astype(bf16)
            for g in range(2):
                hd = 2 * h + g
                e = jnp.exp2(mm_nt(kv, qz[hd]) * c2)
                if masked:
                    e = jnp.where(causal(s_ref[2] * R), e, 0.0)
                part = jnp.sum(e, axis=0, keepdims=True)
                o = mm(kvt, e.astype(bf16))
                if masked:
                    tot[hd] = jnp.broadcast_to(part, (8, B))
                    acc[hd] = o
                else:
                    tot[hd] += jnp.broadcast_to(part, (8, B))
                    acc[hd] += o

        @pl.when(r == 0)
        def _():
            step(True)

        @pl.when((here ^ r) < here)
        def _():
            step(False)

        @pl.when((r == NC - 1) & (h == KH - 1))
        def _():
            outs = [acc[hd][hw:] / tot[hd][0:1] for hd in range(QH)]
            att_ref[...] = jnp.concatenate(outs, axis=0).T.astype(bf16)
            for hd in range(QH):
                lse_ref[hd : hd + 1] = jnp.log(tot[hd][0:1])

    fixed = lambda shape: pl.BlockSpec(shape, lambda r, h: (0,) * len(shape))
    kv_spec = pl.BlockSpec((1, B, pw), lambda r, h: (r, 0, h))
    attended, lse = pl.pallas_call(
        fwd_body,
        grid=(NC, KH),
        out_shape=[sds((B, C), bf16), sds((QH, B), f32)],
        in_specs=[SM, fixed((B, C)), kv_spec],
        out_specs=[fixed((B, C)), fixed((QH, B))],
        scratch_shapes=[
            pltpu.VMEM((QH, B, pw), bf16),
            pltpu.VMEM((QH, pw, B), f32),
            pltpu.VMEM((QH, 8, B), f32),
        ],
        cost_estimate=pl.CostEstimate(
            flops=16 * QH * B * B * pw, bytes_accessed=4 * B * C * 2, transcendentals=4 * QH * B * B
        ),
        name="attention_forward",
    )(where, rot_q, kv_all)

    att_pieces = spread_column(attended)

    def out_body(*refs):
        pieces, (om, oo, t_ref, g_ref, res, nrm) = refs[:NT], refs[NT:]
        a = jnp.concatenate([p[...] for p in pieces], axis=1)
        x = t_ref[...].astype(f32) + jnp.concatenate([mm_nt(a, om[0]), mm_nt(a, oo[0])], axis=1)
        res[...] = x
        inv = lax.rsqrt(jnp.mean(x * x, axis=-1, keepdims=True) + epsilon)
        nrm[...] = (x * inv * g_ref[1:2, :]).astype(bf16)

    resid, normed_f = whole_call(
        out_body,
        [sds((R, W), f32), sds((R, W), bf16)],
        (*att_pieces, out_m, out_o, tok, gain2),
        2 * R * W * W,
        "out_norm",
        scalars=False,
    )
    rows_second = jnp.concatenate(gather_column(normed_f), axis=0)

    FB = 384 if F % 384 == 0 else F
    steps = F // FB

    def ffn_body(r_ref, c_ref, wm, wo, out, gnf, mid_r, dg_r, du_r, acc_o, acc_g):
        i = pl.program_id(0)
        rl, rr = r_ref[:, :H], r_ref[:, H:]
        gate = mm(rl, wm[0]) + mm(rr, wo[0])
        up = mm(rl, wm[1]) + mm(rr, wo[1])
        gmid = mm(c_ref[:, :H], wm[2]) + mm(c_ref[:, H:], wo[2])
        sig = jax.nn.sigmoid(gate)
        act = gate * sig
        mid = (act * up).astype(bf16)
        dg = (gmid * up * sig * (1.0 + gate * (1.0 - sig))).astype(bf16)
        du = (gmid * act).astype(bf16)
        mid_r[...] = mid
        dg_r[...] = dg
        du_r[...] = du
        for w, cols in ((wm, slice(0, H)), (wo, slice(H, W))):
            o = mm_nt(mid, w[2])
            g = mm_nt(dg, w[0]) + mm_nt(du, w[1])

            @pl.when(i == 0)
            def _():
                acc_o[:, cols] = o
                acc_g[:, cols] = g

            @pl.when(i > 0)
            def _():
                acc_o[:, cols] += o
                acc_g[:, cols] += g

        @pl.when(i == steps - 1)
        def _():
            out[...] = acc_o[...].astype(bf16)
            gnf[...] = acc_g[...].astype(bf16)

    one = lambda shape: pl.BlockSpec(shape, lambda i: (0,) * len(shape))
    wide = pl.BlockSpec((B, FB), lambda i: (0, i))
    w_spec = pl.BlockSpec((3, H, FB), lambda i: (0, 0, i))
    ffn_part, gnf_part, mid, dgate, dup = pl.pallas_call(
        ffn_body,
        grid=(steps,),
        out_shape=[sds((B, W), bf16), sds((B, W), bf16)] + [sds((B, F), bf16)] * 3,
        in_specs=[one((B, W)), one((B, W)), w_spec, w_spec],
        out_specs=[one((B, W)), one((B, W)), wide, wide, wide],
        scratch_shapes=[pltpu.VMEM((B, W), f32)] * 2,
        cost_estimate=pl.CostEstimate(
            flops=12 * B * W * F, bytes_accessed=6 * W * F + 6 * B * F, transcendentals=B * F
        ),
        name="ffn",
    )(rows_second, cot_rows, ffn_m, ffn_o)
    gnf_pieces = spread_column(gnf_part)

    def back_body(*refs):
        pieces, (res, c_ref, g_ref, om, oo, gres, rg, ga, gg) = refs[:NT], refs[NT:]
        grad = sum(p[...].astype(f32) for p in pieces)
        x = res[...]
        inv = lax.rsqrt(jnp.mean(x * x, axis=-1, keepdims=True) + epsilon)
        hat = x * inv
        gg[...] = jnp.sum(grad * hat, axis=0, keepdims=True)
        scaled = grad * g_ref[1:2, :]
        through = inv * (scaled - hat * jnp.mean(scaled * hat, axis=-1, keepdims=True))
        total = c_ref[...].astype(f32) + through
        gres[...] = total
        half = total.astype(bf16)
        rg[...] = half
        ga[...] = (mm(half[:, :H], om[0]) + mm(half[:, H:], oo[0])).astype(bf16)

    grad_resid, rg16, ga_full, ffn_gain_part = whole_call(
        back_body,
        [sds((R, W), f32), sds((R, W), bf16), sds((R, W), bf16), sds((1, W), f32)],
        (*gnf_pieces, resid, cot, gain2, out_m, out_o),
        2 * R * W * W,
        "second_back",
        scalars=False,
    )
    ga_pieces = [ga_full[:, :C]] + [
        column(ga_full[:, k * C : (k + 1) * C], k) for k in range(1, NT)
    ]
    grad_att = jnp.concatenate(ga_pieces, axis=0)

    def dw_body(r_ref, c_ref, mid_r, dg_r, du_r, gm, go, rt, ct):
        @pl.when(pl.program_id(0) == 0)
        def _():
            rt[...] = r_ref[...].T
            ct[...] = c_ref[...].T

        for k, (lhs, rhs) in enumerate(((rt, dg_r), (rt, du_r), (ct, mid_r))):
            gm[k] = mm(lhs[:H], rhs[...]).astype(bf16)
            go[k] = mm(lhs[H:], rhs[...]).astype(bf16)

    dwf_m, dwf_o = pl.pallas_call(
        dw_body,
        grid=(steps,),
        out_shape=[sds((3, H, F), bf16)] * 2,
        in_specs=[one((B, W)), one((B, W)), wide, wide, wide],
        out_specs=[w_spec, w_spec],
        scratch_shapes=[pltpu.VMEM((W, B), bf16)] * 2,
        cost_estimate=pl.CostEstimate(
            flops=6 * B * W * F, bytes_accessed=6 * W * F + 6 * B * F, transcendentals=0
        ),
        name="ffn_weights",
    )(rows_second, cot_rows, mid, dgate, dup)
    ffn_sum = scatter_plane(dwf_m, dwf_o)

    def bwd_body(s_ref, q_ref, d_ref, a_ref, l_ref, kv_ref, dq_ref, dkv_ref, qz, dz, acc, dl):
        r, h = pl.program_id(0), pl.program_id(1)
        here = s_ref[1]

        @pl.when((r == 0) & (h == 0))
        def _():
            for hd in range(QH):
                cols = slice((hd // 2) * pw, (hd // 2 + 1) * pw)
                qz[hd] = widen(q_ref[:, cols].astype(f32), hd % 2).astype(bf16)
                dz[hd] = widen_high(d_ref[:, cols].astype(f32), hd % 2).astype(bf16)
            prod = d_ref[...].astype(f32) * a_ref[...].astype(f32)
            for hd in range(QH):
                pick = jnp.where(lanes((8, C)) // hw == hd, 1.0, 0.0).astype(f32)
                dl[hd] = lax.dot_general(
                    pick, prod, (((1,), (1,)), ((), ())), precision=exact, preferred_element_type=f32
                )

        def step(masked):
            kv = kv_ref[0]
            kvt = kv.astype(f32).T.astype(bf16)
            total = None
            for g in range(2):
                hd = 2 * h + g
                q, d = qz[hd], dz[hd]
                shift = l_ref[hd] * log2e
                p = jnp.exp2(mm_nt(kv, q) * c2 - shift)
                if masked:
                    p = jnp.where(causal(s_ref[2] * R), p, 0.0)
                ds = (p * (mm_nt(kv, d) - dl[hd][0:1])).astype(bf16)
                t = jnp.where(lanes((B, pw)) < hw, mm(ds, q) * scale, mm(p.astype(bf16), d))
                total = t if total is None else total + t
                o = mm(kvt, ds)
                if masked:
                    acc[hd] = o
                else:
                    acc[hd] += o
            dkv_ref[0] = total.astype(bf16)

        @pl.when(r == 0)
        def _():
            step(True)

        @pl.when((here ^ r) < here)
        def _():
            step(False)

        @pl.when((here ^ r) > here)
        def _():
            dkv_ref[...] = jnp.zeros_like(dkv_ref)

        @pl.when((r == NC - 1) & (h == KH - 1))
        def _():
            outs = [acc[hd][:hw] for hd in range(QH)]
            dq_ref[...] = jnp.concatenate(outs, axis=0).T * scale

    grad_rot_q, dkv = pl.pallas_call(
        bwd_body,
        grid=(NC, KH),
        out_shape=[sds((B, C), f32), sds((NC, B, C), bf16)],
        in_specs=[SM, fixed((B, C)), fixed((B, C)), fixed((B, C)), fixed((QH, 1, B)), kv_spec],
        out_specs=[fixed((B, C)), kv_spec],
        scratch_shapes=[
            pltpu.VMEM((QH, B, pw), bf16),
            pltpu.VMEM((QH, B, pw), bf16),
            pltpu.VMEM((QH, pw, B), f32),
            pltpu.VMEM((QH, 8, B), f32),
        ],
        cost_estimate=pl.CostEstimate(
            flops=40 * QH * B * B * pw, bytes_accessed=8 * B * C * 2, transcendentals=4 * QH * B * B
        ),
        name="attention_backward",
    )(where, rot_q, grad_att, attended, lse[:, None, :], kv_all)

    later = lambda i, j: i > j
    odd = lax.ppermute(dkv[1::2], "ctx", [(i, i ^ 1) for i in range(NC)])
    pair_sum = dkv[0].astype(f32) + odd[0].astype(f32)
    for k in range(1, NC // 2):
        part = (dkv[2 * k].astype(f32) + odd[k].astype(f32)).astype(bf16)
        pair_sum = pair_sum + along(part, 2 * k, lambda i, j: i // 2 > j // 2).astype(f32)

    rg_rows = jnp.concatenate(gather_column(after(rg16, grad_att)), axis=0)
    ffn_pieces = spread_column(after(ffn_part, rg_rows))

    def dwo_body(g_ref, a_ref, gm, go):
        a = a_ref[...]
        gm[0] = lax.dot_general(
            g_ref[:, :H], a, (((0,), (0,)), ((), ())), preferred_element_type=f32
        ).astype(bf16)
        go[0] = lax.dot_general(
            g_ref[:, H:], a, (((0,), (0,)), ((), ())), preferred_element_type=f32
        ).astype(bf16)

    dwo_m, dwo_o = whole_call(
        dwo_body,
        [sds((1, H, C), bf16)] * 2,
        (rg_rows, attended),
        2 * B * W * C,
        "output_weights",
        scalars=False,
    )

    def qk_body(
        dq, dp, q_raw_r, p_raw_r, cs, sn, qg_ref, kg_ref, r_ref, wm, wo, g_ref,
        gna, gm, go, qgg, kgg, agg,
    ):
        def back(grad, raw, gain, live):
            turned = grad * cs[...] - swap_halves(grad) * sn[...]
            inv = lax.rsqrt(head_mean(raw * raw) + epsilon)
            hat = raw * inv
            scaled = turned * gain
            out = inv * (scaled - hat * head_mean(scaled * hat))
            gg = jnp.sum(turned * hat, axis=0, keepdims=True)
            if live is not None:
                out = jnp.where(live, out, grad)
            return out.astype(bf16), gg

        gq, qsum = back(dq[...], q_raw_r[...], qg_ref[...], None)
        live = lanes((B, C)) % pw < hw
        gp, ksum = back(dp[...], p_raw_r[...], kg_ref[...], live)
        qgg[...] = qsum
        kgg[...] = ksum
        both = jnp.concatenate([gq, gp], axis=1)
        for w, cols, gw in ((wm, slice(0, H), gm), (wo, slice(H, W), go)):
            part = mm_nt(gq, w[0]) + mm_nt(gp, w[1])
            gna[:, cols] = part.astype(bf16)
            rows = r_ref[:, cols]
            agg[:, cols] = (
                jnp.sum(part * rows.astype(f32), axis=0, keepdims=True) / g_ref[0:1, cols]
            )
            full = lax.dot_general(
                rows, both, (((0,), (0,)), ((), ())), preferred_element_type=f32
            ).astype(bf16)
            gw[0] = full[:, :C]
            gw[1] = full[:, C:]

    gna_part, dwq_m, dwq_o, qg_part, kg_part, att_gain_part = whole_call(
        qk_body,
        [
            sds((B, W), bf16),
            sds((2, H, C), bf16),
            sds((2, H, C), bf16),
            sds((1, C), f32),
            sds((1, C), f32),
            sds((1, W), f32),
        ],
        (
            grad_rot_q, pair_sum, q_raw, p_raw, cosine, sine, qg, kg,
            rows_first, qkv_m, qkv_o, gain2,
        ),
        8 * B * W * C,
        "projections_back",
        scalars=False,
    )
    gna_pieces = spread_column(gna_part)
    last_m = jnp.concatenate([dwq_m, dwo_m], axis=0)
    last_o = jnp.concatenate([dwq_o, dwo_o], axis=0)
    att_sum = scatter_plane(last_m, last_o)

    order_back = masks
    inverse_order = [order_back.index(m) for m in range(N)]
    gain_parts = jnp.concatenate([att_gain_part, ffn_gain_part], axis=0)
    slot_of = jnp.take(jnp.array(inverse_order, jnp.int32), me ^ jnp.arange(N, dtype=jnp.int32))
    gain_parts = jnp.take(gain_parts.reshape(2, N, blk), slot_of, axis=1).reshape(2 * W)
    q_part = qg_part.reshape(QH, hw).sum(0)
    k_part = kg_part.reshape(KH, 2, hw)[:, 0].sum(0)
    packed = jnp.concatenate([gain_parts, q_part, k_part]).reshape(-1, 128)
    packed = sum(gather_column(packed))
    bit = 1
    while bit < N:
        packed = packed + plane(packed, bit)
        bit *= 2
    packed = packed.reshape(-1)

    def end_body(*refs):
        s_ref, rest = refs[0], refs[1:]
        gp, fp, (t_ref, res, gres, g_ref, gt, bo) = rest[:NT], rest[NT : 2 * NT], rest[2 * NT :]
        index = s_ref[0]
        grad = sum(p[...].astype(f32) for p in gp)
        x = t_ref[...].astype(f32)
        inv = lax.rsqrt(jnp.mean(x * x, axis=-1, keepdims=True) + epsilon)
        hat = x * inv
        scaled = grad * g_ref[0:1, :]
        total = gres[...] + inv * (scaled - hat * jnp.mean(scaled * hat, axis=-1, keepdims=True))
        block = (res[...] + sum(p[...].astype(f32) for p in fp)).astype(bf16)
        for s, mask in enumerate(masks):
            src = slice(s * blk, (s + 1) * blk)
            if aligned:
                dst = pl.ds(pl.multiple_of((index ^ mask) * blk, blk), blk)
            else:
                dst = src
            gt[:, dst] = total[:, src]
            bo[:, dst] = block[:, src]

    grad_tokens, block_out = whole_call(
        end_body,
        [sds((R, W), f32), sds((R, W), bf16)],
        (where, *gna_pieces, *ffn_pieces, tok, resid, grad_resid, gain2),
        R * W * 16,
        "end",
    )
    if not aligned:
        back_cols = lambda v: jnp.take(
            v.reshape(R, N, blk), slot_of, axis=1
        ).reshape(R, W)
        grad_tokens, block_out = back_cols(grad_tokens), back_cols(block_out)

    lse_out = jnp.take(
        lse.reshape(QH, NT, R), z ^ jnp.arange(NT, dtype=jnp.int32), axis=1
    ).reshape(1, QH, B)
    return (
        block_out[None],
        grad_tokens[None],
        lse_out,
        packed[:W],
        att_sum[0],
        att_sum[1],
        packed[2 * W : 2 * W + hw],
        packed[2 * W + hw : 2 * W + 2 * hw],
        att_sum[2].T,
        packed[W : 2 * W],
        ffn_sum[0],
        ffn_sum[1],
        ffn_sum[2].T,
    )


def solution(mesh):
    in_specs = (
        P("dp", ("ctx", "tp"), None),
        P(),
        P(("dp", "ctx"), "tp"),
        P(("dp", "ctx"), "tp"),
        P(),
        P(),
        P("tp", ("dp", "ctx")),
        P(),
        P(("dp", "ctx"), "tp"),
        P(("dp", "ctx"), "tp"),
        P("tp", ("dp", "ctx")),
        P("dp", ("ctx", "tp"), None),
    )
    out_specs = (
        P("dp", ("ctx", "tp"), None),
        P("dp", ("ctx", "tp"), None),
        P("dp", "tp", "ctx"),
        P(),
        P(("dp", "ctx"), "tp"),
        P(("dp", "ctx"), "tp"),
        P(),
        P(),
        P("tp", ("dp", "ctx")),
        P(),
        P(("dp", "ctx"), "tp"),
        P(("dp", "ctx"), "tp"),
        P("tp", ("dp", "ctx")),
    )
    return jax.shard_map(
        on_device, mesh=mesh, in_specs=in_specs, out_specs=out_specs, check_vma=False
    )
```

```python
import math

import jax
import jax.numpy as jnp
from jax import lax
from jax.experimental import pallas as pl
from jax.experimental.pallas import tpu as pltpu
from jax.sharding import PartitionSpec as P


epsilon = 1e-05
rope_base = 1000000.0
f32 = jnp.float32
bf16 = jnp.bfloat16
exact = lax.Precision.HIGHEST
log2e = math.log2(math.e)


def mm(a, b):
    return lax.dot_general(a, b, (((1,), (0,)), ((), ())), preferred_element_type=f32)


def mm_nt(a, b):
    return lax.dot_general(a, b, (((1,), (1,)), ((), ())), preferred_element_type=f32)


def lanes(shape):
    return lax.broadcasted_iota(jnp.int32, shape, len(shape) - 1)


def rows_of(shape):
    return lax.broadcasted_iota(jnp.int32, shape, 0)


def sds(shape, dtype):
    return jax.ShapeDtypeStruct(shape, dtype)


VM = pl.BlockSpec(memory_space=pltpu.VMEM)
SM = pl.BlockSpec(memory_space=pltpu.SMEM)


def whole_call(body, outs, args, flops, scratch=(), scalars=True):
    moved = sum(math.prod(a.shape) * a.dtype.itemsize for a in list(args) + list(outs))
    specs = [VM] * len(args)
    if scalars:
        specs[0] = SM
    return pl.pallas_call(
        body,
        out_shape=list(outs),
        in_specs=specs,
        out_specs=[VM] * len(outs),
        scratch_shapes=list(scratch),
        cost_estimate=pl.CostEstimate(flops=int(flops), bytes_accessed=int(moved), transcendentals=0),
    )(*args)


def on_device(
    tokens,
    attention_gain,
    query_weight,
    key_value_weight,
    query_gain,
    key_gain,
    output_weight,
    ffn_gain,
    gate_weight,
    up_weight,
    down_weight,
    cotangent,
):
    hw = query_gain.shape[0]
    pw = 2 * hw
    R = tokens.shape[1]
    W = tokens.shape[2]
    NT = lax.axis_size("tp")
    NC = lax.axis_size("ctx")
    N = lax.axis_size("dp") * NC
    B = R * NT
    C = query_weight.shape[1]
    F = gate_weight.shape[1]
    QH = C // hw
    KH = key_value_weight.shape[1] // pw
    assert QH == 2 * KH
    H = W // 2
    blk = W // N
    scale = 1.0 / math.sqrt(hw)
    c2 = scale * log2e
    masks = list(range(0, N, 2)) + list(range(1, N, 2))
    me = lax.axis_index("dp") * NC + lax.axis_index("ctx")
    ctx = lax.axis_index("ctx")
    z = lax.axis_index("tp")
    where = jnp.stack([me, ctx, z]).astype(jnp.int32)
    aligned = blk % 128 == 0

    def plane(v, mask):
        return lax.ppermute(v, ("dp", "ctx"), [(i, i ^ mask) for i in range(N)])

    def column(v, mask):
        return lax.ppermute(v, "tp", [(i, i ^ mask) for i in range(NT)])

    def along(v, mask, keep):
        pairs = [(i, i ^ mask) for i in range(NC) if keep(i, i ^ mask)]
        return lax.ppermute(v, "ctx", pairs)

    def after(v, *deps):
        return lax.optimization_barrier((v,) + deps)[0]

    def gather_near(own):
        if N == 8:
            return [own, plane(own, 2), plane(own, 4)]
        return [own] + [plane(own, r) for r in range(2, N, 2)]

    def gather_far(near):
        if N == 8:
            own, fx, fy = near
            half = own.shape[1] // 2
            top = plane(fx[:, :half], 4)
            low = plane(fy[:, half:], 2)
            near = near + [top, low]
        mine = jnp.concatenate(near, axis=1)
        return mine, plane(mine, 1)

    def scatter_core(mine, other):
        got = plane(other, 1)
        m = mine.shape[1] * 2 // N
        return [
            mine[:, i * m : (i + 1) * m].astype(f32) + got[:, i * m : (i + 1) * m].astype(f32)
            for i in range(N // 2)
        ]

    def scatter_far(parts):
        if N != 8:
            return [p.astype(bf16) for p in parts[1:]]
        half = parts[0].shape[1] // 2
        far = parts[3].astype(bf16)
        tx = plane(far[:, :half], 2)
        ty = plane(far[:, half:], 4)
        ysend = jnp.concatenate(
            [parts[2][:, :half] + tx.astype(f32), parts[2][:, half:]], axis=1
        ).astype(bf16)
        xsend = jnp.concatenate(
            [parts[1][:, :half], parts[1][:, half:] + ty.astype(f32)], axis=1
        ).astype(bf16)
        return [xsend, ysend]

    def scatter_near(own, sends):
        total = own
        for i, v in enumerate(sends):
            total = total + plane(v, 2 * (i + 1)).astype(f32)
        return total

    def gather_column(own):
        return [own] + [column(own, k) for k in range(1, NT)]

    def spread_column(pieces):
        return [pieces[0]] + [column(pieces[k], k) for k in range(1, NT)]

    def put_slots(refs, value):
        for k, ref in enumerate(refs):
            ref[...] = value[k * R : (k + 1) * R].astype(ref.dtype)

    def join_slots(refs):
        return jnp.concatenate([ref[...] for ref in refs], axis=0)

    def take_cols(v, index, size, order):
        picks = index ^ jnp.array(order, jnp.int32)
        return jnp.take(v.reshape(v.shape[0], -1, size), picks, axis=1).reshape(v.shape)

    own_qkv = jnp.stack([query_weight, key_value_weight])
    own_out = output_weight.T

    def pre_body(s_ref, t_ref, c_ref, g_ref, n_ref, t_out, c_out, g_out):
        index = s_ref[0]
        for s, mask in enumerate(masks):
            if aligned:
                src = pl.ds(pl.multiple_of((index ^ mask) * blk, blk), blk)
            else:
                src = slice(s * blk, (s + 1) * blk)
            dst = slice(s * blk, (s + 1) * blk)
            t_out[:, dst] = t_ref[:, src]
            c_out[:, dst] = c_ref[:, src]
            g_out[:, dst] = g_ref[:, src]
        x = t_out[...].astype(f32)
        inv = lax.rsqrt(jnp.mean(x * x, axis=-1, keepdims=True) + epsilon)
        n_ref[...] = (x * inv * g_out[0:1, :]).astype(bf16)

    gains = jnp.stack([attention_gain, ffn_gain])
    t_in, c_in, g_in = tokens[0], cotangent[0], gains
    if not aligned:
        t_in, c_in, g_in = (take_cols(v, me, blk, masks) for v in (t_in, c_in, g_in))
    normed, tok, cot, gain2 = whole_call(
        pre_body,
        [sds((R, W), bf16), sds((R, W), bf16), sds((R, W), bf16), sds((2, W), f32)],
        (where, t_in, c_in, g_in),
        R * W * 8,
    )
    first_pieces = gather_column(normed)
    qkv_near = gather_near(after(own_qkv, normed))
    qkv_m, qkv_o = gather_far(qkv_near)
    own_ffn = jnp.stack([gate_weight, up_weight, down_weight.T])
    ffn_near = gather_near(after(own_ffn, *qkv_near))

    out_cols = jnp.concatenate(gather_column(after(own_out, *first_pieces)), axis=1)
    cot_pieces = gather_column(after(cot, *first_pieces))

    half_width = hw // 2
    freq = jnp.exp(jnp.arange(half_width, dtype=f32) * (-2.0 * math.log(rope_base) / hw))
    positions = ctx * B + (jnp.arange(B, dtype=jnp.int32) ^ (z * R))
    angle = positions.astype(f32)[:, None] * freq[None, :]
    cos_h, sin_h = jnp.cos(angle), jnp.sin(angle)
    cosine = jnp.tile(cos_h, (1, 2 * QH))
    sine = jnp.tile(jnp.concatenate([-sin_h, sin_h], -1), (1, QH))
    qg = jnp.tile(query_gain, QH)[None]
    kg = jnp.tile(jnp.concatenate([key_gain, jnp.ones_like(key_gain)]), KH)[None]

    def head_mean(x):
        n = x.shape[1]
        same = rows_of((n, n)) // hw == lanes((n, n)) // hw
        ones = jnp.where(same, 1.0 / hw, 0.0).astype(f32)
        return jnp.dot(x, ones, precision=exact, preferred_element_type=f32)

    def swap_halves(x):
        first = lanes(x.shape) % hw < half_width
        return jnp.where(
            first, pltpu.roll(x, x.shape[1] - half_width, 1), pltpu.roll(x, half_width, 1)
        )

    def qkv_body(*refs):
        wm, wo, cs, sn, qg_ref, kg_ref, rq, pr, q_raw, p_raw = refs[NT:]
        rows = join_slots(refs[:NT])
        left, right = rows[:, :H], rows[:, H:]
        q = mm(left, wm[0]) + mm(right, wo[0])
        p = mm(left, wm[1]) + mm(right, wo[1])
        q_raw[...] = q
        p_raw[...] = p
        qn = q * lax.rsqrt(head_mean(q * q) + epsilon) * qg_ref[...]
        rq[...] = (qn * cs[...] + swap_halves(qn) * sn[...]).astype(bf16)
        kn = p * lax.rsqrt(head_mean(p * p) + epsilon) * kg_ref[...]
        kr = kn * cs[...] + swap_halves(kn) * sn[...]
        pr[...] = jnp.where(lanes(p.shape) % pw < hw, kr, p).astype(bf16)

    rot_q, pair, q_raw, p_raw = whole_call(
        qkv_body,
        [sds((B, C), bf16), sds((B, C), bf16), sds((B, C), f32), sds((B, C), f32)],
        (*first_pieces, qkv_m, qkv_o, cosine, sine, qg, kg),
        4 * B * W * C,
        scalars=False,
    )

    earlier = lambda i, j: i < j
    kv_even = [pair] + [along(pair, r, earlier) for r in range(2, NC, 2)]
    kv_odd = [along(pair, 1, earlier)]
    for r in range(2, NC, 2):
        kv_odd.append(along(kv_even[r // 2], 1, lambda i, j: (i ^ r) < i))
    kv_all = jnp.stack([v for pq in zip(kv_even, kv_odd) for v in pq])
    out_m, out_o = gather_far(gather_near(out_cols[None]))

    def widen(x, part):
        moved = x if part == 0 else pltpu.roll(x, hw, 1)
        return jnp.where(lanes(x.shape) < hw, moved, 0.0)

    def widen_high(x, part):
        moved = x if part == 1 else pltpu.roll(x, hw, 1)
        return jnp.where(lanes(x.shape) >= hw, moved, 0.0)

    def causal(zz):
        key = rows_of((B, B)) ^ zz
        qry = lanes((B, B)) ^ zz
        return key <= qry

    def fwd_body(s_ref, q_ref, kv_ref, *refs):
        slot_refs, (att_ref, lse_ref, qz, acc, tot) = refs[:NT], refs[NT:]
        r, h = pl.program_id(0), pl.program_id(1)
        here = s_ref[1]

        @pl.when((r == 0) & (h == 0))
        def _():
            for hd in range(QH):
                x = q_ref[:, (hd // 2) * pw : (hd // 2 + 1) * pw].astype(f32)
                qz[hd] = widen(x, hd % 2).astype(bf16)

        def step(masked):
            kv = kv_ref[0]
            kvt = kv.astype(f32).T.astype(bf16)
            for g in range(2):
                hd = 2 * h + g
                e = jnp.exp2(mm_nt(kv, qz[hd]) * c2)
                if masked:
                    e = jnp.where(causal(s_ref[2] * R), e, 0.0)
                part = jnp.sum(e, axis=0, keepdims=True)
                o = mm(kvt, e.astype(bf16))
                if masked:
                    tot[hd] = jnp.broadcast_to(part, (8, B))
                    acc[hd] = o
                else:
                    tot[hd] += jnp.broadcast_to(part, (8, B))
                    acc[hd] += o

        @pl.when(r == 0)
        def _():
            step(True)

        @pl.when((here ^ r) < here)
        def _():
            step(False)

        @pl.when((r == NC - 1) & (h == KH - 1))
        def _():
            outs = [acc[hd][hw:] / tot[hd][0:1] for hd in range(QH)]
            att = jnp.concatenate(outs, axis=0).T.astype(bf16)
            att_ref[...] = att
            put_slots(slot_refs, att)
            for hd in range(QH):
                lse_ref[hd : hd + 1] = jnp.log(tot[hd][0:1])

    fixed = lambda shape: pl.BlockSpec(shape, lambda r, h: (0,) * len(shape))
    kv_spec = pl.BlockSpec((1, B, pw), lambda r, h: (r, 0, h))
    *att_slots, attended, lse = pl.pallas_call(
        fwd_body,
        grid=(NC, KH),
        out_shape=[sds((R, C), bf16)] * NT + [sds((B, C), bf16), sds((QH, B), f32)],
        in_specs=[SM, fixed((B, C)), kv_spec],
        out_specs=[fixed((R, C))] * NT + [fixed((B, C)), fixed((QH, B))],
        scratch_shapes=[
            pltpu.VMEM((QH, B, pw), bf16),
            pltpu.VMEM((QH, pw, B), f32),
            pltpu.VMEM((QH, 8, B), f32),
        ],
        cost_estimate=pl.CostEstimate(
            flops=16 * QH * B * B * pw, bytes_accessed=4 * B * C * 2, transcendentals=4 * QH * B * B
        ),
        name="attention_forward",
    )(where, rot_q, kv_all)

    att_pieces = spread_column(att_slots)
    _, *ffn_near = lax.optimization_barrier((attended, *ffn_near))
    ffn_m, ffn_o = gather_far(list(ffn_near))

    def out_body(*refs):
        pieces, (om, oo, t_ref, g_ref, res, nrm) = refs[:NT], refs[NT:]
        a = jnp.concatenate([p[...] for p in pieces], axis=1)
        x = t_ref[...].astype(f32) + jnp.concatenate([mm_nt(a, om[0]), mm_nt(a, oo[0])], axis=1)
        res[...] = x
        inv = lax.rsqrt(jnp.mean(x * x, axis=-1, keepdims=True) + epsilon)
        nrm[...] = (x * inv * g_ref[1:2, :]).astype(bf16)

    resid, normed_f = whole_call(
        out_body,
        [sds((R, W), f32), sds((R, W), bf16)],
        (*att_pieces, out_m, out_o, tok, gain2),
        2 * R * W * W,
        scalars=False,
    )
    second_pieces = gather_column(normed_f)

    FB = 384 if F % 384 == 0 else F
    steps = F // FB

    def ffn_body(*refs):
        r_in, c_in, (wm, wo) = refs[:NT], refs[NT : 2 * NT], refs[2 * NT : 2 * NT + 2]
        refs = refs[2 * NT + 2 :]
        outs, gnfs = refs[:NT], refs[NT : 2 * NT]
        mid_r, dg_r, du_r, r_ref, c_ref, acc_o, acc_g = refs[2 * NT :]
        i = pl.program_id(0)

        @pl.when(i == 0)
        def _():
            r_ref[...] = join_slots(r_in)
            c_ref[...] = join_slots(c_in)

        rl, rr = r_ref[:, :H], r_ref[:, H:]
        gate = mm(rl, wm[0]) + mm(rr, wo[0])
        up = mm(rl, wm[1]) + mm(rr, wo[1])
        gmid = mm(c_ref[:, :H], wm[2]) + mm(c_ref[:, H:], wo[2])
        sig = jax.nn.sigmoid(gate)
        act = gate * sig
        mid = (act * up).astype(bf16)
        dg = (gmid * up * sig * (1.0 + gate * (1.0 - sig))).astype(bf16)
        du = (gmid * act).astype(bf16)
        mid_r[...] = mid
        dg_r[...] = dg
        du_r[...] = du
        for w, cols in ((wm, slice(0, H)), (wo, slice(H, W))):
            o = mm_nt(mid, w[2])
            g = mm_nt(dg, w[0]) + mm_nt(du, w[1])

            @pl.when(i == 0)
            def _():
                acc_o[:, cols] = o
                acc_g[:, cols] = g

            @pl.when(i > 0)
            def _():
                acc_o[:, cols] += o
                acc_g[:, cols] += g

        @pl.when(i == steps - 1)
        def _():
            put_slots(outs, acc_o)
            put_slots(gnfs, acc_g)

    one = lambda shape: pl.BlockSpec(shape, lambda i: (0,) * len(shape))
    wide = pl.BlockSpec((B, FB), lambda i: (0, i))
    w_spec = pl.BlockSpec((3, H, FB), lambda i: (0, 0, i))
    *ffn_slots, mid, dgate, dup = pl.pallas_call(
        ffn_body,
        grid=(steps,),
        out_shape=[sds((R, W), bf16)] * (2 * NT) + [sds((B, F), bf16)] * 3,
        in_specs=[one((R, W))] * (2 * NT) + [w_spec, w_spec],
        out_specs=[one((R, W))] * (2 * NT) + [wide, wide, wide],
        scratch_shapes=[pltpu.VMEM((B, W), bf16)] * 2 + [pltpu.VMEM((B, W), f32)] * 2,
        cost_estimate=pl.CostEstimate(
            flops=12 * B * W * F, bytes_accessed=6 * W * F + 6 * B * F, transcendentals=B * F
        ),
        name="ffn",
    )(*second_pieces, *cot_pieces, ffn_m, ffn_o)
    gnf_pieces = spread_column(ffn_slots[NT:])

    def dw_body(*refs):
        r_in, c_in, (mid_r, dg_r, du_r, gm, go, rt, ct) = refs[:NT], refs[NT : 2 * NT], refs[2 * NT :]

        @pl.when(pl.program_id(0) == 0)
        def _():
            rt[...] = join_slots(r_in).T
            ct[...] = join_slots(c_in).T

        for k, (lhs, rhs) in enumerate(((rt, dg_r), (rt, du_r), (ct, mid_r))):
            gm[k] = mm(lhs[:H], rhs[...]).astype(bf16)
            go[k] = mm(lhs[H:], rhs[...]).astype(bf16)

    dwf_m, dwf_o = pl.pallas_call(
        dw_body,
        grid=(steps,),
        out_shape=[sds((3, H, F), bf16)] * 2,
        in_specs=[one((R, W))] * (2 * NT) + [wide, wide, wide],
        out_specs=[w_spec, w_spec],
        scratch_shapes=[pltpu.VMEM((W, B), bf16)] * 2,
        cost_estimate=pl.CostEstimate(
            flops=6 * B * W * F, bytes_accessed=6 * W * F + 6 * B * F, transcendentals=0
        ),
        name="ffn_weights",
    )(*second_pieces, *cot_pieces, mid, dgate, dup)
    ffn_parts = scatter_core(dwf_m, dwf_o)
    gnf_pieces, ffn_parts = lax.optimization_barrier((gnf_pieces, ffn_parts))

    def back_body(*refs):
        pieces, (res, c_ref, g_ref, om, oo, gres, rg, gg, *gas) = refs[:NT], refs[NT:]
        grad = sum(p[...].astype(f32) for p in pieces)
        x = res[...]
        inv = lax.rsqrt(jnp.mean(x * x, axis=-1, keepdims=True) + epsilon)
        hat = x * inv
        gg[...] = jnp.sum(grad * hat, axis=0, keepdims=True)
        scaled = grad * g_ref[1:2, :]
        through = inv * (scaled - hat * jnp.mean(scaled * hat, axis=-1, keepdims=True))
        total = c_ref[...].astype(f32) + through
        gres[...] = total
        half = total.astype(bf16)
        rg[...] = half
        ga = (mm(half[:, :H], om[0]) + mm(half[:, H:], oo[0])).astype(bf16)
        for k, ref in enumerate(gas):
            ref[...] = ga[:, k * C : (k + 1) * C]

    grad_resid, rg16, ffn_gain_part, *ga_slots = whole_call(
        back_body,
        [sds((R, W), f32), sds((R, W), bf16), sds((1, W), f32)] + [sds((R, C), bf16)] * NT,
        (*gnf_pieces, resid, cot, gain2, out_m, out_o),
        2 * R * W * W,
        scalars=False,
    )
    ga_pieces = spread_column(ga_slots)
    grad_att = jnp.concatenate(ga_pieces, axis=0)
    ffn_sends = scatter_far(ffn_parts)
    grad_att, ffn_sends = lax.optimization_barrier((grad_att, ffn_sends))
    ffn_sum = scatter_near(ffn_parts[0], ffn_sends)

    def bwd_body(s_ref, q_ref, d_ref, a_ref, l_ref, kv_ref, dq_ref, dkv_ref, qz, dz, acc, dl):
        r, h = pl.program_id(0), pl.program_id(1)
        here = s_ref[1]

        @pl.when((r == 0) & (h == 0))
        def _():
            for hd in range(QH):
                cols = slice((hd // 2) * pw, (hd // 2 + 1) * pw)
                qz[hd] = widen(q_ref[:, cols].astype(f32), hd % 2).astype(bf16)
                dz[hd] = widen_high(d_ref[:, cols].astype(f32), hd % 2).astype(bf16)
            prod = d_ref[...].astype(f32) * a_ref[...].astype(f32)
            for hd in range(QH):
                pick = jnp.where(lanes((8, C)) // hw == hd, 1.0, 0.0).astype(f32)
                dl[hd] = lax.dot_general(
                    pick, prod, (((1,), (1,)), ((), ())), precision=exact, preferred_element_type=f32
                )

        def step(masked):
            kv = kv_ref[0]
            kvt = kv.astype(f32).T.astype(bf16)
            total = None
            for g in range(2):
                hd = 2 * h + g
                q, d = qz[hd], dz[hd]
                shift = l_ref[hd] * log2e
                p = jnp.exp2(mm_nt(kv, q) * c2 - shift)
                if masked:
                    p = jnp.where(causal(s_ref[2] * R), p, 0.0)
                ds = (p * (mm_nt(kv, d) - dl[hd][0:1])).astype(bf16)
                t = jnp.where(lanes((B, pw)) < hw, mm(ds, q) * scale, mm(p.astype(bf16), d))
                total = t if total is None else total + t
                o = mm(kvt, ds)
                if masked:
                    acc[hd] = o
                else:
                    acc[hd] += o
            dkv_ref[0] = total.astype(bf16)

        @pl.when(r == 0)
        def _():
            step(True)

        @pl.when((here ^ r) < here)
        def _():
            step(False)

        @pl.when((here ^ r) > here)
        def _():
            dkv_ref[...] = jnp.zeros_like(dkv_ref)

        @pl.when((r == NC - 1) & (h == KH - 1))
        def _():
            outs = [acc[hd][:hw] for hd in range(QH)]
            dq_ref[...] = jnp.concatenate(outs, axis=0).T * scale

    grad_rot_q, dkv = pl.pallas_call(
        bwd_body,
        grid=(NC, KH),
        out_shape=[sds((B, C), f32), sds((NC, B, C), bf16)],
        in_specs=[SM, fixed((B, C)), fixed((B, C)), fixed((B, C)), fixed((QH, 1, B)), kv_spec],
        out_specs=[fixed((B, C)), kv_spec],
        scratch_shapes=[
            pltpu.VMEM((QH, B, pw), bf16),
            pltpu.VMEM((QH, B, pw), bf16),
            pltpu.VMEM((QH, pw, B), f32),
            pltpu.VMEM((QH, 8, B), f32),
        ],
        cost_estimate=pl.CostEstimate(
            flops=40 * QH * B * B * pw, bytes_accessed=8 * B * C * 2, transcendentals=4 * QH * B * B
        ),
        name="attention_backward",
    )(where, rot_q, grad_att, attended, lse[:, None, :], kv_all)

    odd = lax.ppermute(dkv[1::2], "ctx", [(i, i ^ 1) for i in range(NC)])
    pair_sum = dkv[0].astype(f32) + odd[0].astype(f32)
    for k in range(1, NC // 2):
        part = (dkv[2 * k].astype(f32) + odd[k].astype(f32)).astype(bf16)
        pair_sum = pair_sum + along(part, 2 * k, lambda i, j: i // 2 > j // 2).astype(f32)

    rg_rows = gather_column(after(rg16, grad_att))
    out_slots = list(lax.optimization_barrier((*ffn_slots[:NT], grad_att))[:NT])
    ffn_pieces = spread_column(out_slots)

    def qk_body(
        dq, dp, q_raw_r, p_raw_r, cs, sn, qg_ref, kg_ref, wm, wo, g_ref, *refs
    ):
        r_in, gnas, (gm, go, qgg, kgg, agg) = refs[:NT], refs[NT : 2 * NT], refs[2 * NT :]
        r_all = join_slots(r_in)

        def back(grad, raw, gain, live):
            turned = grad * cs[...] - swap_halves(grad) * sn[...]
            inv = lax.rsqrt(head_mean(raw * raw) + epsilon)
            hat = raw * inv
            scaled = turned * gain
            out = inv * (scaled - hat * head_mean(scaled * hat))
            gg = jnp.sum(turned * hat, axis=0, keepdims=True)
            if live is not None:
                out = jnp.where(live, out, grad)
            return out.astype(bf16), gg

        gq, qsum = back(dq[...], q_raw_r[...], qg_ref[...], None)
        live = lanes((B, C)) % pw < hw
        gp, ksum = back(dp[...], p_raw_r[...], kg_ref[...], live)
        qgg[...] = qsum
        kgg[...] = ksum
        both = jnp.concatenate([gq, gp], axis=1)
        for w, cols, gw in ((wm, slice(0, H), gm), (wo, slice(H, W), go)):
            part = mm_nt(gq, w[0]) + mm_nt(gp, w[1])
            for k, ref in enumerate(gnas):
                ref[:, cols] = part[k * R : (k + 1) * R].astype(bf16)
            rows = r_all[:, cols]
            agg[:, cols] = (
                jnp.sum(part * rows.astype(f32), axis=0, keepdims=True) / g_ref[0:1, cols]
            )
            full = lax.dot_general(
                rows, both, (((0,), (0,)), ((), ())), preferred_element_type=f32
            ).astype(bf16)
            gw[0] = full[:, :C]
            gw[1] = full[:, C:]

    *gna_slots, dwq_m, dwq_o, qg_part, kg_part, att_gain_part = whole_call(
        qk_body,
        [
            *[sds((R, W), bf16)] * NT,
            sds((2, H, C), bf16),
            sds((2, H, C), bf16),
            sds((1, C), f32),
            sds((1, C), f32),
            sds((1, W), f32),
        ],
        (
            grad_rot_q, pair_sum, q_raw, p_raw, cosine, sine, qg, kg,
            qkv_m, qkv_o, gain2, *first_pieces,
        ),
        8 * B * W * C,
        scalars=False,
    )
    gna_pieces = spread_column(gna_slots)
    rg_rows = lax.optimization_barrier((*rg_rows, *gna_slots))[:NT]

    def dwo_body(*refs):
        a_ref, gm, go = refs[NT:]
        a, g = a_ref[...], join_slots(refs[:NT])
        gm[0] = lax.dot_general(
            g[:, :H], a, (((0,), (0,)), ((), ())), preferred_element_type=f32
        ).astype(bf16)
        go[0] = lax.dot_general(
            g[:, H:], a, (((0,), (0,)), ((), ())), preferred_element_type=f32
        ).astype(bf16)

    dwo_m, dwo_o = whole_call(
        dwo_body, [sds((1, H, C), bf16)] * 2, (*rg_rows, attended), 2 * B * W * C, scalars=False
    )

    last_m = jnp.concatenate([dwq_m, dwo_m], axis=0)
    last_o = jnp.concatenate([dwq_o, dwo_o], axis=0)
    att_parts = scatter_core(last_m, last_o)
    att_sum = scatter_near(att_parts[0], scatter_far(att_parts))

    order_back = masks
    inverse_order = [order_back.index(m) for m in range(N)]
    gain_parts = jnp.concatenate([att_gain_part, ffn_gain_part], axis=0)
    slot_of = jnp.take(jnp.array(inverse_order, jnp.int32), me ^ jnp.arange(N, dtype=jnp.int32))
    gain_parts = jnp.take(gain_parts.reshape(2, N, blk), slot_of, axis=1).reshape(2 * W)
    q_part = qg_part.reshape(QH, hw).sum(0)
    k_part = kg_part.reshape(KH, 2, hw)[:, 0].sum(0)
    packed = jnp.concatenate([gain_parts, q_part, k_part]).reshape(-1, 128)
    packed = sum(gather_column(packed))
    bit = 1
    while bit < N:
        packed = packed + plane(packed, bit)
        bit *= 2
    packed = packed.reshape(-1)

    def end_body(*refs):
        s_ref, rest = refs[0], refs[1:]
        gp, fp, (t_ref, res, gres, g_ref, gt, bo) = rest[:NT], rest[NT : 2 * NT], rest[2 * NT :]
        index = s_ref[0]
        grad = sum(p[...].astype(f32) for p in gp)
        x = t_ref[...].astype(f32)
        inv = lax.rsqrt(jnp.mean(x * x, axis=-1, keepdims=True) + epsilon)
        hat = x * inv
        scaled = grad * g_ref[0:1, :]
        total = gres[...] + inv * (scaled - hat * jnp.mean(scaled * hat, axis=-1, keepdims=True))
        block = (res[...] + sum(p[...].astype(f32) for p in fp)).astype(bf16)
        for s, mask in enumerate(masks):
            src = slice(s * blk, (s + 1) * blk)
            if aligned:
                dst = pl.ds(pl.multiple_of((index ^ mask) * blk, blk), blk)
            else:
                dst = src
            gt[:, dst] = total[:, src]
            bo[:, dst] = block[:, src]

    gna_pieces, att_sum, ffn_sum, packed = lax.optimization_barrier(
        (gna_pieces, att_sum, ffn_sum, packed)
    )
    grad_tokens, block_out = whole_call(
        end_body,
        [sds((R, W), f32), sds((R, W), bf16)],
        (where, *gna_pieces, *ffn_pieces, tok, resid, grad_resid, gain2),
        R * W * 16,
    )
    if not aligned:
        back_cols = lambda v: jnp.take(
            v.reshape(R, N, blk), slot_of, axis=1
        ).reshape(R, W)
        grad_tokens, block_out = back_cols(grad_tokens), back_cols(block_out)

    lse_out = jnp.take(
        lse.reshape(QH, NT, R), z ^ jnp.arange(NT, dtype=jnp.int32), axis=1
    ).reshape(1, QH, B)
    return (
        block_out[None],
        grad_tokens[None],
        lse_out,
        packed[:W],
        att_sum[0],
        att_sum[1],
        packed[2 * W : 2 * W + hw],
        packed[2 * W + hw : 2 * W + 2 * hw],
        att_sum[2].T,
        packed[W : 2 * W],
        ffn_sum[0],
        ffn_sum[1],
        ffn_sum[2].T,
    )


def solution(mesh):
    in_specs = (
        P("dp", ("ctx", "tp"), None),
        P(),
        P(("dp", "ctx"), "tp"),
        P(("dp", "ctx"), "tp"),
        P(),
        P(),
        P("tp", ("dp", "ctx")),
        P(),
        P(("dp", "ctx"), "tp"),
        P(("dp", "ctx"), "tp"),
        P("tp", ("dp", "ctx")),
        P("dp", ("ctx", "tp"), None),
    )
    out_specs = (
        P("dp", ("ctx", "tp"), None),
        P("dp", ("ctx", "tp"), None),
        P("dp", "tp", "ctx"),
        P(),
        P(("dp", "ctx"), "tp"),
        P(("dp", "ctx"), "tp"),
        P(),
        P(),
        P("tp", ("dp", "ctx")),
        P(),
        P(("dp", "ctx"), "tp"),
        P(("dp", "ctx"), "tp"),
        P("tp", ("dp", "ctx")),
    )

    return jax.shard_map(
        on_device, mesh=mesh, in_specs=in_specs, out_specs=out_specs, check_vma=False
    )
```

```python
import math

import jax
import jax.numpy as jnp
from jax import lax
from jax.experimental import pallas as pl
from jax.experimental.pallas import tpu as pltpu
from jax.sharding import PartitionSpec as P


epsilon = 1e-05
rope_base = 1000000.0
f32 = jnp.float32
bf16 = jnp.bfloat16
exact = lax.Precision.HIGHEST
log2e = math.log2(math.e)


def mm(a, b):
    return lax.dot_general(a, b, (((1,), (0,)), ((), ())), preferred_element_type=f32)


def mm_nt(a, b):
    return lax.dot_general(a, b, (((1,), (1,)), ((), ())), preferred_element_type=f32)


def lanes(shape):
    return lax.broadcasted_iota(jnp.int32, shape, len(shape) - 1)


def rows_of(shape):
    return lax.broadcasted_iota(jnp.int32, shape, 0)


def sds(shape, dtype):
    return jax.ShapeDtypeStruct(shape, dtype)


VM = pl.BlockSpec(memory_space=pltpu.VMEM)
SM = pl.BlockSpec(memory_space=pltpu.SMEM)


def whole_call(body, outs, args, flops, scratch=(), scalars=True):
    moved = sum(math.prod(a.shape) * a.dtype.itemsize for a in list(args) + list(outs))
    specs = [VM] * len(args)
    if scalars:
        specs[0] = SM
    return pl.pallas_call(
        body,
        out_shape=list(outs),
        in_specs=specs,
        out_specs=[VM] * len(outs),
        scratch_shapes=list(scratch),
        cost_estimate=pl.CostEstimate(flops=int(flops), bytes_accessed=int(moved), transcendentals=0),
    )(*args)


def on_device(
    tokens,
    attention_gain,
    query_weight,
    key_value_weight,
    query_gain,
    key_gain,
    output_weight,
    ffn_gain,
    gate_weight,
    up_weight,
    down_weight,
    cotangent,
):
    hw = query_gain.shape[0]
    pw = 2 * hw
    R = tokens.shape[1]
    W = tokens.shape[2]
    NT = lax.axis_size("tp")
    NC = lax.axis_size("ctx")
    N = lax.axis_size("dp") * NC
    B = R * NT
    C = query_weight.shape[1]
    F = gate_weight.shape[1]
    QH = C // hw
    KH = key_value_weight.shape[1] // pw
    assert QH == 2 * KH
    H = W // 2
    blk = W // N
    scale = 1.0 / math.sqrt(hw)
    c2 = scale * log2e
    masks = list(range(0, N, 2)) + list(range(1, N, 2))
    me = lax.axis_index("dp") * NC + lax.axis_index("ctx")
    ctx = lax.axis_index("ctx")
    z = lax.axis_index("tp")
    where = jnp.stack([me, ctx, z]).astype(jnp.int32)
    aligned = blk % 128 == 0
    assert R == blk

    def plane(v, mask):
        return lax.ppermute(v, ("dp", "ctx"), [(i, i ^ mask) for i in range(N)])

    def column(v, mask):
        return lax.ppermute(v, "tp", [(i, i ^ mask) for i in range(NT)])

    def along(v, mask, keep):
        pairs = [(i, i ^ mask) for i in range(NC) if keep(i, i ^ mask)]
        return lax.ppermute(v, "ctx", pairs)

    def after(v, *deps):
        return lax.optimization_barrier((v,) + deps)[0]

    def gather_near(own):
        return [own] + [plane(own, r) for r in range(2, N, 2)]

    def gather_core(near):
        mine = jnp.concatenate(near, axis=1)
        return mine, plane(mine, 1)

    def merge_core(mine, got):
        kinds, half, cols = mine.shape
        m = half * 2 // N

        def body(a, b, first, *rest):
            for i in range(N // 2):
                rows = slice(i * m, (i + 1) * m)
                total = a[0, rows].astype(f32) + b[0, rows].astype(f32)
                if i == 0:
                    first[0] = total
                else:
                    rest[i - 1][0] = total.astype(bf16)

        big = pl.BlockSpec((1, half, cols), lambda k: (k, 0, 0))
        small = pl.BlockSpec((1, m, cols), lambda k: (k, 0, 0))
        own, *sends = pl.pallas_call(
            body,
            grid=(kinds,),
            out_shape=[sds((kinds, m, cols), f32)] + [sds((kinds, m, cols), bf16)] * (N // 2 - 1),
            in_specs=[big, big],
            out_specs=[small] * (N // 2),
            cost_estimate=pl.CostEstimate(
                flops=kinds * half * cols, bytes_accessed=7 * kinds * half * cols, transcendentals=0
            ),
        )(mine, got)
        return own, sends

    def close_sum(own, parts):
        kinds, m, cols = own.shape

        def body(first, *refs):
            parts, outs = refs[: len(parts_in)], refs[len(parts_in) :]
            for k in range(kinds):
                total = first[k]
                for p in parts:
                    total = total + p[k].astype(f32)
                outs[k][...] = total if k < kinds - 1 else total.T

        parts_in = parts
        return whole_call(
            body,
            [sds((m, cols), f32)] * (kinds - 1) + [sds((cols, m), f32)],
            (own, *parts),
            own.size * N,
            scalars=False,
        )

    def gather_column(own):
        return [own] + [column(own, k) for k in range(1, NT)]

    def spread_column(pieces):
        return [pieces[0]] + [column(pieces[k], k) for k in range(1, NT)]

    def put_slots(refs, value):
        for k, ref in enumerate(refs):
            ref[...] = value[k * R : (k + 1) * R].astype(ref.dtype)

    def join_slots(refs):
        return jnp.concatenate([ref[...] for ref in refs], axis=0)

    def take_cols(v, index, size, order):
        picks = index ^ jnp.array(order, jnp.int32)
        return jnp.take(v.reshape(v.shape[0], -1, size), picks, axis=1).reshape(v.shape)

    own_qkv = jnp.stack([query_weight, key_value_weight])

    def pre_body(s_ref, t_ref, c_ref, g_ref, o_ref, n_ref, t_out, c_out, g_out):
        index = s_ref[0]
        for s, mask in enumerate(masks):
            if aligned:
                src = pl.ds(pl.multiple_of((index ^ mask) * blk, blk), blk)
            else:
                src = slice(s * blk, (s + 1) * blk)
            dst = slice(s * blk, (s + 1) * blk)
            t_out[:, dst] = t_ref[:, src]
            c_out[:, dst] = c_ref[:, src]
            g_out[:, dst] = g_ref[:, src]
        x = t_out[...].astype(f32)
        inv = lax.rsqrt(jnp.mean(x * x, axis=-1, keepdims=True) + epsilon)
        n_ref[:, :W] = (x * inv * g_out[0:1, :]).astype(bf16)
        n_ref[:, W:] = o_ref[...].T

    gains = jnp.stack([attention_gain, ffn_gain])
    t_in, c_in, g_in = tokens[0], cotangent[0], gains
    if not aligned:
        t_in, c_in, g_in = (take_cols(v, me, blk, masks) for v in (t_in, c_in, g_in))
    normed, tok, cot, gain2 = whole_call(
        pre_body,
        [sds((R, W + C), bf16), sds((R, W), bf16), sds((R, W), bf16), sds((2, W), f32)],
        (where, t_in, c_in, g_in, output_weight),
        R * W * 8,
    )
    first_pieces = gather_column(normed)
    qkv_near = gather_near(after(own_qkv, normed))
    qkv_m, qkv_o = gather_core(qkv_near)
    own_ffn = jnp.stack([gate_weight, up_weight, down_weight.T])
    ffn_near = gather_near(after(own_ffn, normed))
    out_cols = jnp.concatenate([p[:, W:] for p in first_pieces], axis=1)[None]
    out_near = gather_near(out_cols)
    cot_pieces = gather_column(after(cot, *first_pieces))

    half_width = hw // 2
    freq = jnp.exp(jnp.arange(half_width, dtype=f32) * (-2.0 * math.log(rope_base) / hw))
    positions = ctx * B + (jnp.arange(B, dtype=jnp.int32) ^ (z * R))
    angle = positions.astype(f32)[:, None] * freq[None, :]
    cos_h, sin_h = jnp.cos(angle), jnp.sin(angle)
    cosine = jnp.tile(cos_h, (1, 2 * QH))
    sine = jnp.tile(jnp.concatenate([-sin_h, sin_h], -1), (1, QH))
    qg = jnp.tile(query_gain, QH)[None]
    kg = jnp.tile(jnp.concatenate([key_gain, jnp.ones_like(key_gain)]), KH)[None]

    def head_mean(x):
        n = x.shape[1]
        same = rows_of((n, n)) // hw == lanes((n, n)) // hw
        ones = jnp.where(same, 1.0 / hw, 0.0).astype(bf16)
        high = x.astype(bf16)
        rest = x - high.astype(f32)
        low = rest.astype(bf16)
        tail = (rest - low.astype(f32)).astype(bf16)
        return mm(high, ones) + mm(low, ones) + mm(tail, ones)

    def swap_halves(x):
        first = lanes(x.shape) % hw < half_width
        return jnp.where(
            first, pltpu.roll(x, x.shape[1] - half_width, 1), pltpu.roll(x, half_width, 1)
        )

    def qkv_body(*refs):
        wm, wo, cs, sn, qg_ref, kg_ref, rq, pr, q_raw, p_raw = refs[NT:]
        rows = join_slots(refs[:NT])
        left, right = rows[:, :H], rows[:, H:W]
        q = mm(left, wm[0]) + mm(right, wo[0])
        p = mm(left, wm[1]) + mm(right, wo[1])
        q_raw[...] = q
        p_raw[...] = p
        qn = q * lax.rsqrt(head_mean(q * q) + epsilon) * qg_ref[...]
        rq[...] = (qn * cs[...] + swap_halves(qn) * sn[...]).astype(bf16)
        kn = p * lax.rsqrt(head_mean(p * p) + epsilon) * kg_ref[...]
        kr = kn * cs[...] + swap_halves(kn) * sn[...]
        pr[...] = jnp.where(lanes(p.shape) % pw < hw, kr, p).astype(bf16)

    rot_q, pair, q_raw, p_raw = whole_call(
        qkv_body,
        [sds((B, C), bf16), sds((B, C), bf16), sds((B, C), f32), sds((B, C), f32)],
        (*first_pieces, qkv_m, qkv_o, cosine, sine, qg, kg),
        4 * B * W * C,
        scalars=False,
    )

    earlier = lambda i, j: i < j
    kv_even = [pair] + [along(pair, r, earlier) for r in range(2, NC, 2)]
    kv_odd = [along(pair, 1, earlier)]
    for r in range(2, NC, 2):
        kv_odd.append(along(kv_even[r // 2], 1, lambda i, j: (i ^ r) < i))
    kv_pieces = [v for pq in zip(kv_even, kv_odd) for v in pq]
    out_m, out_o = gather_core(out_near)

    def widen(x, part):
        moved = x if part == 0 else pltpu.roll(x, hw, 1)
        return jnp.where(lanes(x.shape) < hw, moved, 0.0)

    def widen_high(x, part):
        moved = x if part == 1 else pltpu.roll(x, hw, 1)
        return jnp.where(lanes(x.shape) >= hw, moved, 0.0)

    def causal(zz):
        key = rows_of((B, B)) ^ zz
        qry = lanes((B, B)) ^ zz
        return key <= qry

    def fwd_body(s_ref, q_ref, *refs):
        kv_in, slot_refs = refs[:NC], refs[NC : NC + NT]
        att_ref, lse_ref, qz, acc, tot, kv_ref = refs[NC + NT :]
        r, h = pl.program_id(0), pl.program_id(1)
        here = s_ref[1]

        @pl.when((r == 0) & (h == 0))
        def _():
            for hd in range(QH):
                x = q_ref[:, (hd // 2) * pw : (hd // 2 + 1) * pw].astype(f32)
                qz[hd] = widen(x, hd % 2).astype(bf16)
            for k in range(NC):
                kv_ref[k] = kv_in[k][...]

        def step(masked):
            kv = kv_ref[r, :, pl.ds(pl.multiple_of(h * pw, pw), pw)]
            kvt = kv.astype(f32).T.astype(bf16)
            for g in range(2):
                hd = 2 * h + g
                e = jnp.exp2(mm_nt(kv, qz[hd]) * c2)
                if masked:
                    e = jnp.where(causal(s_ref[2] * R), e, 0.0)
                part = jnp.sum(e, axis=0, keepdims=True)
                o = mm(kvt, e.astype(bf16))
                if masked:
                    tot[hd] = jnp.broadcast_to(part, (8, B))
                    acc[hd] = o
                else:
                    tot[hd] += jnp.broadcast_to(part, (8, B))
                    acc[hd] += o

        @pl.when(r == 0)
        def _():
            step(True)

        @pl.when((here ^ r) < here)
        def _():
            step(False)

        @pl.when((r == NC - 1) & (h == KH - 1))
        def _():
            outs = [acc[hd][hw:] / tot[hd][0:1] for hd in range(QH)]
            att = jnp.concatenate(outs, axis=0).T.astype(bf16)
            att_ref[...] = att
            put_slots(slot_refs, att)
            for hd in range(QH):
                lse_ref[hd] = jnp.log(tot[hd][0:1])

    fixed = lambda shape: pl.BlockSpec(shape, lambda r, h: (0,) * len(shape))
    *att_slots, attended, lse = pl.pallas_call(
        fwd_body,
        grid=(NC, KH),
        out_shape=[sds((R, C), bf16)] * NT + [sds((B, C), bf16), sds((QH, 1, B), f32)],
        in_specs=[SM] + [fixed((B, C))] * (1 + NC),
        out_specs=[fixed((R, C))] * NT + [fixed((B, C)), fixed((QH, 1, B))],
        scratch_shapes=[
            pltpu.VMEM((QH, B, pw), bf16),
            pltpu.VMEM((QH, pw, B), f32),
            pltpu.VMEM((QH, 8, B), f32),
            pltpu.VMEM((NC, B, C), bf16),
        ],
        cost_estimate=pl.CostEstimate(
            flops=16 * QH * B * B * pw, bytes_accessed=4 * B * C * 2, transcendentals=4 * QH * B * B
        ),
        name="attention_forward",
    )(where, rot_q, *kv_pieces)

    att_pieces = spread_column(att_slots)
    ffn_m, ffn_o = gather_core(ffn_near)

    def out_body(*refs):
        pieces, (om, oo, t_ref, g_ref, res, nrm) = refs[:NT], refs[NT:]
        a = jnp.concatenate([p[...] for p in pieces], axis=1)
        x = t_ref[...].astype(f32) + jnp.concatenate([mm_nt(a, om[0]), mm_nt(a, oo[0])], axis=1)
        res[...] = x
        inv = lax.rsqrt(jnp.mean(x * x, axis=-1, keepdims=True) + epsilon)
        nrm[...] = (x * inv * g_ref[1:2, :]).astype(bf16)

    resid, normed_f = whole_call(
        out_body,
        [sds((R, W), f32), sds((R, W), bf16)],
        (*att_pieces, out_m, out_o, tok, gain2),
        2 * R * W * W,
        scalars=False,
    )
    second_pieces = gather_column(normed_f)

    FB = 384 if F % 384 == 0 else F
    steps = F // FB

    def ffn_body(*refs):
        r_in, c_in, (wm, wo) = refs[:NT], refs[NT : 2 * NT], refs[2 * NT : 2 * NT + 2]
        refs = refs[2 * NT + 2 :]
        outs, gnfs = refs[:NT], refs[NT : 2 * NT]
        mid_r, dg_r, du_r, r_ref, c_ref, acc_o, acc_g = refs[2 * NT :]
        i = pl.program_id(0)

        @pl.when(i == 0)
        def _():
            r_ref[...] = join_slots(r_in)
            c_ref[...] = join_slots(c_in)

        rl, rr = r_ref[:, :H], r_ref[:, H:]
        gate = mm(rl, wm[0]) + mm(rr, wo[0])
        up = mm(rl, wm[1]) + mm(rr, wo[1])
        gmid = mm(c_ref[:, :H], wm[2]) + mm(c_ref[:, H:], wo[2])
        sig = jax.nn.sigmoid(gate)
        act = gate * sig
        mid = (act * up).astype(bf16)
        dg = (gmid * up * sig * (1.0 + gate * (1.0 - sig))).astype(bf16)
        du = (gmid * act).astype(bf16)
        mid_r[...] = mid
        dg_r[...] = dg
        du_r[...] = du
        for w, cols in ((wm, slice(0, H)), (wo, slice(H, W))):
            o = mm_nt(mid, w[2])
            g = mm_nt(dg, w[0]) + mm_nt(du, w[1])

            @pl.when(i == 0)
            def _():
                acc_o[:, cols] = o
                acc_g[:, cols] = g

            @pl.when(i > 0)
            def _():
                acc_o[:, cols] += o
                acc_g[:, cols] += g

        @pl.when(i == steps - 1)
        def _():
            put_slots(outs, acc_o)
            put_slots(gnfs, acc_g)

    one = lambda shape: pl.BlockSpec(shape, lambda i: (0,) * len(shape))
    wide = pl.BlockSpec((B, FB), lambda i: (0, i))
    w_spec = pl.BlockSpec((3, H, FB), lambda i: (0, 0, i))
    *ffn_slots, mid, dgate, dup = pl.pallas_call(
        ffn_body,
        grid=(steps,),
        out_shape=[sds((R, W), bf16)] * (2 * NT) + [sds((B, F), bf16)] * 3,
        in_specs=[one((R, W))] * (2 * NT) + [w_spec, w_spec],
        out_specs=[one((R, W))] * (2 * NT) + [wide, wide, wide],
        scratch_shapes=[pltpu.VMEM((B, W), bf16)] * 2 + [pltpu.VMEM((B, W), f32)] * 2,
        cost_estimate=pl.CostEstimate(
            flops=12 * B * W * F, bytes_accessed=6 * W * F + 6 * B * F, transcendentals=B * F
        ),
        name="ffn",
    )(*second_pieces, *cot_pieces, ffn_m, ffn_o)
    gnf_pieces = spread_column(ffn_slots[NT:])

    def dw_body(*refs):
        r_in, c_in, (mid_r, dg_r, du_r, gm, go, rt, ct) = refs[:NT], refs[NT : 2 * NT], refs[2 * NT :]

        @pl.when(pl.program_id(0) == 0)
        def _():
            rt[...] = join_slots(r_in).T
            ct[...] = join_slots(c_in).T

        for k, (lhs, rhs) in enumerate(((rt, dg_r), (rt, du_r), (ct, mid_r))):
            gm[k] = mm(lhs[:H], rhs[...]).astype(bf16)
            go[k] = mm(lhs[H:], rhs[...]).astype(bf16)

    dwf_m, dwf_o = pl.pallas_call(
        dw_body,
        grid=(steps,),
        out_shape=[sds((3, H, F), bf16)] * 2,
        in_specs=[one((R, W))] * (2 * NT) + [wide, wide, wide],
        out_specs=[w_spec, w_spec],
        scratch_shapes=[pltpu.VMEM((W, B), bf16)] * 2,
        cost_estimate=pl.CostEstimate(
            flops=6 * B * W * F, bytes_accessed=6 * W * F + 6 * B * F, transcendentals=0
        ),
        name="ffn_weights",
    )(*second_pieces, *cot_pieces, mid, dgate, dup)
    ffn_own, ffn_sends = merge_core(dwf_m, plane(dwf_o, 1))
    gnf_pieces, ffn_own, ffn_sends = lax.optimization_barrier((gnf_pieces, ffn_own, ffn_sends))
    ffn_got = [plane(v, 2 * (i + 1)) for i, v in enumerate(ffn_sends)]

    def back_body(*refs):
        pieces, outs_in = refs[:NT], refs[NT : 2 * NT]
        res, c_ref, g_ref, om, oo, gres, gg, *more = refs[2 * NT :]
        gas, both = more[:NT], more[NT:]
        grad = sum(p[...].astype(f32) for p in pieces)
        x = res[...]
        inv = lax.rsqrt(jnp.mean(x * x, axis=-1, keepdims=True) + epsilon)
        hat = x * inv
        gg[...] = jnp.sum(grad * hat, axis=0, keepdims=True)
        scaled = grad * g_ref[1:2, :]
        through = inv * (scaled - hat * jnp.mean(scaled * hat, axis=-1, keepdims=True))
        total = c_ref[...].astype(f32) + through
        gres[...] = total
        half = total.astype(bf16)
        for k, ref in enumerate(both):
            ref[:R] = half
            ref[R:] = outs_in[k][...]
        ga = (mm(half[:, :H], om[0]) + mm(half[:, H:], oo[0])).astype(bf16)
        for k, ref in enumerate(gas):
            ref[...] = ga[:, k * C : (k + 1) * C]

    grad_resid, ffn_gain_part, *ga_slots = whole_call(
        back_body,
        [sds((R, W), f32), sds((1, W), f32)]
        + [sds((R, C), bf16)] * NT
        + [sds((2 * R, W), bf16)] * NT,
        (*gnf_pieces, *ffn_slots[:NT], resid, cot, gain2, out_m, out_o),
        2 * R * W * W,
        scalars=False,
    )
    ga_slots, both_slots = ga_slots[:NT], ga_slots[NT:]
    ga_pieces = spread_column(ga_slots)
    *both_slots, ga_pieces = lax.optimization_barrier((*both_slots, ga_pieces))
    both_pieces = spread_column(both_slots)

    def bwd_body(s_ref, q_ref, a_ref, l_ref, *refs):
        d_in, kv_in = refs[:NT], refs[NT : NT + NC]
        dq_ref, even, odd, qz, dz, acc, dl, kv_ref = refs[NT + NC :]
        r, h = pl.program_id(0), pl.program_id(1)
        here = s_ref[1]

        @pl.when((r == 0) & (h == 0))
        def _():
            d_all = join_slots(d_in).astype(f32)
            for hd in range(QH):
                cols = slice((hd // 2) * pw, (hd // 2 + 1) * pw)
                qz[hd] = widen(q_ref[:, cols].astype(f32), hd % 2).astype(bf16)
                dz[hd] = widen_high(d_all[:, cols], hd % 2).astype(bf16)
            for k in range(NC):
                kv_ref[k] = kv_in[k][...]
            prod = d_all * a_ref[...].astype(f32)
            for hd in range(QH):
                pick = jnp.where(lanes((8, C)) // hw == hd, 1.0, 0.0).astype(f32)
                dl[hd] = lax.dot_general(
                    pick, prod, (((1,), (1,)), ((), ())), precision=exact, preferred_element_type=f32
                )

        here_cols = pl.ds(pl.multiple_of(h * pw, pw), pw)

        def put(value):
            @pl.when(r % 2 == 0)
            def _():
                even[r // 2, :, here_cols] = value

            @pl.when(r % 2 == 1)
            def _():
                odd[r // 2, :, here_cols] = value

        def step(masked):
            kv = kv_ref[r, :, here_cols]
            kvt = kv.astype(f32).T.astype(bf16)
            total = None
            for g in range(2):
                hd = 2 * h + g
                q, d = qz[hd], dz[hd]
                shift = l_ref[hd] * log2e
                p = jnp.exp2(mm_nt(kv, q) * c2 - shift)
                if masked:
                    p = jnp.where(causal(s_ref[2] * R), p, 0.0)
                ds = (p * (mm_nt(kv, d) - dl[hd][0:1])).astype(bf16)
                t = jnp.where(lanes((B, pw)) < hw, mm(ds, q) * scale, mm(p.astype(bf16), d))
                total = t if total is None else total + t
                o = mm(kvt, ds)
                if masked:
                    acc[hd] = o
                else:
                    acc[hd] += o
            put(total.astype(bf16))

        @pl.when(r == 0)
        def _():
            step(True)

        @pl.when((here ^ r) < here)
        def _():
            step(False)

        @pl.when((here ^ r) > here)
        def _():
            put(jnp.zeros((B, pw), bf16))

        @pl.when((r == NC - 1) & (h == KH - 1))
        def _():
            outs = [acc[hd][:hw] for hd in range(QH)]
            dq_ref[...] = jnp.concatenate(outs, axis=0).T * scale

    grad_rot_q, dkv_even, dkv_odd = pl.pallas_call(
        bwd_body,
        grid=(NC, KH),
        out_shape=[sds((B, C), f32)] + [sds((NC // 2, B, C), bf16)] * 2,
        in_specs=[SM, fixed((B, C)), fixed((B, C)), fixed((QH, 1, B))]
        + [fixed((R, C))] * NT
        + [fixed((B, C))] * NC,
        out_specs=[fixed((B, C))] + [fixed((NC // 2, B, C))] * 2,
        scratch_shapes=[
            pltpu.VMEM((QH, B, pw), bf16),
            pltpu.VMEM((QH, B, pw), bf16),
            pltpu.VMEM((QH, pw, B), f32),
            pltpu.VMEM((QH, 8, B), f32),
            pltpu.VMEM((NC, B, C), bf16),
        ],
        cost_estimate=pl.CostEstimate(
            flops=40 * QH * B * B * pw, bytes_accessed=8 * B * C * 2, transcendentals=4 * QH * B * B
        ),
        name="attention_backward",
    )(where, rot_q, attended, lse, *ga_pieces, *kv_pieces)

    odd = lax.ppermute(dkv_odd, "ctx", [(i, i ^ 1) for i in range(NC)])
    pair_parts = []
    for k in range(1, NC // 2):
        part = (dkv_even[k].astype(f32) + odd[k].astype(f32)).astype(bf16)
        pair_parts.append(along(part, 2 * k, lambda i, j: i // 2 > j // 2))

    def qk_body(s_ref, dq, even, odd_ref, q_raw_r, p_raw_r, cs, sn, qg_ref, kg_ref, wm, wo, g_ref, fg_ref, *refs):
        index = s_ref[0]
        n_parts = len(pair_parts)
        parts, r_in, gnas = refs[:n_parts], refs[n_parts : n_parts + NT], refs[n_parts + NT : n_parts + 2 * NT]
        both_ref, pack = refs[n_parts + 2 * NT :]
        r_all = jnp.concatenate([ref[:, :W] for ref in r_in], axis=0)

        def back(grad, raw, gain, live):
            turned = grad * cs[...] - swap_halves(grad) * sn[...]
            inv = lax.rsqrt(head_mean(raw * raw) + epsilon)
            hat = raw * inv
            scaled = turned * gain
            out = inv * (scaled - hat * head_mean(scaled * hat))
            gg = jnp.sum(turned * hat, axis=0, keepdims=True)
            if live is not None:
                out = jnp.where(live, out, grad)
            return out.astype(bf16), gg

        dp = even[0].astype(f32) + odd_ref[0].astype(f32)
        for p in parts:
            dp = dp + p[...].astype(f32)
        gq, qsum = back(dq[...], q_raw_r[...], qg_ref[...], None)
        live = lanes((B, C)) % pw < hw
        gp, ksum = back(dp, p_raw_r[...], kg_ref[...], live)
        both_ref[...] = jnp.concatenate([gq, gp], axis=1)
        pack[...] = jnp.zeros_like(pack)
        for w, cols, first in ((wm, slice(0, H), 0), (wo, slice(H, W), N // 2)):
            part = mm_nt(gq, w[0]) + mm_nt(gp, w[1])
            for k, ref in enumerate(gnas):
                ref[:, cols] = part[k * R : (k + 1) * R].astype(bf16)
            agg = jnp.sum(part * r_all[:, cols].astype(f32), axis=0, keepdims=True) / g_ref[0:1, cols]
            for i in range(N // 2):
                to = index ^ masks[first + i]
                pack[pl.ds(to, 1), :] = agg[:, i * blk : (i + 1) * blk]
                pack[pl.ds(N + to, 1), :] = fg_ref[:, (first + i) * blk : (first + i + 1) * blk]
        heads_q = sum(qsum[:, i * pw : (i + 1) * pw] for i in range(KH))
        heads_q = heads_q + pltpu.roll(heads_q, hw, 1)
        heads_k = sum(ksum[:, i * pw : (i + 1) * pw] for i in range(KH))
        pack[2 * N : 2 * N + 1, :hw] = heads_q[:, :hw]
        pack[2 * N + 1 : 2 * N + 2, :hw] = heads_k[:, :hw]

    *gna_slots, both16, packed = whole_call(
        qk_body,
        [sds((R, W), bf16)] * NT + [sds((B, 2 * C), bf16), sds((2 * N + 8, blk), f32)],
        (
            where, grad_rot_q, dkv_even, odd, q_raw, p_raw, cosine, sine, qg, kg,
            qkv_m, qkv_o, gain2, ffn_gain_part, *pair_parts, *first_pieces,
        ),
        4 * B * W * C,
    )
    gna_pieces = spread_column(gna_slots)

    *both_pieces, both16 = lax.optimization_barrier((*both_pieces, both16))

    def last_body(*refs):
        r_in, g_in, (a_ref, b_ref, gm, go) = refs[:NT], refs[NT : 2 * NT], refs[2 * NT :]
        rt = jnp.concatenate([ref[:, :W] for ref in r_in], axis=0).T
        gt = jnp.concatenate([ref[:R] for ref in g_in], axis=0).T
        for ref, rows in ((gm, slice(0, H)), (go, slice(H, W))):
            full = mm(rt[rows], b_ref[...]).astype(bf16)
            ref[0] = full[:, :C]
            ref[1] = full[:, C:]
            ref[2] = mm(gt[rows], a_ref[...]).astype(bf16)

    last_m, last_o = whole_call(
        last_body,
        [sds((3, H, C), bf16)] * 2,
        (*first_pieces, *both_pieces, attended, both16),
        6 * B * W * C,
        scalars=False,
    )
    att_own, att_sends = merge_core(last_m, plane(last_o, 1))
    att_got = [plane(v, 2 * (i + 1)) for i, v in enumerate(att_sends)]

    packed = sum(gather_column(packed))
    bit = 1
    while bit < N:
        packed = packed + plane(packed, bit)
        bit *= 2

    grad_gate, grad_up, grad_down = close_sum(ffn_own, ffn_got)
    grad_query, grad_pairs, grad_output = close_sum(att_own, att_got)

    def end_body(*refs):
        s_ref, rest = refs[0], refs[1:]
        gp, fp, (t_ref, res, gres, g_ref, gt, bo) = rest[:NT], rest[NT : 2 * NT], rest[2 * NT :]
        index = s_ref[0]
        grad = sum(p[...].astype(f32) for p in gp)
        x = t_ref[...].astype(f32)
        inv = lax.rsqrt(jnp.mean(x * x, axis=-1, keepdims=True) + epsilon)
        hat = x * inv
        scaled = grad * g_ref[0:1, :]
        total = gres[...] + inv * (scaled - hat * jnp.mean(scaled * hat, axis=-1, keepdims=True))
        block = (res[...] + sum(p[R:].astype(f32) for p in fp)).astype(bf16)
        for s, mask in enumerate(masks):
            src = slice(s * blk, (s + 1) * blk)
            if aligned:
                dst = pl.ds(pl.multiple_of((index ^ mask) * blk, blk), blk)
            else:
                dst = src
            gt[:, dst] = total[:, src]
            bo[:, dst] = block[:, src]

    gna_pieces, packed, grad_down, grad_output = lax.optimization_barrier(
        (gna_pieces, packed, grad_down, grad_output)
    )
    grad_tokens, block_out = whole_call(
        end_body,
        [sds((R, W), f32), sds((R, W), bf16)],
        (where, *gna_pieces, *both_pieces, tok, resid, grad_resid, gain2),
        R * W * 16,
    )
    if not aligned:
        inverse = [masks.index(m) for m in range(N)]
        slot_of = jnp.take(jnp.array(inverse), me ^ jnp.arange(N, dtype=jnp.int32))
        back_cols = lambda v: jnp.take(
            v.reshape(R, N, blk), slot_of, axis=1
        ).reshape(R, W)
        grad_tokens, block_out = back_cols(grad_tokens), back_cols(block_out)

    lse_out = jnp.take(
        lse.reshape(QH, NT, R), z ^ jnp.arange(NT, dtype=jnp.int32), axis=1
    ).reshape(1, QH, B)
    return (
        block_out[None],
        grad_tokens[None],
        lse_out,
        packed[:N].reshape(W),
        grad_query,
        grad_pairs,
        packed[2 * N, :hw],
        packed[2 * N + 1, :hw],
        grad_output,
        packed[N : 2 * N].reshape(W),
        grad_gate,
        grad_up,
        grad_down,
    )


def solution(mesh):
    in_specs = (
        P("dp", ("ctx", "tp"), None),
        P(),
        P(("dp", "ctx"), "tp"),
        P(("dp", "ctx"), "tp"),
        P(),
        P(),
        P("tp", ("dp", "ctx")),
        P(),
        P(("dp", "ctx"), "tp"),
        P(("dp", "ctx"), "tp"),
        P("tp", ("dp", "ctx")),
        P("dp", ("ctx", "tp"), None),
    )
    out_specs = (
        P("dp", ("ctx", "tp"), None),
        P("dp", ("ctx", "tp"), None),
        P("dp", "tp", "ctx"),
        P(),
        P(("dp", "ctx"), "tp"),
        P(("dp", "ctx"), "tp"),
        P(),
        P(),
        P("tp", ("dp", "ctx")),
        P(),
        P(("dp", "ctx"), "tp"),
        P(("dp", "ctx"), "tp"),
        P("tp", ("dp", "ctx")),
    )

    return jax.shard_map(
        on_device, mesh=mesh, in_specs=in_specs, out_specs=out_specs, check_vma=False
    )
```

```python
import math

import jax
import jax.numpy as jnp
from jax import lax
from jax.experimental import pallas as pl
from jax.experimental.pallas import tpu as pltpu
from jax.sharding import PartitionSpec as P


epsilon = 1e-05
rope_base = 1000000.0
f32 = jnp.float32
bf16 = jnp.bfloat16
exact = lax.Precision.HIGHEST
log2e = math.log2(math.e)


def mm(a, b):
    return lax.dot_general(a, b, (((1,), (0,)), ((), ())), preferred_element_type=f32)


def mm_nt(a, b):
    return lax.dot_general(a, b, (((1,), (1,)), ((), ())), preferred_element_type=f32)


def lanes(shape):
    return lax.broadcasted_iota(jnp.int32, shape, len(shape) - 1)


def rows_of(shape):
    return lax.broadcasted_iota(jnp.int32, shape, 0)


def sds(shape, dtype):
    return jax.ShapeDtypeStruct(shape, dtype)


VM = pl.BlockSpec(memory_space=pltpu.VMEM)
SM = pl.BlockSpec(memory_space=pltpu.SMEM)


def whole_call(body, outs, args, flops, scratch=(), scalars=True):
    moved = sum(math.prod(a.shape) * a.dtype.itemsize for a in list(args) + list(outs))
    specs = [VM] * len(args)
    if scalars:
        specs[0] = SM
    return pl.pallas_call(
        body,
        out_shape=list(outs),
        in_specs=specs,
        out_specs=[VM] * len(outs),
        scratch_shapes=list(scratch),
        cost_estimate=pl.CostEstimate(flops=int(flops), bytes_accessed=int(moved), transcendentals=0),
    )(*args)


def on_device(
    tokens,
    attention_gain,
    query_weight,
    key_value_weight,
    query_gain,
    key_gain,
    output_weight,
    ffn_gain,
    gate_weight,
    up_weight,
    down_weight,
    cotangent,
):
    hw = query_gain.shape[0]
    pw = 2 * hw
    R = tokens.shape[1]
    W = tokens.shape[2]
    NT = lax.axis_size("tp")
    NC = lax.axis_size("ctx")
    N = lax.axis_size("dp") * NC
    B = R * NT
    C = query_weight.shape[1]
    F = gate_weight.shape[1]
    QH = C // hw
    KH = key_value_weight.shape[1] // pw
    assert QH == 2 * KH
    H = W // 2
    blk = W // N
    scale = 1.0 / math.sqrt(hw)
    c2 = scale * log2e
    masks = list(range(0, N, 2)) + list(range(1, N, 2))
    me = lax.axis_index("dp") * NC + lax.axis_index("ctx")
    ctx = lax.axis_index("ctx")
    z = lax.axis_index("tp")
    where = jnp.stack([me, ctx, z]).astype(jnp.int32)
    aligned = blk % 128 == 0
    assert R == blk

    def plane(v, mask):
        return lax.ppermute(v, ("dp", "ctx"), [(i, i ^ mask) for i in range(N)])

    def column(v, mask):
        return lax.ppermute(v, "tp", [(i, i ^ mask) for i in range(NT)])

    def along(v, mask, keep):
        pairs = [(i, i ^ mask) for i in range(NC) if keep(i, i ^ mask)]
        return lax.ppermute(v, "ctx", pairs)

    def after(v, *deps):
        return lax.optimization_barrier((v,) + deps)[0]

    def gather_near(own):
        return [own] + [plane(own, r) for r in range(2, N, 2)]

    def gather_core(near):
        mine = jnp.concatenate(near, axis=1)
        return mine, plane(mine, 1)

    def merge_core(mine, got):
        kinds, half, cols = mine.shape
        m = half * 2 // N

        def body(a, b, first, *rest):
            for i in range(N // 2):
                rows = slice(i * m, (i + 1) * m)
                total = a[0, rows].astype(f32) + b[0, rows].astype(f32)
                if i == 0:
                    first[0] = total
                else:
                    rest[i - 1][0] = total.astype(bf16)

        big = pl.BlockSpec((1, half, cols), lambda k: (k, 0, 0))
        small = pl.BlockSpec((1, m, cols), lambda k: (k, 0, 0))
        own, *sends = pl.pallas_call(
            body,
            grid=(kinds,),
            out_shape=[sds((kinds, m, cols), f32)] + [sds((kinds, m, cols), bf16)] * (N // 2 - 1),
            in_specs=[big, big],
            out_specs=[small] * (N // 2),
            cost_estimate=pl.CostEstimate(
                flops=kinds * half * cols, bytes_accessed=7 * kinds * half * cols, transcendentals=0
            ),
        )(mine, got)
        return own, sends

    def close_sum(own, parts):
        kinds, m, cols = own.shape

        def body(first, *refs):
            parts, outs = refs[: len(parts_in)], refs[len(parts_in) :]
            for k in range(kinds):
                total = first[k]
                for p in parts:
                    total = total + p[k].astype(f32)
                outs[k][...] = total if k < kinds - 1 else total.T

        parts_in = parts
        return whole_call(
            body,
            [sds((m, cols), f32)] * (kinds - 1) + [sds((cols, m), f32)],
            (own, *parts),
            own.size * N,
            scalars=False,
        )

    def gather_column(own):
        return [own] + [column(own, k) for k in range(1, NT)]

    def spread_column(pieces):
        return [pieces[0]] + [column(pieces[k], k) for k in range(1, NT)]

    def put_slots(refs, value):
        for k, ref in enumerate(refs):
            ref[...] = value[k * R : (k + 1) * R].astype(ref.dtype)

    def join_slots(refs):
        return jnp.concatenate([ref[...] for ref in refs], axis=0)

    def take_cols(v, index, size, order):
        picks = index ^ jnp.array(order, jnp.int32)
        return jnp.take(v.reshape(v.shape[0], -1, size), picks, axis=1).reshape(v.shape)

    own_qkv = jnp.stack([query_weight, key_value_weight])

    def pre_body(s_ref, t_ref, c_ref, g_ref, o_ref, n_ref, t_out, c_out, g_out):
        index = s_ref[0]
        for s, mask in enumerate(masks):
            if aligned:
                src = pl.ds(pl.multiple_of((index ^ mask) * blk, blk), blk)
            else:
                src = slice(s * blk, (s + 1) * blk)
            dst = slice(s * blk, (s + 1) * blk)
            t_out[:, dst] = t_ref[:, src]
            c_out[:, dst] = c_ref[:, src]
            g_out[:, dst] = g_ref[:, src]
        x = t_out[...].astype(f32)
        inv = lax.rsqrt(jnp.mean(x * x, axis=-1, keepdims=True) + epsilon)
        n_ref[:, :W] = (x * inv * g_out[0:1, :]).astype(bf16)
        n_ref[:, W:] = o_ref[...].T

    gains = jnp.stack([attention_gain, ffn_gain])
    t_in, c_in, g_in = tokens[0], cotangent[0], gains
    if not aligned:
        t_in, c_in, g_in = (take_cols(v, me, blk, masks) for v in (t_in, c_in, g_in))
    normed, tok, cot, gain2 = whole_call(
        pre_body,
        [sds((R, W + C), bf16), sds((R, W), bf16), sds((R, W), bf16), sds((2, W), f32)],
        (where, t_in, c_in, g_in, output_weight),
        R * W * 8,
    )
    first_pieces = gather_column(normed)
    qkv_near = gather_near(after(own_qkv, normed))
    qkv_m, qkv_o = gather_core(qkv_near)
    own_ffn = jnp.stack([gate_weight, up_weight, down_weight.T])
    ffn_near = gather_near(after(own_ffn, normed))
    out_cols = jnp.concatenate([p[:, W:] for p in first_pieces], axis=1)[None]
    out_near = gather_near(out_cols)
    cot_pieces = gather_column(after(cot, *first_pieces))

    half_width = hw // 2
    freq = jnp.exp(jnp.arange(half_width, dtype=f32) * (-2.0 * math.log(rope_base) / hw))
    positions = ctx * B + (jnp.arange(B, dtype=jnp.int32) ^ (z * R))
    angle = positions.astype(f32)[:, None] * freq[None, :]
    cos_h, sin_h = jnp.cos(angle), jnp.sin(angle)
    cosine = jnp.tile(cos_h, (1, 2 * QH))
    sine = jnp.tile(jnp.concatenate([-sin_h, sin_h], -1), (1, QH))
    qg = jnp.tile(query_gain, QH)[None]
    kg = jnp.tile(jnp.concatenate([key_gain, jnp.ones_like(key_gain)]), KH)[None]

    def head_mean(x):
        n = x.shape[1]
        same = rows_of((n, n)) // hw == lanes((n, n)) // hw
        ones = jnp.where(same, 1.0 / hw, 0.0).astype(bf16)
        high = x.astype(bf16)
        rest = x - high.astype(f32)
        low = rest.astype(bf16)
        tail = (rest - low.astype(f32)).astype(bf16)
        return mm(high, ones) + mm(low, ones) + mm(tail, ones)

    def swap_halves(x):
        first = lanes(x.shape) % hw < half_width
        return jnp.where(
            first, pltpu.roll(x, x.shape[1] - half_width, 1), pltpu.roll(x, half_width, 1)
        )

    def qkv_body(*refs):
        wm, wo, cs, sn, qg_ref, kg_ref, rq, pr, q_raw, p_raw = refs[NT:]
        rows = join_slots(refs[:NT])
        left, right = rows[:, :H], rows[:, H:W]
        q = mm(left, wm[0]) + mm(right, wo[0])
        p = mm(left, wm[1]) + mm(right, wo[1])
        q_raw[...] = q
        p_raw[...] = p
        qn = q * lax.rsqrt(head_mean(q * q) + epsilon) * qg_ref[...]
        rq[...] = (qn * cs[...] + swap_halves(qn) * sn[...]).astype(bf16)
        kn = p * lax.rsqrt(head_mean(p * p) + epsilon) * kg_ref[...]
        kr = kn * cs[...] + swap_halves(kn) * sn[...]
        pr[...] = jnp.where(lanes(p.shape) % pw < hw, kr, p).astype(bf16)

    rot_q, pair, q_raw, p_raw = whole_call(
        qkv_body,
        [sds((B, C), bf16), sds((B, C), bf16), sds((B, C), f32), sds((B, C), f32)],
        (*first_pieces, qkv_m, qkv_o, cosine, sine, qg, kg),
        4 * B * W * C,
        scalars=False,
    )

    earlier = lambda i, j: i < j
    kv_even = [pair] + [along(pair, r, earlier) for r in range(2, NC, 2)]
    kv_odd = [along(pair, 1, earlier)]
    for r in range(2, NC, 2):
        kv_odd.append(along(kv_even[r // 2], 1, lambda i, j: (i ^ r) < i))
    kv_pieces = [v for pq in zip(kv_even, kv_odd) for v in pq]
    out_m, out_o = gather_core(out_near)

    def widen(x, part):
        moved = x if part == 0 else pltpu.roll(x, hw, 1)
        return jnp.where(lanes(x.shape) < hw, moved, 0.0)

    def widen_high(x, part):
        moved = x if part == 1 else pltpu.roll(x, hw, 1)
        return jnp.where(lanes(x.shape) >= hw, moved, 0.0)

    def causal(zz):
        key = rows_of((B, B)) ^ zz
        qry = lanes((B, B)) ^ zz
        return key <= qry

    def fwd_body(s_ref, q_ref, *refs):
        kv_in, slot_refs = refs[:NC], refs[NC : NC + NT]
        att_ref, lse_ref, qz, acc, tot, kv_ref = refs[NC + NT :]
        r, h = pl.program_id(0), pl.program_id(1)
        here = s_ref[1]

        @pl.when((r == 0) & (h == 0))
        def _():
            for hd in range(QH):
                x = q_ref[:, (hd // 2) * pw : (hd // 2 + 1) * pw].astype(f32)
                qz[hd] = widen(x, hd % 2).astype(bf16)
            for k in range(NC):
                kv_ref[k] = kv_in[k][...]

        def step(masked):
            kv = kv_ref[r, :, pl.ds(pl.multiple_of(h * pw, pw), pw)]
            kvt = kv.astype(f32).T.astype(bf16)
            for g in range(2):
                hd = 2 * h + g
                e = jnp.exp2(mm_nt(kv, qz[hd]) * c2)
                if masked:
                    e = jnp.where(causal(s_ref[2] * R), e, 0.0)
                part = jnp.sum(e, axis=0, keepdims=True)
                o = mm(kvt, e.astype(bf16))
                if masked:
                    tot[hd] = jnp.broadcast_to(part, (8, B))
                    acc[hd] = o
                else:
                    tot[hd] += jnp.broadcast_to(part, (8, B))
                    acc[hd] += o

        @pl.when(r == 0)
        def _():
            step(True)

        @pl.when((here ^ r) < here)
        def _():
            step(False)

        @pl.when((r == NC - 1) & (h == KH - 1))
        def _():
            outs = [acc[hd][hw:] / tot[hd][0:1] for hd in range(QH)]
            att = jnp.concatenate(outs, axis=0).T.astype(bf16)
            att_ref[...] = att
            put_slots(slot_refs, att)
            for hd in range(QH):
                lse_ref[hd] = jnp.log(tot[hd][0:1])

    fixed = lambda shape: pl.BlockSpec(shape, lambda r, h: (0,) * len(shape))
    *att_slots, attended, lse = pl.pallas_call(
        fwd_body,
        grid=(NC, KH),
        out_shape=[sds((R, C), bf16)] * NT + [sds((B, C), bf16), sds((QH, 1, B), f32)],
        in_specs=[SM] + [fixed((B, C))] * (1 + NC),
        out_specs=[fixed((R, C))] * NT + [fixed((B, C)), fixed((QH, 1, B))],
        scratch_shapes=[
            pltpu.VMEM((QH, B, pw), bf16),
            pltpu.VMEM((QH, pw, B), f32),
            pltpu.VMEM((QH, 8, B), f32),
            pltpu.VMEM((NC, B, C), bf16),
        ],
        cost_estimate=pl.CostEstimate(
            flops=16 * QH * B * B * pw, bytes_accessed=4 * B * C * 2, transcendentals=4 * QH * B * B
        ),
        name="attention_forward",
    )(where, rot_q, *kv_pieces)

    att_pieces = spread_column(att_slots)
    ffn_m, ffn_o = gather_core(ffn_near)

    def out_body(*refs):
        pieces, (om, oo, t_ref, g_ref, res, nrm) = refs[:NT], refs[NT:]
        a = jnp.concatenate([p[...] for p in pieces], axis=1)
        x = t_ref[...].astype(f32) + jnp.concatenate([mm_nt(a, om[0]), mm_nt(a, oo[0])], axis=1)
        res[...] = x
        inv = lax.rsqrt(jnp.mean(x * x, axis=-1, keepdims=True) + epsilon)
        nrm[...] = (x * inv * g_ref[1:2, :]).astype(bf16)

    resid, normed_f = whole_call(
        out_body,
        [sds((R, W), f32), sds((R, W), bf16)],
        (*att_pieces, out_m, out_o, tok, gain2),
        2 * R * W * W,
        scalars=False,
    )
    second_pieces = gather_column(normed_f)

    FB = 384 if F % 384 == 0 else F
    steps = F // FB

    def ffn_body(*refs):
        r_in, c_in, (wm, wo) = refs[:NT], refs[NT : 2 * NT], refs[2 * NT : 2 * NT + 2]
        refs = refs[2 * NT + 2 :]
        outs, gnfs = refs[:NT], refs[NT : 2 * NT]
        mid_r, dg_r, du_r, r_ref, c_ref, acc_o, acc_g = refs[2 * NT :]
        i = pl.program_id(0)

        @pl.when(i == 0)
        def _():
            r_ref[...] = join_slots(r_in)
            c_ref[...] = join_slots(c_in)

        rl, rr = r_ref[:, :H], r_ref[:, H:]
        gate = mm(rl, wm[0]) + mm(rr, wo[0])
        up = mm(rl, wm[1]) + mm(rr, wo[1])
        gmid = mm(c_ref[:, :H], wm[2]) + mm(c_ref[:, H:], wo[2])
        sig = jax.nn.sigmoid(gate)
        act = gate * sig
        mid = (act * up).astype(bf16)
        dg = (gmid * up * sig * (1.0 + gate * (1.0 - sig))).astype(bf16)
        du = (gmid * act).astype(bf16)
        mid_r[...] = mid
        dg_r[...] = dg
        du_r[...] = du
        for w, cols in ((wm, slice(0, H)), (wo, slice(H, W))):
            o = mm_nt(mid, w[2])
            g = mm_nt(dg, w[0]) + mm_nt(du, w[1])

            @pl.when(i == 0)
            def _():
                acc_o[:, cols] = o
                acc_g[:, cols] = g

            @pl.when(i > 0)
            def _():
                acc_o[:, cols] += o
                acc_g[:, cols] += g

        @pl.when(i == steps - 1)
        def _():
            put_slots(outs, acc_o)
            put_slots(gnfs, acc_g)

    one = lambda shape: pl.BlockSpec(shape, lambda i: (0,) * len(shape))
    wide = pl.BlockSpec((B, FB), lambda i: (0, i))
    w_spec = pl.BlockSpec((3, H, FB), lambda i: (0, 0, i))
    *ffn_slots, mid, dgate, dup = pl.pallas_call(
        ffn_body,
        grid=(steps,),
        out_shape=[sds((R, W), bf16)] * (2 * NT) + [sds((B, F), bf16)] * 3,
        in_specs=[one((R, W))] * (2 * NT) + [w_spec, w_spec],
        out_specs=[one((R, W))] * (2 * NT) + [wide, wide, wide],
        scratch_shapes=[pltpu.VMEM((B, W), bf16)] * 2 + [pltpu.VMEM((B, W), f32)] * 2,
        cost_estimate=pl.CostEstimate(
            flops=12 * B * W * F, bytes_accessed=6 * W * F + 6 * B * F, transcendentals=B * F
        ),
        name="ffn",
    )(*second_pieces, *cot_pieces, ffn_m, ffn_o)
    gnf_pieces = spread_column(ffn_slots[NT:])

    def dw_body(*refs):
        r_in, c_in, (mid_r, dg_r, du_r, gm, go, rt, ct) = refs[:NT], refs[NT : 2 * NT], refs[2 * NT :]

        @pl.when(pl.program_id(0) == 0)
        def _():
            rt[...] = join_slots(r_in).T
            ct[...] = join_slots(c_in).T

        for k, (lhs, rhs) in enumerate(((rt, dg_r), (rt, du_r), (ct, mid_r))):
            gm[k] = mm(lhs[:H], rhs[...]).astype(bf16)
            go[k] = mm(lhs[H:], rhs[...]).astype(bf16)

    dwf_m, dwf_o = pl.pallas_call(
        dw_body,
        grid=(steps,),
        out_shape=[sds((3, H, F), bf16)] * 2,
        in_specs=[one((R, W))] * (2 * NT) + [wide, wide, wide],
        out_specs=[w_spec, w_spec],
        scratch_shapes=[pltpu.VMEM((W, B), bf16)] * 2,
        cost_estimate=pl.CostEstimate(
            flops=6 * B * W * F, bytes_accessed=6 * W * F + 6 * B * F, transcendentals=0
        ),
        name="ffn_weights",
    )(*second_pieces, *cot_pieces, mid, dgate, dup)
    ffn_own, ffn_sends = merge_core(dwf_m, plane(dwf_o, 1))
    gnf_pieces, ffn_own, ffn_sends = lax.optimization_barrier((gnf_pieces, ffn_own, ffn_sends))
    ffn_got = [plane(v, 2 * (i + 1)) for i, v in enumerate(ffn_sends)]

    def back_body(*refs):
        pieces, outs_in = refs[:NT], refs[NT : 2 * NT]
        res, c_ref, g_ref, om, oo, gres, gg, *more = refs[2 * NT :]
        gas, both = more[:NT], more[NT:]
        grad = sum(p[...].astype(f32) for p in pieces)
        x = res[...]
        inv = lax.rsqrt(jnp.mean(x * x, axis=-1, keepdims=True) + epsilon)
        hat = x * inv
        gg[...] = jnp.sum(grad * hat, axis=0, keepdims=True)
        scaled = grad * g_ref[1:2, :]
        through = inv * (scaled - hat * jnp.mean(scaled * hat, axis=-1, keepdims=True))
        total = c_ref[...].astype(f32) + through
        gres[...] = total
        half = total.astype(bf16)
        for k, ref in enumerate(both):
            ref[:R] = half
            ref[R:] = outs_in[k][...]
        ga = (mm(half[:, :H], om[0]) + mm(half[:, H:], oo[0])).astype(bf16)
        for k, ref in enumerate(gas):
            ref[...] = ga[:, k * C : (k + 1) * C]

    grad_resid, ffn_gain_part, *ga_slots = whole_call(
        back_body,
        [sds((R, W), f32), sds((1, W), f32)]
        + [sds((R, C), bf16)] * NT
        + [sds((2 * R, W), bf16)] * NT,
        (*gnf_pieces, *ffn_slots[:NT], resid, cot, gain2, out_m, out_o),
        2 * R * W * W,
        scalars=False,
    )
    ga_slots, both_slots = ga_slots[:NT], ga_slots[NT:]
    ga_pieces = spread_column(ga_slots)
    *both_slots, ga_pieces = lax.optimization_barrier((*both_slots, ga_pieces))
    both_pieces = spread_column(both_slots)

    def bwd_body(s_ref, q_ref, a_ref, l_ref, *refs):
        d_in, kv_in = refs[:NT], refs[NT : NT + NC]
        dq_ref, even, odd, qz, dz, acc, dl, kv_ref = refs[NT + NC :]
        r, h = pl.program_id(0), pl.program_id(1)
        here = s_ref[1]

        @pl.when((r == 0) & (h == 0))
        def _():
            d_all = join_slots(d_in).astype(f32)
            for hd in range(QH):
                cols = slice((hd // 2) * pw, (hd // 2 + 1) * pw)
                qz[hd] = widen(q_ref[:, cols].astype(f32), hd % 2).astype(bf16)
                dz[hd] = widen_high(d_all[:, cols], hd % 2).astype(bf16)
            for k in range(NC):
                kv_ref[k] = kv_in[k][...]
            prod = d_all * a_ref[...].astype(f32)
            for hd in range(QH):
                pick = jnp.where(lanes((8, C)) // hw == hd, 1.0, 0.0).astype(f32)
                dl[hd] = lax.dot_general(
                    pick, prod, (((1,), (1,)), ((), ())), precision=exact, preferred_element_type=f32
                )

        here_cols = pl.ds(pl.multiple_of(h * pw, pw), pw)

        def put(value):
            @pl.when(r % 2 == 0)
            def _():
                even[r // 2, :, here_cols] = value

            @pl.when(r % 2 == 1)
            def _():
                odd[r // 2, :, here_cols] = value

        def step(masked):
            kv = kv_ref[r, :, here_cols]
            kvt = kv.astype(f32).T.astype(bf16)
            total = None
            for g in range(2):
                hd = 2 * h + g
                q, d = qz[hd], dz[hd]
                shift = l_ref[hd] * log2e
                p = jnp.exp2(mm_nt(kv, q) * c2 - shift)
                if masked:
                    p = jnp.where(causal(s_ref[2] * R), p, 0.0)
                ds = (p * (mm_nt(kv, d) - dl[hd][0:1])).astype(bf16)
                t = jnp.where(lanes((B, pw)) < hw, mm(ds, q) * scale, mm(p.astype(bf16), d))
                total = t if total is None else total + t
                o = mm(kvt, ds)
                if masked:
                    acc[hd] = o
                else:
                    acc[hd] += o
            put(total.astype(bf16))

        @pl.when(r == 0)
        def _():
            step(True)

        @pl.when((here ^ r) < here)
        def _():
            step(False)

        @pl.when((here ^ r) > here)
        def _():
            put(jnp.zeros((B, pw), bf16))

        @pl.when((r == NC - 1) & (h == KH - 1))
        def _():
            outs = [acc[hd][:hw] for hd in range(QH)]
            dq_ref[...] = jnp.concatenate(outs, axis=0).T * scale

    grad_rot_q, dkv_even, dkv_odd = pl.pallas_call(
        bwd_body,
        grid=(NC, KH),
        out_shape=[sds((B, C), f32)] + [sds((NC // 2, B, C), bf16)] * 2,
        in_specs=[SM, fixed((B, C)), fixed((B, C)), fixed((QH, 1, B))]
        + [fixed((R, C))] * NT
        + [fixed((B, C))] * NC,
        out_specs=[fixed((B, C))] + [fixed((NC // 2, B, C))] * 2,
        scratch_shapes=[
            pltpu.VMEM((QH, B, pw), bf16),
            pltpu.VMEM((QH, B, pw), bf16),
            pltpu.VMEM((QH, pw, B), f32),
            pltpu.VMEM((QH, 8, B), f32),
            pltpu.VMEM((NC, B, C), bf16),
        ],
        cost_estimate=pl.CostEstimate(
            flops=40 * QH * B * B * pw, bytes_accessed=8 * B * C * 2, transcendentals=4 * QH * B * B
        ),
        name="attention_backward",
    )(where, rot_q, attended, lse, *ga_pieces, *kv_pieces)

    odd = lax.ppermute(dkv_odd, "ctx", [(i, i ^ 1) for i in range(NC)])
    pair_parts = []
    for k in range(1, NC // 2):
        part = (dkv_even[k].astype(f32) + odd[k].astype(f32)).astype(bf16)
        pair_parts.append(along(part, 2 * k, lambda i, j: i // 2 > j // 2))

    def qk_body(s_ref, dq, even, odd_ref, q_raw_r, p_raw_r, cs, sn, qg_ref, kg_ref, wm, wo, g_ref, fg_ref, *refs):
        index = s_ref[0]
        n_parts = len(pair_parts)
        parts, r_in, gnas = refs[:n_parts], refs[n_parts : n_parts + NT], refs[n_parts + NT : n_parts + 2 * NT]
        both_ref, pack = refs[n_parts + 2 * NT :]
        r_all = jnp.concatenate([ref[:, :W] for ref in r_in], axis=0)

        def back(grad, raw, gain, live):
            turned = grad * cs[...] - swap_halves(grad) * sn[...]
            inv = lax.rsqrt(head_mean(raw * raw) + epsilon)
            hat = raw * inv
            scaled = turned * gain
            out = inv * (scaled - hat * head_mean(scaled * hat))
            gg = jnp.sum(turned * hat, axis=0, keepdims=True)
            if live is not None:
                out = jnp.where(live, out, grad)
            return out.astype(bf16), gg

        dp = even[0].astype(f32) + odd_ref[0].astype(f32)
        for p in parts:
            dp = dp + p[...].astype(f32)
        gq, qsum = back(dq[...], q_raw_r[...], qg_ref[...], None)
        live = lanes((B, C)) % pw < hw
        gp, ksum = back(dp, p_raw_r[...], kg_ref[...], live)
        both_ref[...] = jnp.concatenate([gq, gp], axis=1)
        pack[...] = jnp.zeros_like(pack)
        for w, cols, first in ((wm, slice(0, H), 0), (wo, slice(H, W), N // 2)):
            part = mm_nt(gq, w[0]) + mm_nt(gp, w[1])
            for k, ref in enumerate(gnas):
                ref[:, cols] = part[k * R : (k + 1) * R].astype(bf16)
            agg = jnp.sum(part * r_all[:, cols].astype(f32), axis=0, keepdims=True) / g_ref[0:1, cols]
            for i in range(N // 2):
                to = index ^ masks[first + i]
                pack[pl.ds(to, 1), :] = agg[:, i * blk : (i + 1) * blk]
                pack[pl.ds(N + to, 1), :] = fg_ref[:, (first + i) * blk : (first + i + 1) * blk]
        heads_q = sum(qsum[:, i * pw : (i + 1) * pw] for i in range(KH))
        heads_q = heads_q + pltpu.roll(heads_q, hw, 1)
        heads_k = sum(ksum[:, i * pw : (i + 1) * pw] for i in range(KH))
        pack[2 * N : 2 * N + 1, :hw] = heads_q[:, :hw]
        pack[2 * N + 1 : 2 * N + 2, :hw] = heads_k[:, :hw]

    *gna_slots, both16, packed = whole_call(
        qk_body,
        [sds((R, W), bf16)] * NT + [sds((B, 2 * C), bf16), sds((2 * N + 8, blk), f32)],
        (
            where, grad_rot_q, dkv_even, odd, q_raw, p_raw, cosine, sine, qg, kg,
            qkv_m, qkv_o, gain2, ffn_gain_part, *pair_parts, *first_pieces,
        ),
        4 * B * W * C,
    )
    gna_pieces = spread_column(gna_slots)

    *both_pieces, both16 = lax.optimization_barrier((*both_pieces, both16))

    def last_body(*refs):
        r_in, g_in, (a_ref, b_ref, gm, go) = refs[:NT], refs[NT : 2 * NT], refs[2 * NT :]
        rt = jnp.concatenate([ref[:, :W] for ref in r_in], axis=0).T
        gt = jnp.concatenate([ref[:R] for ref in g_in], axis=0).T
        for ref, rows in ((gm, slice(0, H)), (go, slice(H, W))):
            full = mm(rt[rows], b_ref[...]).astype(bf16)
            ref[0] = full[:, :C]
            ref[1] = full[:, C:]
            ref[2] = mm(gt[rows], a_ref[...]).astype(bf16)

    last_m, last_o = whole_call(
        last_body,
        [sds((3, H, C), bf16)] * 2,
        (*first_pieces, *both_pieces, attended, both16),
        6 * B * W * C,
        scalars=False,
    )
    att_own, att_sends = merge_core(last_m, plane(last_o, 1))
    att_got = [plane(v, 2 * (i + 1)) for i, v in enumerate(att_sends)]

    def block_body(*refs):
        index = refs[0][0]
        fp, (res, bo) = refs[1 : NT + 1], refs[NT + 1 :]
        block = (res[...] + sum(p[R:].astype(f32) for p in fp)).astype(bf16)
        for s, mask in enumerate(masks):
            src = slice(s * blk, (s + 1) * blk)
            if aligned:
                dst = pl.ds(pl.multiple_of((index ^ mask) * blk, blk), blk)
            else:
                dst = src
            bo[:, dst] = block[:, src]

    (block_out,) = whole_call(
        block_body, [sds((R, W), bf16)], (where, *both_pieces, resid), R * W * 8
    )

    bit = 1
    while bit < N:
        packed = packed + plane(packed, bit)
        bit *= 2
    packed = sum(gather_column(packed))

    grad_gate, grad_up, grad_down = close_sum(ffn_own, ffn_got)
    grad_query, grad_pairs, grad_output = close_sum(att_own, att_got)

    def end_body(*refs):
        s_ref, rest = refs[0], refs[1:]
        gp, (t_ref, gres, g_ref, gt) = rest[:NT], rest[NT:]
        index = s_ref[0]
        grad = sum(p[...].astype(f32) for p in gp)
        x = t_ref[...].astype(f32)
        inv = lax.rsqrt(jnp.mean(x * x, axis=-1, keepdims=True) + epsilon)
        hat = x * inv
        scaled = grad * g_ref[0:1, :]
        total = gres[...] + inv * (scaled - hat * jnp.mean(scaled * hat, axis=-1, keepdims=True))
        for s, mask in enumerate(masks):
            src = slice(s * blk, (s + 1) * blk)
            if aligned:
                dst = pl.ds(pl.multiple_of((index ^ mask) * blk, blk), blk)
            else:
                dst = src
            gt[:, dst] = total[:, src]

    gna_pieces, packed, grad_down, grad_output, block_out = lax.optimization_barrier(
        (gna_pieces, packed, grad_down, grad_output, block_out)
    )
    (grad_tokens,) = whole_call(
        end_body, [sds((R, W), f32)], (where, *gna_pieces, tok, grad_resid, gain2), R * W * 16
    )
    if not aligned:
        inverse = [masks.index(m) for m in range(N)]
        slot_of = jnp.take(jnp.array(inverse), me ^ jnp.arange(N, dtype=jnp.int32))
        back_cols = lambda v: jnp.take(
            v.reshape(R, N, blk), slot_of, axis=1
        ).reshape(R, W)
        grad_tokens, block_out = back_cols(grad_tokens), back_cols(block_out)

    lse_out = jnp.take(
        lse.reshape(QH, NT, R), z ^ jnp.arange(NT, dtype=jnp.int32), axis=1
    ).reshape(1, QH, B)
    return (
        block_out[None],
        grad_tokens[None],
        lse_out,
        packed[:N].reshape(W),
        grad_query,
        grad_pairs,
        packed[2 * N, :hw],
        packed[2 * N + 1, :hw],
        grad_output,
        packed[N : 2 * N].reshape(W),
        grad_gate,
        grad_up,
        grad_down,
    )


def solution(mesh):
    in_specs = (
        P("dp", ("ctx", "tp"), None),
        P(),
        P(("dp", "ctx"), "tp"),
        P(("dp", "ctx"), "tp"),
        P(),
        P(),
        P("tp", ("dp", "ctx")),
        P(),
        P(("dp", "ctx"), "tp"),
        P(("dp", "ctx"), "tp"),
        P("tp", ("dp", "ctx")),
        P("dp", ("ctx", "tp"), None),
    )
    out_specs = (
        P("dp", ("ctx", "tp"), None),
        P("dp", ("ctx", "tp"), None),
        P("dp", "tp", "ctx"),
        P(),
        P(("dp", "ctx"), "tp"),
        P(("dp", "ctx"), "tp"),
        P(),
        P(),
        P("tp", ("dp", "ctx")),
        P(),
        P(("dp", "ctx"), "tp"),
        P(("dp", "ctx"), "tp"),
        P("tp", ("dp", "ctx")),
    )

    return jax.shard_map(
        on_device, mesh=mesh, in_specs=in_specs, out_specs=out_specs, check_vma=False
    )
```

```python
import functools
import math

import jax
import jax.numpy as jnp
from jax import lax
from jax.experimental import pallas as pl
from jax.experimental.pallas import tpu as pltpu
from jax.sharding import PartitionSpec as P


epsilon = 1e-05
rope_base = 1000000.0
f32 = jnp.float32
bf16 = jnp.bfloat16
log2e = math.log2(math.e)


def mm(a, b):
    return lax.dot_general(a, b, (((1,), (0,)), ((), ())), preferred_element_type=f32)


def mm_nt(a, b):
    return lax.dot_general(a, b, (((1,), (1,)), ((), ())), preferred_element_type=f32)


def lanes(shape):
    return lax.broadcasted_iota(jnp.int32, shape, len(shape) - 1)


def rows_of(shape):
    return lax.broadcasted_iota(jnp.int32, shape, 0)


def sds(shape, dtype):
    return jax.ShapeDtypeStruct(shape, dtype)


VM = pl.BlockSpec(memory_space=pltpu.VMEM)
SM = pl.BlockSpec(memory_space=pltpu.SMEM)


def whole_call(body, outs, args, flops, scratch=(), scalars=True):
    moved = sum(math.prod(a.shape) * a.dtype.itemsize for a in list(args) + list(outs))
    specs = [VM] * len(args)
    if scalars:
        specs[0] = SM
    return pl.pallas_call(
        body,
        out_shape=list(outs),
        in_specs=specs,
        out_specs=[VM] * len(outs),
        scratch_shapes=list(scratch),
        cost_estimate=pl.CostEstimate(flops=int(flops), bytes_accessed=int(moved), transcendentals=0),
    )(*args)


def on_device(
    tokens,
    attention_gain,
    query_weight,
    key_value_weight,
    query_gain,
    key_gain,
    output_weight,
    ffn_gain,
    gate_weight,
    up_weight,
    down_weight,
    cotangent,
):
    hw = query_gain.shape[0]
    pw = 2 * hw
    R = tokens.shape[1]
    W = tokens.shape[2]
    NT = lax.axis_size("tp")
    NC = lax.axis_size("ctx")
    N = lax.axis_size("dp") * NC
    B = R * NT
    C = query_weight.shape[1]
    F = gate_weight.shape[1]
    QH = C // hw
    KH = key_value_weight.shape[1] // pw
    assert QH == 2 * KH
    H = W // 2
    blk = W // N
    scale = 1.0 / math.sqrt(hw)
    c2 = scale * log2e
    masks = list(range(0, N, 2)) + list(range(1, N, 2))
    me = lax.axis_index("dp") * NC + lax.axis_index("ctx")
    ctx = lax.axis_index("ctx")
    z = lax.axis_index("tp")
    where = jnp.stack([me, ctx, z]).astype(jnp.int32)
    aligned = blk % 128 == 0

    def plane(v, mask):
        return lax.ppermute(v, ("dp", "ctx"), [(i, i ^ mask) for i in range(N)])

    def column(v, mask):
        return lax.ppermute(v, "tp", [(i, i ^ mask) for i in range(NT)])

    def along(v, mask, keep):
        pairs = [(i, i ^ mask) for i in range(NC) if keep(i, i ^ mask)]
        return lax.ppermute(v, "ctx", pairs)

    def after(v, *deps):
        return lax.optimization_barrier((v,) + deps)[0]

    def gather_near(own):
        return [own] + [plane(own, r) for r in range(2, N, 2)]

    def gather_core(near):
        mine = jnp.concatenate(near, axis=1)
        return mine, plane(mine, 1)

    def merge_core(mine, got):
        kinds, half, cols = mine.shape
        m = half * 2 // N

        def body(a, b, first, *rest):
            for i in range(N // 2):
                rows = slice(i * m, (i + 1) * m)
                total = a[0, rows].astype(f32) + b[0, rows].astype(f32)
                if i == 0:
                    first[0] = total
                else:
                    rest[i - 1][0] = total.astype(bf16)

        part = 384 if cols % 384 == 0 else cols
        big = pl.BlockSpec((1, half, part), lambda k, i: (k, 0, i))
        small = pl.BlockSpec((1, m, part), lambda k, i: (k, 0, i))
        own, *sends = pl.pallas_call(
            body,
            grid=(kinds, cols // part),
            out_shape=[sds((kinds, m, cols), f32)] + [sds((kinds, m, cols), bf16)] * (N // 2 - 1),
            in_specs=[big, big],
            out_specs=[small] * (N // 2),
            cost_estimate=pl.CostEstimate(
                flops=kinds * half * cols, bytes_accessed=7 * kinds * half * cols, transcendentals=0
            ),
        )(mine, got)
        return own, sends

    def close_sum(own, parts):
        kinds, m, cols = own.shape

        def body(first, *refs):
            parts, outs = refs[: len(parts_in)], refs[len(parts_in) :]
            for k in range(kinds):
                total = first[k]
                for p in parts:
                    total = total + p[k].astype(f32)
                outs[k][...] = total if k < kinds - 1 else total.T

        parts_in = parts
        return whole_call(
            body,
            [sds((m, cols), f32)] * (kinds - 1) + [sds((cols, m), f32)],
            (own, *parts),
            own.size * N,
            scalars=False,
        )

    def gather_column(own):
        return [own] + [column(own, k) for k in range(1, NT)]

    def spread_column(pieces):
        return [pieces[0]] + [column(pieces[k], k) for k in range(1, NT)]

    def put_slots(refs, value):
        for k, ref in enumerate(refs):
            ref[...] = value[k * R : (k + 1) * R].astype(ref.dtype)

    def join_slots(refs):
        return jnp.concatenate([ref[...] for ref in refs], axis=0)

    def take_cols(v, index, size, order):
        picks = index ^ jnp.array(order, jnp.int32)
        return jnp.take(v.reshape(v.shape[0], -1, size), picks, axis=1).reshape(v.shape)

    own_qkv = jnp.stack([query_weight, key_value_weight])

    def pre_body(s_ref, t_ref, c_ref, g_ref, o_ref, n_ref, t_out, c_out, g_out, ot_out):
        index = s_ref[0]
        for s, mask in enumerate(masks):
            if aligned:
                src = pl.ds(pl.multiple_of((index ^ mask) * blk, blk), blk)
            else:
                src = slice(s * blk, (s + 1) * blk)
            dst = slice(s * blk, (s + 1) * blk)
            t_out[:, dst] = t_ref[:, src]
            c_out[:, dst] = c_ref[:, src]
            g_out[:, dst] = g_ref[:, src]
        x = t_out[...].astype(f32)
        inv = lax.rsqrt(jnp.mean(x * x, axis=-1, keepdims=True) + epsilon)
        n_ref[...] = (x * inv * g_out[0:1, :]).astype(bf16)
        ot_out[...] = o_ref[...].T

    gains = jnp.stack([attention_gain, ffn_gain])
    t_in, c_in, g_in = tokens[0], cotangent[0], gains
    if not aligned:
        t_in, c_in, g_in = (take_cols(v, me, blk, masks) for v in (t_in, c_in, g_in))
    normed, tok, cot, gain2, own_out = whole_call(
        pre_body,
        [sds((R, W), bf16)] * 3 + [sds((2, W), f32), sds((blk, C), bf16)],
        (where, t_in, c_in, g_in, output_weight),
        R * W * 8,
    )
    first_pieces = gather_column(normed)
    qkv_near = gather_near(after(own_qkv, normed))
    qkv_m, qkv_o = gather_core(qkv_near)
    own_ffn = jnp.stack([gate_weight, up_weight, down_weight.T])
    ffn_near = gather_near(after(own_ffn, normed))
    out_cols = jnp.concatenate(gather_column(own_out), axis=1)[None]
    out_near = gather_near(out_cols)
    cot_pieces = gather_column(cot)

    half_width = hw // 2
    freq = jnp.exp(jnp.arange(half_width, dtype=f32) * (-2.0 * math.log(rope_base) / hw))
    positions = ctx * B + (jnp.arange(B, dtype=jnp.int32) ^ (z * R))
    angle = positions.astype(f32)[:, None] * freq[None, :]
    cos_h, sin_h = jnp.cos(angle), jnp.sin(angle)
    cosine = jnp.tile(cos_h, (1, 2 * QH))
    sine = jnp.tile(jnp.concatenate([-sin_h, sin_h], -1), (1, QH))
    qg = jnp.tile(query_gain, QH)[None]
    kg = jnp.tile(jnp.concatenate([key_gain, jnp.ones_like(key_gain)]), KH)[None]

    def three_terms(x):
        high = x.astype(bf16)
        rest = x - high.astype(f32)
        low = rest.astype(bf16)
        return high, low, (rest - low.astype(f32)).astype(bf16)

    def head_mean(x):
        n = x.shape[1]
        same = rows_of((n, n)) // hw == lanes((n, n)) // hw
        ones = jnp.where(same, 1.0 / hw, 0.0).astype(bf16)
        return sum(mm(term, ones) for term in three_terms(x))

    def swap_halves(x):
        first = lanes(x.shape) % hw < half_width
        return jnp.where(
            first, pltpu.roll(x, x.shape[1] - half_width, 1), pltpu.roll(x, half_width, 1)
        )

    def qkv_body(*refs):
        wm, wo, cs, sn, qg_ref, kg_ref, rq, pr, q_raw, p_raw = refs[NT:]
        rows = join_slots(refs[:NT])
        left, right = rows[:, :H], rows[:, H:]
        q = mm(left, wm[0]) + mm(right, wo[0])
        p = mm(left, wm[1]) + mm(right, wo[1])
        q_raw[...] = q
        p_raw[...] = p
        qn = q * lax.rsqrt(head_mean(q * q) + epsilon) * qg_ref[...]
        rq[...] = (qn * cs[...] + swap_halves(qn) * sn[...]).astype(bf16)
        kn = p * lax.rsqrt(head_mean(p * p) + epsilon) * kg_ref[...]
        kr = kn * cs[...] + swap_halves(kn) * sn[...]
        pr[...] = jnp.where(lanes(p.shape) % pw < hw, kr, p).astype(bf16)

    rot_q, pair, q_raw, p_raw = whole_call(
        qkv_body,
        [sds((B, C), bf16), sds((B, C), bf16), sds((B, C), f32), sds((B, C), f32)],
        (*first_pieces, qkv_m, qkv_o, cosine, sine, qg, kg),
        4 * B * W * C,
        scalars=False,
    )

    earlier = lambda i, j: i < j
    kv_even = [pair] + [along(pair, r, earlier) for r in range(2, NC, 2)]
    kv_odd = [along(pair, 1, earlier)]
    for r in range(2, NC, 2):
        kv_odd.append(along(kv_even[r // 2], 1, lambda i, j: (i ^ r) < i))
    kv_pieces = [v for pq in zip(kv_even, kv_odd) for v in pq]
    out_m, out_o = gather_core(out_near)

    def widen(x, part):
        moved = x if part == 0 else pltpu.roll(x, hw, 1)
        return jnp.where(lanes(x.shape) < hw, moved, 0.0)

    def widen_high(x, part):
        moved = x if part == 1 else pltpu.roll(x, hw, 1)
        return jnp.where(lanes(x.shape) >= hw, moved, 0.0)

    def causal(zz):
        key = rows_of((B, B)) ^ zz
        qry = lanes((B, B)) ^ zz
        return key <= qry

    def fwd_body(s_ref, q_ref, *refs):
        kv_in, slot_refs = refs[:NC], refs[NC : NC + NT]
        att_ref, lse_ref, qz, acc, tot, kv_ref = refs[NC + NT :]
        r, h = pl.program_id(0), pl.program_id(1)
        here = s_ref[1]

        @pl.when((r == 0) & (h == 0))
        def _():
            for hd in range(QH):
                x = q_ref[:, (hd // 2) * pw : (hd // 2 + 1) * pw].astype(f32)
                qz[hd] = widen(x, hd % 2).astype(bf16)
            for k in range(NC):
                kv_ref[k] = kv_in[k][...]

        def step(masked):
            kv = kv_ref[r, :, pl.ds(pl.multiple_of(h * pw, pw), pw)]
            kvt = kv.astype(f32).T.astype(bf16)
            for g in range(2):
                hd = 2 * h + g
                e = jnp.exp2(mm_nt(kv, qz[hd]) * c2)
                if masked:
                    e = jnp.where(causal(s_ref[2] * R), e, 0.0)
                part = jnp.sum(e, axis=0, keepdims=True)
                o = mm(kvt, e.astype(bf16))
                if masked:
                    tot[hd] = jnp.broadcast_to(part, (8, B))
                    acc[hd] = o
                else:
                    tot[hd] += jnp.broadcast_to(part, (8, B))
                    acc[hd] += o

        @pl.when(r == 0)
        def _():
            step(True)

        @pl.when((here ^ r) < here)
        def _():
            step(False)

        @pl.when((r == NC - 1) & (h == KH - 1))
        def _():
            outs = [acc[hd][hw:] / tot[hd][0:1] for hd in range(QH)]
            att = jnp.concatenate(outs, axis=0).T.astype(bf16)
            att_ref[...] = att
            put_slots(slot_refs, att)
            for hd in range(QH):
                lse_ref[hd] = jnp.log(tot[hd][0:1])

    fixed = lambda shape: pl.BlockSpec(shape, lambda r, h: (0,) * len(shape))
    *att_slots, attended, lse = pl.pallas_call(
        fwd_body,
        grid=(NC, KH),
        out_shape=[sds((R, C), bf16)] * NT + [sds((B, C), bf16), sds((QH, 1, B), f32)],
        in_specs=[SM] + [fixed((B, C))] * (1 + NC),
        out_specs=[fixed((R, C))] * NT + [fixed((B, C)), fixed((QH, 1, B))],
        scratch_shapes=[
            pltpu.VMEM((QH, B, pw), bf16),
            pltpu.VMEM((QH, pw, B), f32),
            pltpu.VMEM((QH, 8, B), f32),
            pltpu.VMEM((NC, B, C), bf16),
        ],
        cost_estimate=pl.CostEstimate(
            flops=16 * QH * B * B * pw, bytes_accessed=4 * B * C * 2, transcendentals=4 * QH * B * B
        ),
        name="attention_forward",
    )(where, rot_q, *kv_pieces)

    att_pieces = spread_column(att_slots)
    ffn_m, ffn_o = gather_core(ffn_near)

    def out_body(*refs):
        pieces, (om, oo, t_ref, g_ref, res, nrm) = refs[:NT], refs[NT:]
        a = jnp.concatenate([p[...] for p in pieces], axis=1)
        x = t_ref[...].astype(f32) + jnp.concatenate([mm_nt(a, om[0]), mm_nt(a, oo[0])], axis=1)
        res[...] = x
        inv = lax.rsqrt(jnp.mean(x * x, axis=-1, keepdims=True) + epsilon)
        nrm[...] = (x * inv * g_ref[1:2, :]).astype(bf16)

    resid, normed_f = whole_call(
        out_body,
        [sds((R, W), f32), sds((R, W), bf16)],
        (*att_pieces, out_m, out_o, tok, gain2),
        2 * R * W * W,
        scalars=False,
    )
    second_pieces = gather_column(normed_f)

    chunks = [slice(i, min(i + 256, F)) for i in range(0, F, 256)]

    def hidden_body(*refs):
        wm, wo, out = refs[NT:]
        c = join_slots(refs[:NT])
        for cols in chunks:
            out[:, cols] = mm(c[:, :H], wm[2, :, cols]) + mm(c[:, H:], wo[2, :, cols])

    (grad_mid,) = whole_call(
        hidden_body, [sds((B, F), f32)], (*cot_pieces, ffn_m, ffn_o), 2 * B * W * F, scalars=False
    )

    def ffn_body(*refs):
        wm, wo, gmid_r, mid_r, dg_r, du_r = refs[NT : NT + 6]
        gnfs = refs[NT + 6 :]
        r = join_slots(refs[:NT])
        rl, rr = r[:, :H], r[:, H:]
        for cols in chunks:
            gate = mm(rl, wm[0, :, cols]) + mm(rr, wo[0, :, cols])
            up = mm(rl, wm[1, :, cols]) + mm(rr, wo[1, :, cols])
            gmid = gmid_r[:, cols]
            sig = jax.nn.sigmoid(gate)
            act = gate * sig
            mid_r[:, cols] = (act * up).astype(bf16)
            dg_r[:, cols] = (gmid * up * sig * (1.0 + gate * (1.0 - sig))).astype(bf16)
            du_r[:, cols] = (gmid * act).astype(bf16)
        for w, cols in ((wm, slice(0, H)), (wo, slice(H, W))):
            g = mm_nt(dg_r[...], w[0]) + mm_nt(du_r[...], w[1])
            for k, ref in enumerate(gnfs):
                ref[:, cols] = g[k * R : (k + 1) * R].astype(bf16)

    mid, dgate, dup, *gnf_slots = whole_call(
        ffn_body,
        [sds((B, F), bf16)] * 3 + [sds((R, W), bf16)] * NT,
        (*second_pieces, ffn_m, ffn_o, grad_mid),
        8 * B * W * F,
        scalars=False,
    )
    gnf_pieces = spread_column(gnf_slots)

    def dw_body(cols, *refs):
        c_in, (mid_r, dg_r, du_r, out) = refs[NT : 2 * NT], refs[2 * NT :]
        rt = jnp.concatenate([ref[:, cols] for ref in refs[:NT]], axis=0).T
        ct = jnp.concatenate([ref[:, cols] for ref in c_in], axis=0).T
        for k, (lhs, rhs) in enumerate(((rt, dg_r), (rt, du_r), (ct, mid_r))):
            out[k] = mm(lhs, rhs[...]).astype(bf16)

    def half_weights(cols, dg):
        return whole_call(
            functools.partial(dw_body, cols),
            [sds((3, H, F), bf16)],
            (*second_pieces, *cot_pieces, mid, dg, dup),
            3 * B * W * F,
            scalars=False,
        )[0]

    dwf_o = half_weights(slice(H, W), dgate)
    dwf_m = half_weights(slice(0, H), after(dgate, dwf_o))

    def out_part_body(m_ref, wm, wo, *outs):
        for w, cols in ((wm, slice(0, H)), (wo, slice(H, W))):
            o = mm_nt(m_ref[...], w[2])
            for k, ref in enumerate(outs):
                ref[:, cols] = o[k * R : (k + 1) * R].astype(bf16)

    ffn_slots = whole_call(
        out_part_body,
        [sds((R, W), bf16)] * NT,
        (after(mid, dwf_m), ffn_m, ffn_o),
        2 * B * W * F,
        scalars=False,
    )
    ffn_own, ffn_sends = merge_core(dwf_m, plane(dwf_o, 1))
    gnf_pieces, ffn_own, ffn_sends = lax.optimization_barrier((gnf_pieces, ffn_own, ffn_sends))
    ffn_got = [plane(v, 2 * (i + 1)) for i, v in enumerate(ffn_sends)]

    def back_body(*refs):
        pieces, outs_in = refs[:NT], refs[NT : 2 * NT]
        res, c_ref, g_ref, om, oo, gres, gg, *more = refs[2 * NT :]
        gas, both = more[:NT], more[NT:]
        grad = sum(p[...].astype(f32) for p in pieces)
        x = res[...]
        inv = lax.rsqrt(jnp.mean(x * x, axis=-1, keepdims=True) + epsilon)
        hat = x * inv
        gg[...] = jnp.sum(grad * hat, axis=0, keepdims=True)
        scaled = grad * g_ref[1:2, :]
        through = inv * (scaled - hat * jnp.mean(scaled * hat, axis=-1, keepdims=True))
        total = c_ref[...].astype(f32) + through
        gres[...] = total
        half = total.astype(bf16)
        for k, ref in enumerate(both):
            ref[:R] = half
            ref[R:] = outs_in[k][...]
        ga = (mm(half[:, :H], om[0]) + mm(half[:, H:], oo[0])).astype(bf16)
        for k, ref in enumerate(gas):
            ref[...] = ga[:, k * C : (k + 1) * C]

    grad_resid, ffn_gain_part, *ga_slots = whole_call(
        back_body,
        [sds((R, W), f32), sds((1, W), f32)]
        + [sds((R, C), bf16)] * NT
        + [sds((2 * R, W), bf16)] * NT,
        (*gnf_pieces, *ffn_slots[:NT], resid, cot, gain2, out_m, out_o),
        2 * R * W * W,
        scalars=False,
    )
    ga_slots, both_slots = ga_slots[:NT], ga_slots[NT:]
    ga_pieces = spread_column(ga_slots)
    both_pieces = spread_column(both_slots)

    def bwd_body(s_ref, q_ref, a_ref, l_ref, *refs):
        d_in, kv_in = refs[:NT], refs[NT : NT + NC]
        dq_ref, even, odd, qz, dz, acc, dl, kv_ref = refs[NT + NC :]
        r, h = pl.program_id(0), pl.program_id(1)
        here = s_ref[1]

        @pl.when((r == 0) & (h == 0))
        def _():
            d_all = join_slots(d_in).astype(f32)
            for hd in range(QH):
                cols = slice((hd // 2) * pw, (hd // 2 + 1) * pw)
                qz[hd] = widen(q_ref[:, cols].astype(f32), hd % 2).astype(bf16)
                dz[hd] = widen_high(d_all[:, cols], hd % 2).astype(bf16)
            for k in range(NC):
                kv_ref[k] = kv_in[k][...]
            prod = d_all * a_ref[...].astype(f32)
            pick = jnp.where(lanes((8, C)) // hw == rows_of((8, C)), 1.0, 0.0).astype(bf16)
            sums = sum(mm_nt(pick, term) for term in three_terms(prod))
            for hd in range(QH):
                dl[hd] = jnp.broadcast_to(sums[hd : hd + 1], (8, B))

        here_cols = pl.ds(pl.multiple_of(h * pw, pw), pw)

        def put(value):
            @pl.when(r % 2 == 0)
            def _():
                even[r // 2, :, here_cols] = value

            @pl.when(r % 2 == 1)
            def _():
                odd[r // 2, :, here_cols] = value

        def step(masked):
            kv = kv_ref[r, :, here_cols]
            kvt = kv.astype(f32).T.astype(bf16)
            total = None
            for g in range(2):
                hd = 2 * h + g
                q, d = qz[hd], dz[hd]
                shift = l_ref[hd] * log2e
                p = jnp.exp2(mm_nt(kv, q) * c2 - shift)
                if masked:
                    p = jnp.where(causal(s_ref[2] * R), p, 0.0)
                ds = (p * (mm_nt(kv, d) - dl[hd][0:1])).astype(bf16)
                t = jnp.where(lanes((B, pw)) < hw, mm(ds, q) * scale, mm(p.astype(bf16), d))
                total = t if total is None else total + t
                o = mm(kvt, ds)
                if masked:
                    acc[hd] = o
                else:
                    acc[hd] += o
            put(total.astype(bf16))

        @pl.when(r == 0)
        def _():
            step(True)

        @pl.when((here ^ r) < here)
        def _():
            step(False)

        @pl.when((here ^ r) > here)
        def _():
            put(jnp.zeros((B, pw), bf16))

        @pl.when((r == NC - 1) & (h == KH - 1))
        def _():
            outs = [acc[hd][:hw] for hd in range(QH)]
            dq_ref[...] = jnp.concatenate(outs, axis=0).T * scale

    grad_rot_q, dkv_even, dkv_odd = pl.pallas_call(
        bwd_body,
        grid=(NC, KH),
        out_shape=[sds((B, C), f32)] + [sds((NC // 2, B, C), bf16)] * 2,
        in_specs=[SM, fixed((B, C)), fixed((B, C)), fixed((QH, 1, B))]
        + [fixed((R, C))] * NT
        + [fixed((B, C))] * NC,
        out_specs=[fixed((B, C))] + [fixed((NC // 2, B, C))] * 2,
        scratch_shapes=[
            pltpu.VMEM((QH, B, pw), bf16),
            pltpu.VMEM((QH, B, pw), bf16),
            pltpu.VMEM((QH, pw, B), f32),
            pltpu.VMEM((QH, 8, B), f32),
            pltpu.VMEM((NC, B, C), bf16),
        ],
        cost_estimate=pl.CostEstimate(
            flops=40 * QH * B * B * pw, bytes_accessed=8 * B * C * 2, transcendentals=4 * QH * B * B
        ),
        name="attention_backward",
    )(where, rot_q, attended, lse, *ga_pieces, *kv_pieces)

    odd = lax.ppermute(dkv_odd, "ctx", [(i, i ^ 1) for i in range(NC)])
    pair_parts = []
    for k in range(1, NC // 2):
        part = (dkv_even[k].astype(f32) + odd[k].astype(f32)).astype(bf16)
        pair_parts.append(along(part, 2 * k, lambda i, j: i // 2 > j // 2))

    def qk_body(s_ref, dq, even, odd_ref, q_raw_r, p_raw_r, cs, sn, qg_ref, kg_ref, wm, wo, g_ref, fg_ref, *refs):
        index = s_ref[0]
        n_parts = len(pair_parts)
        parts, r_in, gnas = refs[:n_parts], refs[n_parts : n_parts + NT], refs[n_parts + NT : n_parts + 2 * NT]
        both_ref, pack = refs[n_parts + 2 * NT :]
        r_all = join_slots(r_in)

        def back(grad, raw, gain, live):
            turned = grad * cs[...] - swap_halves(grad) * sn[...]
            inv = lax.rsqrt(head_mean(raw * raw) + epsilon)
            hat = raw * inv
            scaled = turned * gain
            out = inv * (scaled - hat * head_mean(scaled * hat))
            gg = jnp.sum(turned * hat, axis=0, keepdims=True)
            if live is not None:
                out = jnp.where(live, out, grad)
            return out.astype(bf16), gg

        dp = even[0].astype(f32) + odd_ref[0].astype(f32)
        for p in parts:
            dp = dp + p[...].astype(f32)
        gq, qsum = back(dq[...], q_raw_r[...], qg_ref[...], None)
        live = lanes((B, C)) % pw < hw
        gp, ksum = back(dp, p_raw_r[...], kg_ref[...], live)
        both_ref[...] = jnp.concatenate([gq, gp], axis=1)
        pack[...] = jnp.zeros_like(pack)
        for w, cols, first in ((wm, slice(0, H), 0), (wo, slice(H, W), N // 2)):
            part = mm_nt(gq, w[0]) + mm_nt(gp, w[1])
            for k, ref in enumerate(gnas):
                ref[:, cols] = part[k * R : (k + 1) * R].astype(bf16)
            agg = jnp.sum(part * r_all[:, cols].astype(f32), axis=0, keepdims=True) / g_ref[0:1, cols]
            for i in range(N // 2):
                to = index ^ masks[first + i]
                pack[pl.ds(to, 1), :] = agg[:, i * blk : (i + 1) * blk]
                pack[pl.ds(N + to, 1), :] = fg_ref[:, (first + i) * blk : (first + i + 1) * blk]
        heads_q = sum(qsum[:, i * pw : (i + 1) * pw] for i in range(KH))
        heads_q = heads_q + pltpu.roll(heads_q, hw, 1)
        heads_k = sum(ksum[:, i * pw : (i + 1) * pw] for i in range(KH))
        pack[2 * N : 2 * N + 1, :hw] = heads_q[:, :hw]
        pack[2 * N + 1 : 2 * N + 2, :hw] = heads_k[:, :hw]

    *gna_slots, both16, packed = whole_call(
        qk_body,
        [sds((R, W), bf16)] * NT + [sds((B, 2 * C), bf16), sds((2 * N + 8, blk), f32)],
        (
            where, grad_rot_q, dkv_even, odd, q_raw, p_raw, cosine, sine, qg, kg,
            qkv_m, qkv_o, gain2, ffn_gain_part, *pair_parts, *first_pieces,
        ),
        4 * B * W * C,
    )
    gna_pieces = spread_column(gna_slots)

    def proj_body(*refs):
        b_ref, gm, go = refs[NT:]
        rt = join_slots(refs[:NT]).T
        for ref, rows in ((gm, slice(0, H)), (go, slice(H, W))):
            full = mm(rt[rows], b_ref[...]).astype(bf16)
            ref[0] = full[:, :C]
            ref[1] = full[:, C:]

    proj_m, proj_o = whole_call(
        proj_body, [sds((2, H, C), bf16)] * 2, (*first_pieces, both16), 4 * B * W * C, scalars=False
    )

    def last_body(*refs):
        g_in, (a_ref, pm, po, gm, go) = refs[:NT], refs[NT:]
        gt = jnp.concatenate([ref[:R] for ref in g_in], axis=0).T
        for ref, part, rows in ((gm, pm, slice(0, H)), (go, po, slice(H, W))):
            ref[:2] = part[...]
            ref[2] = mm(gt[rows], a_ref[...]).astype(bf16)

    last_m, last_o = whole_call(
        last_body,
        [sds((3, H, C), bf16)] * 2,
        (*both_pieces, attended, proj_m, proj_o),
        2 * B * W * C,
        scalars=False,
    )
    att_own, att_sends = merge_core(last_m, plane(last_o, 1))
    att_got = [plane(v, 2 * (i + 1)) for i, v in enumerate(att_sends)]

    def block_body(*refs):
        index = refs[0][0]
        fp, (res, bo) = refs[1 : NT + 1], refs[NT + 1 :]
        block = (res[...] + sum(p[R:].astype(f32) for p in fp)).astype(bf16)
        for s, mask in enumerate(masks):
            src = slice(s * blk, (s + 1) * blk)
            if aligned:
                dst = pl.ds(pl.multiple_of((index ^ mask) * blk, blk), blk)
            else:
                dst = src
            bo[:, dst] = block[:, src]

    (block_out,) = whole_call(
        block_body, [sds((R, W), bf16)], (where, *both_pieces, resid), R * W * 8
    )

    bit = 1
    while bit < N:
        packed = packed + plane(packed, bit)
        bit *= 2
    packed = sum(gather_column(packed))

    grad_gate, grad_up, grad_down = close_sum(ffn_own, ffn_got)
    grad_query, grad_pairs, grad_output = close_sum(att_own, att_got)

    def end_body(*refs):
        s_ref, rest = refs[0], refs[1:]
        gp, (t_ref, gres, g_ref, gt) = rest[:NT], rest[NT:]
        index = s_ref[0]
        grad = sum(p[...].astype(f32) for p in gp)
        x = t_ref[...].astype(f32)
        inv = lax.rsqrt(jnp.mean(x * x, axis=-1, keepdims=True) + epsilon)
        hat = x * inv
        scaled = grad * g_ref[0:1, :]
        total = gres[...] + inv * (scaled - hat * jnp.mean(scaled * hat, axis=-1, keepdims=True))
        for s, mask in enumerate(masks):
            src = slice(s * blk, (s + 1) * blk)
            if aligned:
                dst = pl.ds(pl.multiple_of((index ^ mask) * blk, blk), blk)
            else:
                dst = src
            gt[:, dst] = total[:, src]

    gna_pieces, packed, grad_down, grad_output, block_out = lax.optimization_barrier(
        (gna_pieces, packed, grad_down, grad_output, block_out)
    )
    (grad_tokens,) = whole_call(
        end_body, [sds((R, W), f32)], (where, *gna_pieces, tok, grad_resid, gain2), R * W * 16
    )
    if not aligned:
        inverse = [masks.index(m) for m in range(N)]
        slot_of = jnp.take(jnp.array(inverse), me ^ jnp.arange(N, dtype=jnp.int32))
        back_cols = lambda v: jnp.take(
            v.reshape(R, N, blk), slot_of, axis=1
        ).reshape(R, W)
        grad_tokens, block_out = back_cols(grad_tokens), back_cols(block_out)

    lse_out = jnp.take(
        lse.reshape(QH, NT, R), z ^ jnp.arange(NT, dtype=jnp.int32), axis=1
    ).reshape(1, QH, B)
    return (
        block_out[None],
        grad_tokens[None],
        lse_out,
        packed[:N].reshape(W),
        grad_query,
        grad_pairs,
        packed[2 * N, :hw],
        packed[2 * N + 1, :hw],
        grad_output,
        packed[N : 2 * N].reshape(W),
        grad_gate,
        grad_up,
        grad_down,
    )


def solution(mesh):
    in_specs = (
        P("dp", ("ctx", "tp"), None),
        P(),
        P(("dp", "ctx"), "tp"),
        P(("dp", "ctx"), "tp"),
        P(),
        P(),
        P("tp", ("dp", "ctx")),
        P(),
        P(("dp", "ctx"), "tp"),
        P(("dp", "ctx"), "tp"),
        P("tp", ("dp", "ctx")),
        P("dp", ("ctx", "tp"), None),
    )
    out_specs = (
        P("dp", ("ctx", "tp"), None),
        P("dp", ("ctx", "tp"), None),
        P("dp", "tp", "ctx"),
        P(),
        P(("dp", "ctx"), "tp"),
        P(("dp", "ctx"), "tp"),
        P(),
        P(),
        P("tp", ("dp", "ctx")),
        P(),
        P(("dp", "ctx"), "tp"),
        P(("dp", "ctx"), "tp"),
        P("tp", ("dp", "ctx")),
    )

    return jax.shard_map(
        on_device, mesh=mesh, in_specs=in_specs, out_specs=out_specs, check_vma=False
    )
```

```python
import functools
import math

import jax
import jax.numpy as jnp
from jax import lax
from jax.experimental import pallas as pl
from jax.experimental.pallas import tpu as pltpu
from jax.sharding import PartitionSpec as P


epsilon = 1e-05
rope_base = 1000000.0
f32 = jnp.float32
bf16 = jnp.bfloat16
log2e = math.log2(math.e)


def mm(a, b):
    return lax.dot_general(a, b, (((1,), (0,)), ((), ())), preferred_element_type=f32)


def mm_nt(a, b):
    return lax.dot_general(a, b, (((1,), (1,)), ((), ())), preferred_element_type=f32)


def lanes(shape):
    return lax.broadcasted_iota(jnp.int32, shape, len(shape) - 1)


def rows_of(shape):
    return lax.broadcasted_iota(jnp.int32, shape, 0)


def sds(shape, dtype):
    return jax.ShapeDtypeStruct(shape, dtype)


VM = pl.BlockSpec(memory_space=pltpu.VMEM)
SM = pl.BlockSpec(memory_space=pltpu.SMEM)


def whole_call(body, outs, args, flops, scratch=(), scalars=True):
    moved = sum(math.prod(a.shape) * a.dtype.itemsize for a in list(args) + list(outs))
    specs = [VM] * len(args)
    if scalars:
        specs[0] = SM
    return pl.pallas_call(
        body,
        out_shape=list(outs),
        in_specs=specs,
        out_specs=[VM] * len(outs),
        scratch_shapes=list(scratch),
        cost_estimate=pl.CostEstimate(flops=int(flops), bytes_accessed=int(moved), transcendentals=0),
    )(*args)


def on_device(
    tokens,
    attention_gain,
    query_weight,
    key_value_weight,
    query_gain,
    key_gain,
    output_weight,
    ffn_gain,
    gate_weight,
    up_weight,
    down_weight,
    cotangent,
):
    hw = query_gain.shape[0]
    pw = 2 * hw
    R = tokens.shape[1]
    W = tokens.shape[2]
    NT = lax.axis_size("tp")
    NC = lax.axis_size("ctx")
    N = lax.axis_size("dp") * NC
    B = R * NT
    C = query_weight.shape[1]
    F = gate_weight.shape[1]
    QH = C // hw
    KH = key_value_weight.shape[1] // pw
    assert QH == 2 * KH
    H = W // 2
    blk = W // N
    scale = 1.0 / math.sqrt(hw)
    c2 = scale * log2e
    masks = list(range(0, N, 2)) + list(range(1, N, 2))
    me = lax.axis_index("dp") * NC + lax.axis_index("ctx")
    ctx = lax.axis_index("ctx")
    z = lax.axis_index("tp")
    where = jnp.stack([me, ctx, z]).astype(jnp.int32)
    aligned = blk % 128 == 0

    def plane(v, mask):
        return lax.ppermute(v, ("dp", "ctx"), [(i, i ^ mask) for i in range(N)])

    def column(v, mask):
        return lax.ppermute(v, "tp", [(i, i ^ mask) for i in range(NT)])

    def along(v, mask, keep):
        pairs = [(i, i ^ mask) for i in range(NC) if keep(i, i ^ mask)]
        return lax.ppermute(v, "ctx", pairs)

    def after(v, *deps):
        return lax.optimization_barrier((v,) + deps)[0]

    def gather_near(own):
        return [own] + [plane(own, r) for r in range(2, N, 2)]

    def gather_core(near):
        mine = jnp.concatenate(near, axis=1)
        return mine, plane(mine, 1)

    def share_out(refs, total, k):
        m = total.shape[0] * 2 // N
        for i, ref in enumerate(refs):
            ref[k] = total[i * m : (i + 1) * m].astype(ref.dtype)

    def share_shapes(kinds, cols):
        shape = (kinds, H * 2 // N, cols)
        return [sds(shape, f32)] + [sds(shape, bf16)] * (N // 2 - 1)

    def close_sum(own, parts, turned):
        kinds, m, cols = own.shape

        def body(first, *refs):
            parts, outs = refs[: len(parts_in)], refs[len(parts_in) :]
            for k in range(kinds):
                total = first[k]
                for p in parts:
                    total = total + p[k].astype(f32)
                outs[k][...] = total if k < kinds - turned else total.T

        parts_in = parts
        return whole_call(
            body,
            [sds((m, cols), f32)] * (kinds - turned) + [sds((cols, m), f32)] * turned,
            (own, *parts),
            own.size * N,
            scalars=False,
        )

    def gather_column(own):
        return [own] + [column(own, k) for k in range(1, NT)]

    def spread_column(pieces):
        return [pieces[0]] + [column(pieces[k], k) for k in range(1, NT)]

    def put_slots(refs, value):
        for k, ref in enumerate(refs):
            ref[...] = value[k * R : (k + 1) * R].astype(ref.dtype)

    def join_slots(refs):
        return jnp.concatenate([ref[...] for ref in refs], axis=0)

    def take_cols(v, index, size, order):
        picks = index ^ jnp.array(order, jnp.int32)
        return jnp.take(v.reshape(v.shape[0], -1, size), picks, axis=1).reshape(v.shape)

    own_qkv = jnp.stack([query_weight, key_value_weight])

    def pre_body(s_ref, t_ref, c_ref, g_ref, o_ref, n_ref, t_out, c_out, g_out, ot_out):
        index = s_ref[0]
        for s, mask in enumerate(masks):
            if aligned:
                src = pl.ds(pl.multiple_of((index ^ mask) * blk, blk), blk)
            else:
                src = slice(s * blk, (s + 1) * blk)
            dst = slice(s * blk, (s + 1) * blk)
            t_out[:, dst] = t_ref[:, src]
            c_out[:, dst] = c_ref[:, src]
            g_out[:, dst] = g_ref[:, src]
        x = t_out[...].astype(f32)
        inv = lax.rsqrt(jnp.mean(x * x, axis=-1, keepdims=True) + epsilon)
        n_ref[...] = (x * inv * g_out[0:1, :]).astype(bf16)
        ot_out[...] = o_ref[...].T

    gains = jnp.stack([attention_gain, ffn_gain])
    t_in, c_in, g_in = tokens[0], cotangent[0], gains
    if not aligned:
        t_in, c_in, g_in = (take_cols(v, me, blk, masks) for v in (t_in, c_in, g_in))
    normed, tok, cot, gain2, own_out = whole_call(
        pre_body,
        [sds((R, W), bf16)] * 3 + [sds((2, W), f32), sds((blk, C), bf16)],
        (where, t_in, c_in, g_in, output_weight),
        R * W * 8,
    )
    first_pieces = gather_column(normed)
    qkv_near = gather_near(after(own_qkv, normed))
    qkv_m, qkv_o = gather_core(qkv_near)
    own_ffn = jnp.stack([gate_weight, up_weight, down_weight.T])
    ffn_near = gather_near(after(own_ffn, normed))
    out_cols = jnp.concatenate(gather_column(own_out), axis=1)[None]
    out_near = gather_near(out_cols)
    cot_pieces = gather_column(cot)

    half_width = hw // 2
    freq = jnp.exp(jnp.arange(half_width, dtype=f32) * (-2.0 * math.log(rope_base) / hw))
    positions = ctx * B + (jnp.arange(B, dtype=jnp.int32) ^ (z * R))
    angle = positions.astype(f32)[:, None] * freq[None, :]
    cos_h, sin_h = jnp.cos(angle), jnp.sin(angle)
    cosine = jnp.tile(cos_h, (1, 2 * QH))
    sine = jnp.tile(jnp.concatenate([-sin_h, sin_h], -1), (1, QH))
    qg = jnp.tile(query_gain, QH)[None]
    kg = jnp.tile(jnp.concatenate([key_gain, jnp.ones_like(key_gain)]), KH)[None]

    def three_terms(x):
        high = x.astype(bf16)
        rest = x - high.astype(f32)
        low = rest.astype(bf16)
        return high, low, (rest - low.astype(f32)).astype(bf16)

    def head_mean(x):
        n = x.shape[1]
        same = rows_of((n, n)) // hw == lanes((n, n)) // hw
        ones = jnp.where(same, 1.0 / hw, 0.0).astype(bf16)
        return sum(mm(term, ones) for term in three_terms(x))

    def swap_halves(x):
        first = lanes(x.shape) % hw < half_width
        return jnp.where(
            first, pltpu.roll(x, x.shape[1] - half_width, 1), pltpu.roll(x, half_width, 1)
        )

    def qkv_body(*refs):
        wm, wo, cs, sn, qg_ref, kg_ref, rq, pr, q_raw, p_raw = refs[NT:]
        rows = join_slots(refs[:NT])
        left, right = rows[:, :H], rows[:, H:]
        q = mm(left, wm[0]) + mm(right, wo[0])
        p = mm(left, wm[1]) + mm(right, wo[1])
        q_raw[...] = q
        p_raw[...] = p
        qn = q * lax.rsqrt(head_mean(q * q) + epsilon) * qg_ref[...]
        rq[...] = (qn * cs[...] + swap_halves(qn) * sn[...]).astype(bf16)
        kn = p * lax.rsqrt(head_mean(p * p) + epsilon) * kg_ref[...]
        kr = kn * cs[...] + swap_halves(kn) * sn[...]
        pr[...] = jnp.where(lanes(p.shape) % pw < hw, kr, p).astype(bf16)

    rot_q, pair, q_raw, p_raw = whole_call(
        qkv_body,
        [sds((B, C), bf16), sds((B, C), bf16), sds((B, C), f32), sds((B, C), f32)],
        (*first_pieces, qkv_m, qkv_o, cosine, sine, qg, kg),
        4 * B * W * C,
        scalars=False,
    )

    earlier = lambda i, j: i < j
    kv_even = [pair] + [along(pair, r, earlier) for r in range(2, NC, 2)]
    kv_odd = [along(pair, 1, earlier)]
    for r in range(2, NC, 2):
        kv_odd.append(along(kv_even[r // 2], 1, lambda i, j: (i ^ r) < i))
    kv_pieces = [v for pq in zip(kv_even, kv_odd) for v in pq]
    out_m, out_o = gather_core(out_near)

    def widen(x, part):
        moved = x if part == 0 else pltpu.roll(x, hw, 1)
        return jnp.where(lanes(x.shape) < hw, moved, 0.0)

    def widen_high(x, part):
        moved = x if part == 1 else pltpu.roll(x, hw, 1)
        return jnp.where(lanes(x.shape) >= hw, moved, 0.0)

    def causal(zz):
        key = rows_of((B, B)) ^ zz
        qry = lanes((B, B)) ^ zz
        return key <= qry

    def fwd_body(s_ref, q_ref, *refs):
        kv_in, slot_refs = refs[:NC], refs[NC : NC + NT]
        att_ref, lse_ref, qz, acc, tot, kv_ref = refs[NC + NT :]
        r, h = pl.program_id(0), pl.program_id(1)
        here = s_ref[1]

        @pl.when((r == 0) & (h == 0))
        def _():
            for hd in range(QH):
                x = q_ref[:, (hd // 2) * pw : (hd // 2 + 1) * pw].astype(f32)
                qz[hd] = widen(x, hd % 2).astype(bf16)
            for k in range(NC):
                kv_ref[k] = kv_in[k][...]

        def step(masked):
            kv = kv_ref[r, :, pl.ds(pl.multiple_of(h * pw, pw), pw)]
            kvt = kv.astype(f32).T.astype(bf16)
            for g in range(2):
                hd = 2 * h + g
                e = jnp.exp2(mm_nt(kv, qz[hd]) * c2)
                if masked:
                    e = jnp.where(causal(s_ref[2] * R), e, 0.0)
                part = jnp.sum(e, axis=0, keepdims=True)
                o = mm(kvt, e.astype(bf16))
                if masked:
                    tot[hd] = jnp.broadcast_to(part, (8, B))
                    acc[hd] = o
                else:
                    tot[hd] += jnp.broadcast_to(part, (8, B))
                    acc[hd] += o

        @pl.when(r == 0)
        def _():
            step(True)

        @pl.when((here ^ r) < here)
        def _():
            step(False)

        @pl.when((r == NC - 1) & (h == KH - 1))
        def _():
            outs = [acc[hd][hw:] / tot[hd][0:1] for hd in range(QH)]
            att = jnp.concatenate(outs, axis=0).T.astype(bf16)
            att_ref[...] = att
            put_slots(slot_refs, att)
            for hd in range(QH):
                lse_ref[hd] = jnp.log(tot[hd][0:1])

    fixed = lambda shape: pl.BlockSpec(shape, lambda r, h: (0,) * len(shape))
    *att_slots, attended, lse = pl.pallas_call(
        fwd_body,
        grid=(NC, KH),
        out_shape=[sds((R, C), bf16)] * NT + [sds((B, C), bf16), sds((QH, 1, B), f32)],
        in_specs=[SM] + [fixed((B, C))] * (1 + NC),
        out_specs=[fixed((R, C))] * NT + [fixed((B, C)), fixed((QH, 1, B))],
        scratch_shapes=[
            pltpu.VMEM((QH, B, pw), bf16),
            pltpu.VMEM((QH, pw, B), f32),
            pltpu.VMEM((QH, 8, B), f32),
            pltpu.VMEM((NC, B, C), bf16),
        ],
        cost_estimate=pl.CostEstimate(
            flops=16 * QH * B * B * pw, bytes_accessed=4 * B * C * 2, transcendentals=4 * QH * B * B
        ),
        name="attention_forward",
    )(where, rot_q, *kv_pieces)

    att_pieces = spread_column(att_slots)
    ffn_m, ffn_o = gather_core(ffn_near)

    def out_body(*refs):
        pieces, (om, oo, t_ref, g_ref, res, nrm) = refs[:NT], refs[NT:]
        a = jnp.concatenate([p[...] for p in pieces], axis=1)
        x = t_ref[...].astype(f32) + jnp.concatenate([mm_nt(a, om[0]), mm_nt(a, oo[0])], axis=1)
        res[...] = x
        inv = lax.rsqrt(jnp.mean(x * x, axis=-1, keepdims=True) + epsilon)
        nrm[...] = (x * inv * g_ref[1:2, :]).astype(bf16)

    resid, normed_f = whole_call(
        out_body,
        [sds((R, W), f32), sds((R, W), bf16)],
        (*att_pieces, out_m, out_o, tok, gain2),
        2 * R * W * W,
        scalars=False,
    )
    second_pieces = gather_column(normed_f)

    chunks = [slice(i, min(i + 256, F)) for i in range(0, F, 256)]

    def hidden_body(*refs):
        wm, wo, out = refs[NT:]
        c = join_slots(refs[:NT])
        for cols in chunks:
            out[:, cols] = mm(c[:, :H], wm[0, :, cols]) + mm(c[:, H:], wo[0, :, cols])

    down_spec = pl.BlockSpec((1, H, F), lambda k: (2, 0, 0))
    grad_mid = pl.pallas_call(
        hidden_body,
        grid=(1,),
        out_shape=sds((B, F), f32),
        in_specs=[pl.BlockSpec((R, W), lambda k: (0, 0))] * NT + [down_spec] * 2,
        out_specs=pl.BlockSpec((B, F), lambda k: (0, 0)),
        cost_estimate=pl.CostEstimate(
            flops=2 * B * W * F, bytes_accessed=2 * W * F + 6 * B * F, transcendentals=0
        ),
        name="hidden_back",
    )(*cot_pieces, ffn_m, ffn_o)

    def ffn_body(*refs):
        wm, wo, gmid_r, hid = refs[NT : NT + 4]
        gnfs = refs[NT + 4 :]
        r = join_slots(refs[:NT])
        rl, rr = r[:, :H], r[:, H:]
        for cols in chunks:
            gate = mm(rl, wm[0, :, cols]) + mm(rr, wo[0, :, cols])
            up = mm(rl, wm[1, :, cols]) + mm(rr, wo[1, :, cols])
            gmid = gmid_r[:, cols]
            sig = jax.nn.sigmoid(gate)
            act = gate * sig
            hid[0, :, cols] = (gmid * up * sig * (1.0 + gate * (1.0 - sig))).astype(bf16)
            hid[1, :, cols] = (gmid * act).astype(bf16)
            hid[2, :, cols] = (act * up).astype(bf16)
        for w, cols in ((wm, slice(0, H)), (wo, slice(H, W))):
            g = mm_nt(hid[0], w[0]) + mm_nt(hid[1], w[1])
            for k, ref in enumerate(gnfs):
                ref[:, cols] = g[k * R : (k + 1) * R].astype(bf16)

    hidden, *gnf_slots = whole_call(
        ffn_body,
        [sds((3, B, F), bf16)] + [sds((R, W), bf16)] * NT,
        (*second_pieces, ffn_m, ffn_o, grad_mid),
        8 * B * W * F,
        scalars=False,
    )
    gnf_pieces = spread_column(gnf_slots)

    one = lambda shape: pl.BlockSpec(shape, lambda k: (0,) * len(shape))
    kind = lambda rows: pl.BlockSpec((1, rows, F), lambda k: (k, 0, 0))

    def dw_body(cols, *refs):
        r_in, c_in, (h_ref, *rest) = refs[:NT], refs[NT : 2 * NT], refs[2 * NT :]
        lt = rest[-1]
        k = pl.program_id(0)

        @pl.when(k == 0)
        def _():
            lt[0] = jnp.concatenate([ref[:, cols] for ref in r_in], axis=0).T
            lt[1] = jnp.concatenate([ref[:, cols] for ref in c_in], axis=0).T

        total = mm(lt[k // 2], h_ref[0])
        if len(rest) == 2:
            rest[0][0] = total.astype(bf16)
        else:
            share_out(rest[1:-1], total + rest[0][0].astype(f32), 0)

    def half_weights(cols, hid, got):
        outs = share_shapes(3, F) if got else [sds((3, H, F), bf16)]
        return pl.pallas_call(
            functools.partial(dw_body, cols),
            grid=(3,),
            out_shape=outs,
            in_specs=[one((R, W))] * (2 * NT) + [kind(B)] + [kind(H)] * len(got),
            out_specs=[kind(o.shape[1]) for o in outs],
            scratch_shapes=[pltpu.VMEM((2, H, B), bf16)],
            cost_estimate=pl.CostEstimate(
                flops=3 * B * W * F, bytes_accessed=3 * W * F + 6 * B * F, transcendentals=0
            ),
        )(*second_pieces, *cot_pieces, hid, *got)

    (dwf_o,) = half_weights(slice(H, W), hidden, [])
    dwf_got = plane(dwf_o, 1)

    def out_part_body(h_ref, wm, wo, *outs):
        for w, cols in ((wm, slice(0, H)), (wo, slice(H, W))):
            o = mm_nt(h_ref[0], w[0])
            for k, ref in enumerate(outs):
                ref[:, cols] = o[k * R : (k + 1) * R].astype(bf16)

    third = lambda rows: pl.BlockSpec((1, rows, F), lambda k: (2, 0, 0))
    ffn_slots = pl.pallas_call(
        out_part_body,
        grid=(1,),
        out_shape=[sds((R, W), bf16)] * NT,
        in_specs=[third(B), third(H), third(H)],
        out_specs=[one((R, W))] * NT,
        cost_estimate=pl.CostEstimate(
            flops=2 * B * W * F, bytes_accessed=2 * W * F + 2 * B * F, transcendentals=0
        ),
        name="ffn_out",
    )(after(hidden, dwf_o), ffn_m, ffn_o)
    ffn_own, *ffn_sends = half_weights(slice(0, H), hidden, [dwf_got])
    gnf_pieces, ffn_own, ffn_sends, ffn_slots = lax.optimization_barrier(
        (gnf_pieces, ffn_own, ffn_sends, ffn_slots)
    )
    ffn_got = [plane(v, 2 * (i + 1)) for i, v in enumerate(ffn_sends)]

    def back_body(*refs):
        pieces, (res, c_ref, g_ref, om, oo, gres, gg, rg, *gas) = refs[:NT], refs[NT:]
        grad = sum(p[...].astype(f32) for p in pieces)
        x = res[...]
        inv = lax.rsqrt(jnp.mean(x * x, axis=-1, keepdims=True) + epsilon)
        hat = x * inv
        gg[...] = jnp.sum(grad * hat, axis=0, keepdims=True)
        scaled = grad * g_ref[1:2, :]
        through = inv * (scaled - hat * jnp.mean(scaled * hat, axis=-1, keepdims=True))
        total = c_ref[...].astype(f32) + through
        gres[...] = total
        half = total.astype(bf16)
        rg[...] = half
        ga = (mm(half[:, :H], om[0]) + mm(half[:, H:], oo[0])).astype(bf16)
        for k, ref in enumerate(gas):
            ref[...] = ga[:, k * C : (k + 1) * C]

    grad_resid, ffn_gain_part, rg16, *ga_slots = whole_call(
        back_body,
        [sds((R, W), f32), sds((1, W), f32), sds((R, W), bf16)] + [sds((R, C), bf16)] * NT,
        (*gnf_pieces, resid, cot, gain2, out_m, out_o),
        2 * R * W * W,
        scalars=False,
    )
    ga_pieces = spread_column(ga_slots)
    ffn_pieces = spread_column(ffn_slots)

    def dwo_body(cols, g_ref, *refs):
        g = g_ref[:, cols].T
        a = jnp.concatenate([ref[...] for ref in refs[:NT]], axis=1)
        total = mm(g, a)
        rest = refs[NT:]
        if len(rest) == 1:
            rest[0][0] = total.astype(bf16)
        else:
            share_out(rest[1:], total + rest[0][0].astype(f32), 0)

    def half_out(cols, got):
        return whole_call(
            functools.partial(dwo_body, cols),
            share_shapes(1, NT * C) if got else [sds((1, H, NT * C), bf16)],
            (rg16, *att_pieces, *got),
            R * W * NT * C,
            scalars=False,
        )

    (dwo_o,) = half_out(slice(H, W), [])
    out_own, *out_sends = half_out(slice(0, H), [plane(dwo_o, 1)])
    out_got = [plane(v, 2 * (i + 1)) for i, v in enumerate(out_sends)]

    def bwd_body(s_ref, q_ref, a_ref, l_ref, *refs):
        d_in, kv_in = refs[:NT], refs[NT : NT + NC]
        dq_ref, even, odd, qz, dz, acc, dl, kv_ref = refs[NT + NC :]
        r, h = pl.program_id(0), pl.program_id(1)
        here = s_ref[1]

        @pl.when((r == 0) & (h == 0))
        def _():
            d_all = join_slots(d_in).astype(f32)
            for hd in range(QH):
                cols = slice((hd // 2) * pw, (hd // 2 + 1) * pw)
                qz[hd] = widen(q_ref[:, cols].astype(f32), hd % 2).astype(bf16)
                dz[hd] = widen_high(d_all[:, cols], hd % 2).astype(bf16)
            for k in range(NC):
                kv_ref[k] = kv_in[k][...]
            prod = d_all * a_ref[...].astype(f32)
            pick = jnp.where(lanes((8, C)) // hw == rows_of((8, C)), 1.0, 0.0).astype(bf16)
            sums = sum(mm_nt(pick, term) for term in three_terms(prod))
            for hd in range(QH):
                dl[hd] = jnp.broadcast_to(sums[hd : hd + 1], (8, B))

        here_cols = pl.ds(pl.multiple_of(h * pw, pw), pw)

        def put(value):
            @pl.when(r % 2 == 0)
            def _():
                even[r // 2, :, here_cols] = value

            @pl.when(r % 2 == 1)
            def _():
                odd[r // 2, :, here_cols] = value

        def step(masked):
            kv = kv_ref[r, :, here_cols]
            kvt = kv.astype(f32).T.astype(bf16)
            total = None
            for g in range(2):
                hd = 2 * h + g
                q, d = qz[hd], dz[hd]
                shift = l_ref[hd] * log2e
                p = jnp.exp2(mm_nt(kv, q) * c2 - shift)
                if masked:
                    p = jnp.where(causal(s_ref[2] * R), p, 0.0)
                ds = (p * (mm_nt(kv, d) - dl[hd][0:1])).astype(bf16)
                t = jnp.where(lanes((B, pw)) < hw, mm(ds, q) * scale, mm(p.astype(bf16), d))
                total = t if total is None else total + t
                o = mm(kvt, ds)
                if masked:
                    acc[hd] = o
                else:
                    acc[hd] += o
            put(total.astype(bf16))

        @pl.when(r == 0)
        def _():
            step(True)

        @pl.when((here ^ r) < here)
        def _():
            step(False)

        @pl.when((here ^ r) > here)
        def _():
            put(jnp.zeros((B, pw), bf16))

        @pl.when((r == NC - 1) & (h == KH - 1))
        def _():
            outs = [acc[hd][:hw] for hd in range(QH)]
            dq_ref[...] = jnp.concatenate(outs, axis=0).T * scale

    grad_rot_q, dkv_even, dkv_odd = pl.pallas_call(
        bwd_body,
        grid=(NC, KH),
        out_shape=[sds((B, C), f32)] + [sds((NC // 2, B, C), bf16)] * 2,
        in_specs=[SM, fixed((B, C)), fixed((B, C)), fixed((QH, 1, B))]
        + [fixed((R, C))] * NT
        + [fixed((B, C))] * NC,
        out_specs=[fixed((B, C))] + [fixed((NC // 2, B, C))] * 2,
        scratch_shapes=[
            pltpu.VMEM((QH, B, pw), bf16),
            pltpu.VMEM((QH, B, pw), bf16),
            pltpu.VMEM((QH, pw, B), f32),
            pltpu.VMEM((QH, 8, B), f32),
            pltpu.VMEM((NC, B, C), bf16),
        ],
        cost_estimate=pl.CostEstimate(
            flops=40 * QH * B * B * pw, bytes_accessed=8 * B * C * 2, transcendentals=4 * QH * B * B
        ),
        name="attention_backward",
    )(where, rot_q, attended, lse, *ga_pieces, *kv_pieces)

    odd = lax.ppermute(dkv_odd, "ctx", [(i, i ^ 1) for i in range(NC)])
    pair_parts = []
    for k in range(1, NC // 2):
        part = (dkv_even[k].astype(f32) + odd[k].astype(f32)).astype(bf16)
        pair_parts.append(along(part, 2 * k, lambda i, j: i // 2 > j // 2))

    def qk_body(s_ref, dq, even, odd_ref, q_raw_r, p_raw_r, cs, sn, qg_ref, kg_ref, wm, wo, g_ref, fg_ref, *refs):
        index = s_ref[0]
        n_parts = len(pair_parts)
        parts, r_in, gnas = refs[:n_parts], refs[n_parts : n_parts + NT], refs[n_parts + NT : n_parts + 2 * NT]
        both_ref, pack = refs[n_parts + 2 * NT :]
        r_all = join_slots(r_in)

        def back(grad, raw, gain, live):
            turned = grad * cs[...] - swap_halves(grad) * sn[...]
            inv = lax.rsqrt(head_mean(raw * raw) + epsilon)
            hat = raw * inv
            scaled = turned * gain
            out = inv * (scaled - hat * head_mean(scaled * hat))
            gg = jnp.sum(turned * hat, axis=0, keepdims=True)
            if live is not None:
                out = jnp.where(live, out, grad)
            return out.astype(bf16), gg

        dp = even[0].astype(f32) + odd_ref[0].astype(f32)
        for p in parts:
            dp = dp + p[...].astype(f32)
        gq, qsum = back(dq[...], q_raw_r[...], qg_ref[...], None)
        live = lanes((B, C)) % pw < hw
        gp, ksum = back(dp, p_raw_r[...], kg_ref[...], live)
        both_ref[...] = jnp.concatenate([gq, gp], axis=1)
        pack[...] = jnp.zeros_like(pack)
        for w, cols, first in ((wm, slice(0, H), 0), (wo, slice(H, W), N // 2)):
            part = mm_nt(gq, w[0]) + mm_nt(gp, w[1])
            for k, ref in enumerate(gnas):
                ref[:, cols] = part[k * R : (k + 1) * R].astype(bf16)
            agg = jnp.sum(part * r_all[:, cols].astype(f32), axis=0, keepdims=True) / g_ref[0:1, cols]
            for i in range(N // 2):
                to = index ^ masks[first + i]
                pack[pl.ds(to, 1), :] = agg[:, i * blk : (i + 1) * blk]
                pack[pl.ds(N + to, 1), :] = fg_ref[:, (first + i) * blk : (first + i + 1) * blk]
        heads_q = sum(qsum[:, i * pw : (i + 1) * pw] for i in range(KH))
        heads_q = heads_q + pltpu.roll(heads_q, hw, 1)
        heads_k = sum(ksum[:, i * pw : (i + 1) * pw] for i in range(KH))
        pack[2 * N : 2 * N + 1, :hw] = heads_q[:, :hw]
        pack[2 * N + 1 : 2 * N + 2, :hw] = heads_k[:, :hw]

    *gna_slots, both16, packed = whole_call(
        qk_body,
        [sds((R, W), bf16)] * NT + [sds((B, 2 * C), bf16), sds((2 * N + 8, blk), f32)],
        (
            where, grad_rot_q, dkv_even, odd, q_raw, p_raw, cosine, sine, qg, kg,
            qkv_m, qkv_o, gain2, ffn_gain_part, *pair_parts, *first_pieces,
        ),
        4 * B * W * C,
    )
    gna_pieces = spread_column(gna_slots)

    def proj_body(cols, *refs):
        b_ref, *rest = refs[NT:]
        rt = jnp.concatenate([ref[:, cols] for ref in refs[:NT]], axis=0).T
        full = mm(rt, b_ref[...])
        for k in range(2):
            part = full[:, k * C : (k + 1) * C]
            if len(rest) == 1:
                rest[0][k] = part.astype(bf16)
            else:
                share_out(rest[1:], part + rest[0][k].astype(f32), k)

    def half_proj(cols, got):
        return whole_call(
            functools.partial(proj_body, cols),
            share_shapes(2, C) if got else [sds((2, H, C), bf16)],
            (*first_pieces, both16, *got),
            2 * B * W * C,
            scalars=False,
        )

    (proj_o,) = half_proj(slice(H, W), [])
    att_own, *att_sends = half_proj(slice(0, H), [plane(proj_o, 1)])
    att_got = [plane(v, 2 * (i + 1)) for i, v in enumerate(att_sends)]

    def out_sum_body(first, *refs):
        parts, outs = refs[: len(out_got)], refs[len(out_got) :]
        total = first[0]
        for p in parts:
            total = total + p[0].astype(f32)
        for k, ref in enumerate(outs):
            ref[...] = total[:, k * C : (k + 1) * C].astype(bf16)

    out_slots = whole_call(
        out_sum_body,
        [sds((blk, C), bf16)] * NT,
        (out_own, *out_got),
        blk * NT * C * 4,
        scalars=False,
    )
    out_pieces = spread_column(out_slots)

    def out_close_body(*refs):
        total = refs[0][...].astype(f32)
        for ref in refs[1:NT]:
            total = total + ref[...].astype(f32)
        refs[NT][...] = total.T

    (grad_output,) = whole_call(
        out_close_body, [sds((C, blk), f32)], out_pieces, blk * C * 4, scalars=False
    )

    def block_body(*refs):
        index = refs[0][0]
        fp, (res, bo) = refs[1 : NT + 1], refs[NT + 1 :]
        block = (res[...] + sum(p[...].astype(f32) for p in fp)).astype(bf16)
        for s, mask in enumerate(masks):
            src = slice(s * blk, (s + 1) * blk)
            if aligned:
                dst = pl.ds(pl.multiple_of((index ^ mask) * blk, blk), blk)
            else:
                dst = src
            bo[:, dst] = block[:, src]

    (block_out,) = whole_call(
        block_body, [sds((R, W), bf16)], (where, *ffn_pieces, resid), R * W * 8
    )

    bit = 1
    while bit < N:
        packed = packed + plane(packed, bit)
        bit *= 2
    packed = sum(gather_column(packed))

    grad_gate, grad_up, grad_down = close_sum(ffn_own, ffn_got, 1)
    grad_query, grad_pairs = close_sum(att_own, att_got, 0)

    def end_body(*refs):
        s_ref, rest = refs[0], refs[1:]
        gp, (t_ref, gres, g_ref, gt) = rest[:NT], rest[NT:]
        index = s_ref[0]
        grad = sum(p[...].astype(f32) for p in gp)
        x = t_ref[...].astype(f32)
        inv = lax.rsqrt(jnp.mean(x * x, axis=-1, keepdims=True) + epsilon)
        hat = x * inv
        scaled = grad * g_ref[0:1, :]
        total = gres[...] + inv * (scaled - hat * jnp.mean(scaled * hat, axis=-1, keepdims=True))
        for s, mask in enumerate(masks):
            src = slice(s * blk, (s + 1) * blk)
            if aligned:
                dst = pl.ds(pl.multiple_of((index ^ mask) * blk, blk), blk)
            else:
                dst = src
            gt[:, dst] = total[:, src]

    gna_pieces, packed, grad_down, grad_output, grad_query, block_out = (
        lax.optimization_barrier(
            (gna_pieces, packed, grad_down, grad_output, grad_query, block_out)
        )
    )
    (grad_tokens,) = whole_call(
        end_body, [sds((R, W), f32)], (where, *gna_pieces, tok, grad_resid, gain2), R * W * 16
    )
    if not aligned:
        inverse = [masks.index(m) for m in range(N)]
        slot_of = jnp.take(jnp.array(inverse), me ^ jnp.arange(N, dtype=jnp.int32))
        back_cols = lambda v: jnp.take(
            v.reshape(R, N, blk), slot_of, axis=1
        ).reshape(R, W)
        grad_tokens, block_out = back_cols(grad_tokens), back_cols(block_out)

    lse_out = jnp.take(
        lse.reshape(QH, NT, R), z ^ jnp.arange(NT, dtype=jnp.int32), axis=1
    ).reshape(1, QH, B)
    return (
        block_out[None],
        grad_tokens[None],
        lse_out,
        packed[:N].reshape(W),
        grad_query,
        grad_pairs,
        packed[2 * N, :hw],
        packed[2 * N + 1, :hw],
        grad_output,
        packed[N : 2 * N].reshape(W),
        grad_gate,
        grad_up,
        grad_down,
    )


def solution(mesh):
    in_specs = (
        P("dp", ("ctx", "tp"), None),
        P(),
        P(("dp", "ctx"), "tp"),
        P(("dp", "ctx"), "tp"),
        P(),
        P(),
        P("tp", ("dp", "ctx")),
        P(),
        P(("dp", "ctx"), "tp"),
        P(("dp", "ctx"), "tp"),
        P("tp", ("dp", "ctx")),
        P("dp", ("ctx", "tp"), None),
    )
    out_specs = (
        P("dp", ("ctx", "tp"), None),
        P("dp", ("ctx", "tp"), None),
        P("dp", "tp", "ctx"),
        P(),
        P(("dp", "ctx"), "tp"),
        P(("dp", "ctx"), "tp"),
        P(),
        P(),
        P("tp", ("dp", "ctx")),
        P(),
        P(("dp", "ctx"), "tp"),
        P(("dp", "ctx"), "tp"),
        P("tp", ("dp", "ctx")),
    )

    return jax.shard_map(
        on_device, mesh=mesh, in_specs=in_specs, out_specs=out_specs, check_vma=False
    )
```

```python
import functools
import math

import jax
import jax.numpy as jnp
from jax import lax
from jax.experimental import pallas as pl
from jax.experimental.pallas import tpu as pltpu
from jax.sharding import PartitionSpec as P


epsilon = 1e-05
rope_base = 1000000.0
f32 = jnp.float32
bf16 = jnp.bfloat16
log2e = math.log2(math.e)


def mm(a, b):
    return lax.dot_general(a, b, (((1,), (0,)), ((), ())), preferred_element_type=f32)


def mm_nt(a, b):
    return lax.dot_general(a, b, (((1,), (1,)), ((), ())), preferred_element_type=f32)


def lanes(shape):
    return lax.broadcasted_iota(jnp.int32, shape, len(shape) - 1)


def rows_of(shape):
    return lax.broadcasted_iota(jnp.int32, shape, 0)


def sds(shape, dtype):
    return jax.ShapeDtypeStruct(shape, dtype)


VM = pl.BlockSpec(memory_space=pltpu.VMEM)
SM = pl.BlockSpec(memory_space=pltpu.SMEM)


def whole_call(body, outs, args, flops, scratch=(), scalars=True):
    moved = sum(math.prod(a.shape) * a.dtype.itemsize for a in list(args) + list(outs))
    specs = [VM] * len(args)
    if scalars:
        specs[0] = SM
    return pl.pallas_call(
        body,
        out_shape=list(outs),
        in_specs=specs,
        out_specs=[VM] * len(outs),
        scratch_shapes=list(scratch),
        cost_estimate=pl.CostEstimate(flops=int(flops), bytes_accessed=int(moved), transcendentals=0),
    )(*args)


def on_device(
    tokens,
    attention_gain,
    query_weight,
    key_value_weight,
    query_gain,
    key_gain,
    output_weight,
    ffn_gain,
    gate_weight,
    up_weight,
    down_weight,
    cotangent,
):
    hw = query_gain.shape[0]
    pw = 2 * hw
    R = tokens.shape[1]
    W = tokens.shape[2]
    NT = lax.axis_size("tp")
    NC = lax.axis_size("ctx")
    N = lax.axis_size("dp") * NC
    B = R * NT
    C = query_weight.shape[1]
    F = gate_weight.shape[1]
    QH = C // hw
    KH = key_value_weight.shape[1] // pw
    assert QH == 2 * KH
    H = W // 2
    blk = W // N
    scale = 1.0 / math.sqrt(hw)
    c2 = scale * log2e
    masks = list(range(0, N, 2)) + list(range(1, N, 2))
    me = lax.axis_index("dp") * NC + lax.axis_index("ctx")
    ctx = lax.axis_index("ctx")
    z = lax.axis_index("tp")
    where = jnp.stack([me, ctx, z]).astype(jnp.int32)
    aligned = blk % 128 == 0

    def plane(v, mask):
        return lax.ppermute(v, ("dp", "ctx"), [(i, i ^ mask) for i in range(N)])

    def column(v, mask):
        return lax.ppermute(v, "tp", [(i, i ^ mask) for i in range(NT)])

    def along(v, mask, keep):
        pairs = [(i, i ^ mask) for i in range(NC) if keep(i, i ^ mask)]
        return lax.ppermute(v, "ctx", pairs)

    def after(v, *deps):
        return lax.optimization_barrier((v,) + deps)[0]

    def gather_near(own):
        return [own] + [plane(own, r) for r in range(2, N, 2)]

    def gather_core(near):
        mine = jnp.concatenate(near, axis=1)
        return mine, plane(mine, 1)

    def share_out(refs, total, k):
        m = total.shape[0] * 2 // N
        for i, ref in enumerate(refs):
            ref[k] = total[i * m : (i + 1) * m].astype(ref.dtype)

    def share_shapes(kinds, cols):
        shape = (kinds, H * 2 // N, cols)
        return [sds(shape, f32)] + [sds(shape, bf16)] * (N // 2 - 1)

    def close_sum(own, parts, turned):
        kinds, m, cols = own.shape

        def body(first, *refs):
            parts, outs = refs[: len(parts_in)], refs[len(parts_in) :]
            for k in range(kinds):
                total = first[k]
                for p in parts:
                    total = total + p[k].astype(f32)
                outs[k][...] = total if k < kinds - turned else total.T

        parts_in = parts
        return whole_call(
            body,
            [sds((m, cols), f32)] * (kinds - turned) + [sds((cols, m), f32)] * turned,
            (own, *parts),
            own.size * N,
            scalars=False,
        )

    def gather_column(own):
        return [own] + [column(own, k) for k in range(1, NT)]

    def spread_column(pieces):
        return [pieces[0]] + [column(pieces[k], k) for k in range(1, NT)]

    def put_slots(refs, value):
        for k, ref in enumerate(refs):
            ref[...] = value[k * R : (k + 1) * R].astype(ref.dtype)

    def join_slots(refs):
        return jnp.concatenate([ref[...] for ref in refs], axis=0)

    def take_cols(v, index, size, order):
        picks = index ^ jnp.array(order, jnp.int32)
        return jnp.take(v.reshape(v.shape[0], -1, size), picks, axis=1).reshape(v.shape)

    own_qkv = jnp.stack([query_weight, key_value_weight])

    def pre_body(s_ref, t_ref, c_ref, g_ref, o_ref, n_ref, t_out, c_out, g_out, ot_out):
        index = s_ref[0]
        for s, mask in enumerate(masks):
            if aligned:
                src = pl.ds(pl.multiple_of((index ^ mask) * blk, blk), blk)
            else:
                src = slice(s * blk, (s + 1) * blk)
            dst = slice(s * blk, (s + 1) * blk)
            t_out[:, dst] = t_ref[:, src]
            c_out[:, dst] = c_ref[:, src]
            g_out[:, dst] = g_ref[:, src]
        x = t_out[...].astype(f32)
        inv = lax.rsqrt(jnp.mean(x * x, axis=-1, keepdims=True) + epsilon)
        n_ref[...] = (x * inv * g_out[0:1, :]).astype(bf16)
        ot_out[...] = o_ref[...].T

    gains = jnp.stack([attention_gain, ffn_gain])
    t_in, c_in, g_in = tokens[0], cotangent[0], gains
    if not aligned:
        t_in, c_in, g_in = (take_cols(v, me, blk, masks) for v in (t_in, c_in, g_in))
    normed, tok, cot, gain2, own_out = whole_call(
        pre_body,
        [sds((R, W), bf16)] * 3 + [sds((2, W), f32), sds((blk, C), bf16)],
        (where, t_in, c_in, g_in, output_weight),
        R * W * 8,
    )
    first_pieces = gather_column(normed)
    qkv_near = gather_near(after(own_qkv, normed))
    qkv_m, qkv_o = gather_core(qkv_near)
    own_ffn = jnp.stack([gate_weight, up_weight, down_weight.T])
    ffn_near = gather_near(after(own_ffn, normed))
    out_cols = jnp.concatenate(gather_column(own_out), axis=1)[None]
    out_near = gather_near(out_cols)
    cot_pieces = gather_column(cot)

    half_width = hw // 2
    freq = jnp.exp(jnp.arange(half_width, dtype=f32) * (-2.0 * math.log(rope_base) / hw))
    positions = ctx * B + (jnp.arange(B, dtype=jnp.int32) ^ (z * R))
    angle = positions.astype(f32)[:, None] * freq[None, :]
    cos_h, sin_h = jnp.cos(angle), jnp.sin(angle)
    cosine = jnp.tile(cos_h, (1, 2 * QH))
    sine = jnp.tile(jnp.concatenate([-sin_h, sin_h], -1), (1, QH))
    qg = jnp.tile(query_gain, QH)[None]
    kg = jnp.tile(jnp.concatenate([key_gain, jnp.ones_like(key_gain)]), KH)[None]

    def three_terms(x):
        high = x.astype(bf16)
        rest = x - high.astype(f32)
        low = rest.astype(bf16)
        return high, low, (rest - low.astype(f32)).astype(bf16)

    def head_mean(x):
        n = x.shape[1]
        same = rows_of((n, n)) // hw == lanes((n, n)) // hw
        ones = jnp.where(same, 1.0 / hw, 0.0).astype(bf16)
        return sum(mm(term, ones) for term in three_terms(x))

    def swap_halves(x):
        first = lanes(x.shape) % hw < half_width
        return jnp.where(
            first, pltpu.roll(x, x.shape[1] - half_width, 1), pltpu.roll(x, half_width, 1)
        )

    def qkv_body(*refs):
        wm, wo, cs, sn, qg_ref, kg_ref, rq, pr, q_raw, p_raw = refs[NT:]
        rows = join_slots(refs[:NT])
        left, right = rows[:, :H], rows[:, H:]
        q = mm(left, wm[0]) + mm(right, wo[0])
        p = mm(left, wm[1]) + mm(right, wo[1])
        q_raw[...] = q
        p_raw[...] = p
        qn = q * lax.rsqrt(head_mean(q * q) + epsilon) * qg_ref[...]
        rq[...] = (qn * cs[...] + swap_halves(qn) * sn[...]).astype(bf16)
        kn = p * lax.rsqrt(head_mean(p * p) + epsilon) * kg_ref[...]
        kr = kn * cs[...] + swap_halves(kn) * sn[...]
        pr[...] = jnp.where(lanes(p.shape) % pw < hw, kr, p).astype(bf16)

    rot_q, pair, q_raw, p_raw = whole_call(
        qkv_body,
        [sds((B, C), bf16), sds((B, C), bf16), sds((B, C), f32), sds((B, C), f32)],
        (*first_pieces, qkv_m, qkv_o, cosine, sine, qg, kg),
        4 * B * W * C,
        scalars=False,
    )

    earlier = lambda i, j: i < j
    kv_even = [pair] + [along(pair, r, earlier) for r in range(2, NC, 2)]
    kv_odd = [along(pair, 1, earlier)]
    for r in range(2, NC, 2):
        kv_odd.append(along(kv_even[r // 2], 1, lambda i, j: (i ^ r) < i))
    kv_pieces = [v for pq in zip(kv_even, kv_odd) for v in pq]
    out_m, out_o = gather_core(out_near)

    def widen(x, part):
        moved = x if part == 0 else pltpu.roll(x, hw, 1)
        return jnp.where(lanes(x.shape) < hw, moved, 0.0)

    def widen_high(x, part):
        moved = x if part == 1 else pltpu.roll(x, hw, 1)
        return jnp.where(lanes(x.shape) >= hw, moved, 0.0)

    def causal(zz):
        key = rows_of((B, B)) ^ zz
        qry = lanes((B, B)) ^ zz
        return key <= qry

    def fwd_body(s_ref, q_ref, *refs):
        kv_in, slot_refs = refs[:NC], refs[NC : NC + NT]
        att_ref, lse_ref, qz, acc, tot, kv_ref = refs[NC + NT :]
        r, h = pl.program_id(0), pl.program_id(1)
        here = s_ref[1]

        @pl.when((r == 0) & (h == 0))
        def _():
            for hd in range(QH):
                x = q_ref[:, (hd // 2) * pw : (hd // 2 + 1) * pw].astype(f32)
                qz[hd] = widen(x, hd % 2).astype(bf16)
            for k in range(NC):
                kv_ref[k] = kv_in[k][...]

        def step(masked):
            kv = kv_ref[r, :, pl.ds(pl.multiple_of(h * pw, pw), pw)]
            kvt = kv.astype(f32).T.astype(bf16)
            for g in range(2):
                hd = 2 * h + g
                e = jnp.exp2(mm_nt(kv, qz[hd]) * c2)
                if masked:
                    e = jnp.where(causal(s_ref[2] * R), e, 0.0)
                part = jnp.sum(e, axis=0, keepdims=True)
                o = mm(kvt, e.astype(bf16))
                if masked:
                    tot[hd] = jnp.broadcast_to(part, (8, B))
                    acc[hd] = o
                else:
                    tot[hd] += jnp.broadcast_to(part, (8, B))
                    acc[hd] += o

        @pl.when(r == 0)
        def _():
            step(True)

        @pl.when((here ^ r) < here)
        def _():
            step(False)

        @pl.when((r == NC - 1) & (h == KH - 1))
        def _():
            outs = [acc[hd][hw:] / tot[hd][0:1] for hd in range(QH)]
            att = jnp.concatenate(outs, axis=0).T.astype(bf16)
            att_ref[...] = att
            put_slots(slot_refs, att)
            for hd in range(QH):
                lse_ref[hd] = jnp.log(tot[hd][0:1])

    fixed = lambda shape: pl.BlockSpec(shape, lambda r, h: (0,) * len(shape))
    *att_slots, attended, lse = pl.pallas_call(
        fwd_body,
        grid=(NC, KH),
        out_shape=[sds((R, C), bf16)] * NT + [sds((B, C), bf16), sds((QH, 1, B), f32)],
        in_specs=[SM] + [fixed((B, C))] * (1 + NC),
        out_specs=[fixed((R, C))] * NT + [fixed((B, C)), fixed((QH, 1, B))],
        scratch_shapes=[
            pltpu.VMEM((QH, B, pw), bf16),
            pltpu.VMEM((QH, pw, B), f32),
            pltpu.VMEM((QH, 8, B), f32),
            pltpu.VMEM((NC, B, C), bf16),
        ],
        cost_estimate=pl.CostEstimate(
            flops=16 * QH * B * B * pw, bytes_accessed=4 * B * C * 2, transcendentals=4 * QH * B * B
        ),
        name="attention_forward",
    )(where, rot_q, *kv_pieces)

    att_pieces = spread_column(att_slots)
    ffn_m, ffn_o = gather_core(ffn_near)

    def out_body(*refs):
        pieces, (om, oo, t_ref, g_ref, res, nrm) = refs[:NT], refs[NT:]
        a = jnp.concatenate([p[...] for p in pieces], axis=1)
        x = t_ref[...].astype(f32) + jnp.concatenate([mm_nt(a, om[0]), mm_nt(a, oo[0])], axis=1)
        res[...] = x
        inv = lax.rsqrt(jnp.mean(x * x, axis=-1, keepdims=True) + epsilon)
        nrm[...] = (x * inv * g_ref[1:2, :]).astype(bf16)

    resid, normed_f = whole_call(
        out_body,
        [sds((R, W), f32), sds((R, W), bf16)],
        (*att_pieces, out_m, out_o, tok, gain2),
        2 * R * W * W,
        scalars=False,
    )
    second_pieces = gather_column(normed_f)

    chunks = [slice(i, min(i + 256, F)) for i in range(0, F, 256)]

    def hidden_body(*refs):
        wm, wo, out = refs[NT:]
        c = join_slots(refs[:NT])
        for cols in chunks:
            out[:, cols] = mm(c[:, :H], wm[0, :, cols]) + mm(c[:, H:], wo[0, :, cols])

    down_spec = pl.BlockSpec((1, H, F), lambda k: (2, 0, 0))
    grad_mid = pl.pallas_call(
        hidden_body,
        grid=(1,),
        out_shape=sds((B, F), f32),
        in_specs=[pl.BlockSpec((R, W), lambda k: (0, 0))] * NT + [down_spec] * 2,
        out_specs=pl.BlockSpec((B, F), lambda k: (0, 0)),
        cost_estimate=pl.CostEstimate(
            flops=2 * B * W * F, bytes_accessed=2 * W * F + 6 * B * F, transcendentals=0
        ),
        name="hidden_back",
    )(*cot_pieces, ffn_m, ffn_o)

    def ffn_body(*refs):
        wm, wo, gmid_r, hid = refs[NT : NT + 4]
        gnfs = refs[NT + 4 :]
        r = join_slots(refs[:NT])
        rl, rr = r[:, :H], r[:, H:]
        for cols in chunks:
            gate = mm(rl, wm[0, :, cols]) + mm(rr, wo[0, :, cols])
            up = mm(rl, wm[1, :, cols]) + mm(rr, wo[1, :, cols])
            gmid = gmid_r[:, cols]
            sig = jax.nn.sigmoid(gate)
            act = gate * sig
            hid[0, :, cols] = (gmid * up * sig * (1.0 + gate * (1.0 - sig))).astype(bf16)
            hid[1, :, cols] = (gmid * act).astype(bf16)
            hid[2, :, cols] = (act * up).astype(bf16)
        for w, cols in ((wm, slice(0, H)), (wo, slice(H, W))):
            g = mm_nt(hid[0], w[0]) + mm_nt(hid[1], w[1])
            for k, ref in enumerate(gnfs):
                ref[:, cols] = g[k * R : (k + 1) * R].astype(bf16)

    hidden, *gnf_slots = whole_call(
        ffn_body,
        [sds((3, B, F), bf16)] + [sds((R, W), bf16)] * NT,
        (*second_pieces, ffn_m, ffn_o, grad_mid),
        8 * B * W * F,
        scalars=False,
    )
    gnf_pieces = spread_column(gnf_slots)

    one = lambda shape: pl.BlockSpec(shape, lambda k: (0,) * len(shape))
    kind = lambda rows: pl.BlockSpec((1, rows, F), lambda k: (k, 0, 0))

    def dw_body(cols, *refs):
        r_in, c_in, (h_ref, *rest) = refs[:NT], refs[NT : 2 * NT], refs[2 * NT :]
        lt = rest[-1]
        k = pl.program_id(0)

        @pl.when(k == 0)
        def _():
            lt[0] = jnp.concatenate([ref[:, cols] for ref in r_in], axis=0).T
            lt[1] = jnp.concatenate([ref[:, cols] for ref in c_in], axis=0).T

        total = mm(lt[k // 2], h_ref[0])
        if len(rest) == 2:
            rest[0][0] = total.astype(bf16)
        else:
            share_out(rest[1:-1], total + rest[0][0].astype(f32), 0)

    def half_weights(cols, hid, got):
        outs = share_shapes(3, F) if got else [sds((3, H, F), bf16)]
        return pl.pallas_call(
            functools.partial(dw_body, cols),
            grid=(3,),
            out_shape=outs,
            in_specs=[one((R, W))] * (2 * NT) + [kind(B)] + [kind(H)] * len(got),
            out_specs=[kind(o.shape[1]) for o in outs],
            scratch_shapes=[pltpu.VMEM((2, H, B), bf16)],
            cost_estimate=pl.CostEstimate(
                flops=3 * B * W * F, bytes_accessed=3 * W * F + 6 * B * F, transcendentals=0
            ),
        )(*second_pieces, *cot_pieces, hid, *got)

    (dwf_o,) = half_weights(slice(H, W), hidden, [])
    dwf_got = plane(dwf_o, 1)

    def out_part_body(h_ref, wm, wo, *outs):
        for w, cols in ((wm, slice(0, H)), (wo, slice(H, W))):
            o = mm_nt(h_ref[0], w[0])
            for k, ref in enumerate(outs):
                ref[:, cols] = o[k * R : (k + 1) * R].astype(bf16)

    third = lambda rows: pl.BlockSpec((1, rows, F), lambda k: (2, 0, 0))
    ffn_slots = pl.pallas_call(
        out_part_body,
        grid=(1,),
        out_shape=[sds((R, W), bf16)] * NT,
        in_specs=[third(B), third(H), third(H)],
        out_specs=[one((R, W))] * NT,
        cost_estimate=pl.CostEstimate(
            flops=2 * B * W * F, bytes_accessed=2 * W * F + 2 * B * F, transcendentals=0
        ),
        name="ffn_out",
    )(after(hidden, dwf_o), ffn_m, ffn_o)
    ffn_own, *ffn_sends = half_weights(slice(0, H), hidden, [dwf_got])
    gnf_pieces, ffn_own, ffn_sends, ffn_slots = lax.optimization_barrier(
        (gnf_pieces, ffn_own, ffn_sends, ffn_slots)
    )
    ffn_got = [plane(v, 2 * (i + 1)) for i, v in enumerate(ffn_sends)]

    def back_body(*refs):
        pieces, (res, c_ref, g_ref, om, oo, gres, gg, rg, *gas) = refs[:NT], refs[NT:]
        grad = sum(p[...].astype(f32) for p in pieces)
        x = res[...]
        inv = lax.rsqrt(jnp.mean(x * x, axis=-1, keepdims=True) + epsilon)
        hat = x * inv
        gg[...] = jnp.sum(grad * hat, axis=0, keepdims=True)
        scaled = grad * g_ref[1:2, :]
        through = inv * (scaled - hat * jnp.mean(scaled * hat, axis=-1, keepdims=True))
        total = c_ref[...].astype(f32) + through
        gres[...] = total
        half = total.astype(bf16)
        rg[...] = half
        ga = (mm(half[:, :H], om[0]) + mm(half[:, H:], oo[0])).astype(bf16)
        for k, ref in enumerate(gas):
            ref[...] = ga[:, k * C : (k + 1) * C]

    grad_resid, ffn_gain_part, rg16, *ga_slots = whole_call(
        back_body,
        [sds((R, W), f32), sds((1, W), f32), sds((R, W), bf16)] + [sds((R, C), bf16)] * NT,
        (*gnf_pieces, resid, cot, gain2, out_m, out_o),
        2 * R * W * W,
        scalars=False,
    )
    ga_pieces = spread_column(ga_slots)
    ffn_pieces = spread_column(ffn_slots)

    def dwo_body(cols, g_ref, *refs):
        g = g_ref[:, cols].T
        a = jnp.concatenate([ref[...] for ref in refs[:NT]], axis=1)
        total = mm(g, a)
        rest = refs[NT:]
        if len(rest) == 1:
            rest[0][0] = total.astype(bf16)
        else:
            share_out(rest[1:], total + rest[0][0].astype(f32), 0)

    def half_out(cols, got):
        return whole_call(
            functools.partial(dwo_body, cols),
            share_shapes(1, NT * C) if got else [sds((1, H, NT * C), bf16)],
            (rg16, *att_pieces, *got),
            R * W * NT * C,
            scalars=False,
        )

    (dwo_o,) = half_out(slice(H, W), [])
    out_own, *out_sends = half_out(slice(0, H), [plane(dwo_o, 1)])
    out_got = [plane(v, 2 * (i + 1)) for i, v in enumerate(out_sends)]

    def bwd_body(s_ref, q_ref, a_ref, l_ref, *refs):
        d_in, kv_in = refs[:NT], refs[NT : NT + NC]
        dq_ref, even, odd, qz, dz, acc, dl, kv_ref = refs[NT + NC :]
        r, h = pl.program_id(0), pl.program_id(1)
        here = s_ref[1]

        @pl.when((r == 0) & (h == 0))
        def _():
            d_all = join_slots(d_in).astype(f32)
            for hd in range(QH):
                cols = slice((hd // 2) * pw, (hd // 2 + 1) * pw)
                qz[hd] = widen(q_ref[:, cols].astype(f32), hd % 2).astype(bf16)
                dz[hd] = widen_high(d_all[:, cols], hd % 2).astype(bf16)
            for k in range(NC):
                kv_ref[k] = kv_in[k][...]
            prod = d_all * a_ref[...].astype(f32)
            pick = jnp.where(lanes((8, C)) // hw == rows_of((8, C)), 1.0, 0.0).astype(bf16)
            sums = sum(mm_nt(pick, term) for term in three_terms(prod))
            for hd in range(QH):
                dl[hd] = jnp.broadcast_to(sums[hd : hd + 1], (8, B))

        here_cols = pl.ds(pl.multiple_of(h * pw, pw), pw)

        def put(value):
            @pl.when(r % 2 == 0)
            def _():
                even[r // 2, :, here_cols] = value

            @pl.when(r % 2 == 1)
            def _():
                odd[r // 2, :, here_cols] = value

        def step(masked):
            kv = kv_ref[r, :, here_cols]
            kvt = kv.astype(f32).T.astype(bf16)
            total = None
            for g in range(2):
                hd = 2 * h + g
                q, d = qz[hd], dz[hd]
                shift = l_ref[hd] * log2e
                p = jnp.exp2(mm_nt(kv, q) * c2 - shift)
                if masked:
                    p = jnp.where(causal(s_ref[2] * R), p, 0.0)
                ds = (p * (mm_nt(kv, d) - dl[hd][0:1])).astype(bf16)
                t = jnp.where(lanes((B, pw)) < hw, mm(ds, q) * scale, mm(p.astype(bf16), d))
                total = t if total is None else total + t
                o = mm(kvt, ds)
                if masked:
                    acc[hd] = o
                else:
                    acc[hd] += o
            put(total.astype(bf16))

        @pl.when(r == 0)
        def _():
            step(True)

        @pl.when((here ^ r) < here)
        def _():
            step(False)

        @pl.when((here ^ r) > here)
        def _():
            put(jnp.zeros((B, pw), bf16))

        @pl.when((r == NC - 1) & (h == KH - 1))
        def _():
            outs = [acc[hd][:hw] for hd in range(QH)]
            dq_ref[...] = jnp.concatenate(outs, axis=0).T * scale

    grad_rot_q, dkv_even, dkv_odd = pl.pallas_call(
        bwd_body,
        grid=(NC, KH),
        out_shape=[sds((B, C), f32)] + [sds((NC // 2, B, C), bf16)] * 2,
        in_specs=[SM, fixed((B, C)), fixed((B, C)), fixed((QH, 1, B))]
        + [fixed((R, C))] * NT
        + [fixed((B, C))] * NC,
        out_specs=[fixed((B, C))] + [fixed((NC // 2, B, C))] * 2,
        scratch_shapes=[
            pltpu.VMEM((QH, B, pw), bf16),
            pltpu.VMEM((QH, B, pw), bf16),
            pltpu.VMEM((QH, pw, B), f32),
            pltpu.VMEM((QH, 8, B), f32),
            pltpu.VMEM((NC, B, C), bf16),
        ],
        cost_estimate=pl.CostEstimate(
            flops=40 * QH * B * B * pw, bytes_accessed=8 * B * C * 2, transcendentals=4 * QH * B * B
        ),
        name="attention_backward",
    )(where, rot_q, attended, lse, *ga_pieces, *kv_pieces)

    odd = lax.ppermute(dkv_odd, "ctx", [(i, i ^ 1) for i in range(NC)])
    pair_parts = []
    for k in range(1, NC // 2):
        part = (dkv_even[k].astype(f32) + odd[k].astype(f32)).astype(bf16)
        pair_parts.append(along(part, 2 * k, lambda i, j: i // 2 > j // 2))

    def qk_body(s_ref, dq, even, odd_ref, q_raw_r, p_raw_r, cs, sn, qg_ref, kg_ref, wm, wo, g_ref, fg_ref, *refs):
        index = s_ref[0]
        n_parts = len(pair_parts)
        parts, r_in, gnas = refs[:n_parts], refs[n_parts : n_parts + NT], refs[n_parts + NT : n_parts + 2 * NT]
        both_ref, pack = refs[n_parts + 2 * NT :]
        r_all = join_slots(r_in)

        def back(grad, raw, gain, live):
            turned = grad * cs[...] - swap_halves(grad) * sn[...]
            inv = lax.rsqrt(head_mean(raw * raw) + epsilon)
            hat = raw * inv
            scaled = turned * gain
            out = inv * (scaled - hat * head_mean(scaled * hat))
            gg = jnp.sum(turned * hat, axis=0, keepdims=True)
            if live is not None:
                out = jnp.where(live, out, grad)
            return out.astype(bf16), gg

        dp = even[0].astype(f32) + odd_ref[0].astype(f32)
        for p in parts:
            dp = dp + p[...].astype(f32)
        gq, qsum = back(dq[...], q_raw_r[...], qg_ref[...], None)
        live = lanes((B, C)) % pw < hw
        gp, ksum = back(dp, p_raw_r[...], kg_ref[...], live)
        both_ref[...] = jnp.concatenate([gq, gp], axis=1)
        pack[...] = jnp.zeros_like(pack)
        for w, cols, first in ((wm, slice(0, H), 0), (wo, slice(H, W), N // 2)):
            part = mm_nt(gq, w[0]) + mm_nt(gp, w[1])
            for k, ref in enumerate(gnas):
                ref[:, cols] = part[k * R : (k + 1) * R].astype(bf16)
            agg = jnp.sum(part * r_all[:, cols].astype(f32), axis=0, keepdims=True) / g_ref[0:1, cols]
            for i in range(N // 2):
                to = index ^ masks[first + i]
                pack[pl.ds(to, 1), :] = agg[:, i * blk : (i + 1) * blk]
                pack[pl.ds(N + to, 1), :] = fg_ref[:, (first + i) * blk : (first + i + 1) * blk]
        heads_q = sum(qsum[:, i * pw : (i + 1) * pw] for i in range(KH))
        heads_q = heads_q + pltpu.roll(heads_q, hw, 1)
        heads_k = sum(ksum[:, i * pw : (i + 1) * pw] for i in range(KH))
        pack[2 * N : 2 * N + 1, :hw] = heads_q[:, :hw]
        pack[2 * N + 1 : 2 * N + 2, :hw] = heads_k[:, :hw]

    *gna_slots, both16, packed = whole_call(
        qk_body,
        [sds((R, W), bf16)] * NT + [sds((B, 2 * C), bf16), sds((2 * N + 8, blk), f32)],
        (
            where, grad_rot_q, dkv_even, odd, q_raw, p_raw, cosine, sine, qg, kg,
            qkv_m, qkv_o, gain2, ffn_gain_part, *pair_parts, *first_pieces,
        ),
        4 * B * W * C,
    )
    gna_pieces = spread_column(gna_slots)

    G = 2 * N + 8
    X = -(-G // 16) * 16
    gain_pieces = gather_column(packed)

    def put_gains(ref, at, gains):
        high = gains.astype(bf16)
        low = (gains - high.astype(f32)).astype(bf16)
        for k, part in enumerate((high, low)):
            ref[k, at : at + X] = jnp.zeros((X, C), bf16)
            ref[k, at : at + G, :blk] = part

    def read_gains(ref, at):
        return sum(ref[k, at : at + G, :blk].astype(f32) for k in range(2))

    def proj_body(cols, *refs):
        gains = sum(ref[...] for ref in refs[NT : 2 * NT])
        b_ref, *rest = refs[2 * NT :]
        rt = jnp.concatenate([ref[:, cols] for ref in refs[:NT]], axis=0).T
        full = mm(rt, b_ref[...])
        if len(rest) == 1:
            for k in range(2):
                rest[0][k, :H] = full[:, k * C : (k + 1) * C].astype(bf16)
            put_gains(rest[0], H, gains)
            return
        got, total_gains, own, *sends = rest
        gains = gains + read_gains(got, H)
        total_gains[...] = gains
        for k in range(2):
            part = full[:, k * C : (k + 1) * C] + got[k, :H].astype(f32)
            own[k] = part[:blk]
            for i, ref in enumerate(sends):
                ref[k, :blk] = part[(i + 1) * blk : (i + 2) * blk].astype(bf16)
        for ref in sends:
            put_gains(ref, blk, gains)

    def half_proj(cols, outs, got):
        return whole_call(
            functools.partial(proj_body, cols),
            outs,
            (*first_pieces, *gain_pieces, both16, *got),
            2 * B * W * C,
            scalars=False,
        )

    (proj_o,) = half_proj(slice(H, W), [sds((2, H + X, C), bf16)], [])
    plane_gains, att_own, *att_sends = half_proj(
        slice(0, H),
        [sds((G, blk), f32), sds((2, blk, C), f32)] + [sds((2, blk + X, C), bf16)] * (N // 2 - 1),
        [plane(proj_o, 1)],
    )
    att_got = [plane(v, 2 * (i + 1)) for i, v in enumerate(att_sends)]

    def att_close_body(gains, own, *refs):
        parts, (out_q, out_p, out_g) = refs[: len(att_got)], refs[len(att_got) :]
        for k, ref in enumerate((out_q, out_p)):
            total = own[k]
            for p in parts:
                total = total + p[k, :blk].astype(f32)
            ref[...] = total
        out_g[...] = gains[...] + sum(read_gains(p, blk) for p in parts)

    grad_query, grad_pairs, packed = whole_call(
        att_close_body,
        [sds((blk, C), f32)] * 2 + [sds((G, blk), f32)],
        (plane_gains, att_own, *att_got),
        blk * C * 8,
        scalars=False,
    )

    def out_sum_body(first, *refs):
        parts, outs = refs[: len(out_got)], refs[len(out_got) :]
        total = first[0]
        for p in parts:
            total = total + p[0].astype(f32)
        for k, ref in enumerate(outs):
            ref[...] = total[:, k * C : (k + 1) * C].astype(bf16)

    out_slots = whole_call(
        out_sum_body,
        [sds((blk, C), bf16)] * NT,
        (out_own, *out_got),
        blk * NT * C * 4,
        scalars=False,
    )
    out_pieces = spread_column(out_slots)

    def out_close_body(*refs):
        total = refs[0][...].astype(f32)
        for ref in refs[1:NT]:
            total = total + ref[...].astype(f32)
        refs[NT][...] = total.T

    (grad_output,) = whole_call(
        out_close_body, [sds((C, blk), f32)], out_pieces, blk * C * 4, scalars=False
    )

    def block_body(*refs):
        index = refs[0][0]
        fp, (res, bo) = refs[1 : NT + 1], refs[NT + 1 :]
        block = (res[...] + sum(p[...].astype(f32) for p in fp)).astype(bf16)
        for s, mask in enumerate(masks):
            src = slice(s * blk, (s + 1) * blk)
            if aligned:
                dst = pl.ds(pl.multiple_of((index ^ mask) * blk, blk), blk)
            else:
                dst = src
            bo[:, dst] = block[:, src]

    (block_out,) = whole_call(
        block_body, [sds((R, W), bf16)], (where, *ffn_pieces, resid), R * W * 8
    )

    grad_gate, grad_up, grad_down = close_sum(ffn_own, ffn_got, 1)

    def end_body(*refs):
        s_ref, rest = refs[0], refs[1:]
        gp, (t_ref, gres, g_ref, gt) = rest[:NT], rest[NT:]
        index = s_ref[0]
        grad = sum(p[...].astype(f32) for p in gp)
        x = t_ref[...].astype(f32)
        inv = lax.rsqrt(jnp.mean(x * x, axis=-1, keepdims=True) + epsilon)
        hat = x * inv
        scaled = grad * g_ref[0:1, :]
        total = gres[...] + inv * (scaled - hat * jnp.mean(scaled * hat, axis=-1, keepdims=True))
        for s, mask in enumerate(masks):
            src = slice(s * blk, (s + 1) * blk)
            if aligned:
                dst = pl.ds(pl.multiple_of((index ^ mask) * blk, blk), blk)
            else:
                dst = src
            gt[:, dst] = total[:, src]

    gna_pieces, packed, grad_down, grad_output, grad_query, block_out = (
        lax.optimization_barrier(
            (gna_pieces, packed, grad_down, grad_output, grad_query, block_out)
        )
    )
    (grad_tokens,) = whole_call(
        end_body, [sds((R, W), f32)], (where, *gna_pieces, tok, grad_resid, gain2), R * W * 16
    )
    if not aligned:
        inverse = [masks.index(m) for m in range(N)]
        slot_of = jnp.take(jnp.array(inverse), me ^ jnp.arange(N, dtype=jnp.int32))
        back_cols = lambda v: jnp.take(
            v.reshape(R, N, blk), slot_of, axis=1
        ).reshape(R, W)
        grad_tokens, block_out = back_cols(grad_tokens), back_cols(block_out)

    lse_out = jnp.take(
        lse.reshape(QH, NT, R), z ^ jnp.arange(NT, dtype=jnp.int32), axis=1
    ).reshape(1, QH, B)
    return (
        block_out[None],
        grad_tokens[None],
        lse_out,
        packed[:N].reshape(W),
        grad_query,
        grad_pairs,
        packed[2 * N, :hw],
        packed[2 * N + 1, :hw],
        grad_output,
        packed[N : 2 * N].reshape(W),
        grad_gate,
        grad_up,
        grad_down,
    )


def solution(mesh):
    in_specs = (
        P("dp", ("ctx", "tp"), None),
        P(),
        P(("dp", "ctx"), "tp"),
        P(("dp", "ctx"), "tp"),
        P(),
        P(),
        P("tp", ("dp", "ctx")),
        P(),
        P(("dp", "ctx"), "tp"),
        P(("dp", "ctx"), "tp"),
        P("tp", ("dp", "ctx")),
        P("dp", ("ctx", "tp"), None),
    )
    out_specs = (
        P("dp", ("ctx", "tp"), None),
        P("dp", ("ctx", "tp"), None),
        P("dp", "tp", "ctx"),
        P(),
        P(("dp", "ctx"), "tp"),
        P(("dp", "ctx"), "tp"),
        P(),
        P(),
        P("tp", ("dp", "ctx")),
        P(),
        P(("dp", "ctx"), "tp"),
        P(("dp", "ctx"), "tp"),
        P("tp", ("dp", "ctx")),
    )

    return jax.shard_map(
        on_device, mesh=mesh, in_specs=in_specs, out_specs=out_specs, check_vma=False
    )
```

```python
import functools
import math

import jax
import jax.numpy as jnp
from jax import lax
from jax.experimental import pallas as pl
from jax.experimental.pallas import tpu as pltpu
from jax.sharding import PartitionSpec as P


epsilon = 1e-05
rope_base = 1000000.0
f32 = jnp.float32
bf16 = jnp.bfloat16
log2e = math.log2(math.e)


def mm(a, b):
    return lax.dot_general(a, b, (((1,), (0,)), ((), ())), preferred_element_type=f32)


def mm_nt(a, b):
    return lax.dot_general(a, b, (((1,), (1,)), ((), ())), preferred_element_type=f32)


def lanes(shape):
    return lax.broadcasted_iota(jnp.int32, shape, len(shape) - 1)


def rows_of(shape):
    return lax.broadcasted_iota(jnp.int32, shape, 0)


def sds(shape, dtype):
    return jax.ShapeDtypeStruct(shape, dtype)


VM = pl.BlockSpec(memory_space=pltpu.VMEM)
SM = pl.BlockSpec(memory_space=pltpu.SMEM)


def whole_call(body, outs, args, flops, scratch=(), scalars=True):
    moved = sum(math.prod(a.shape) * a.dtype.itemsize for a in list(args) + list(outs))
    specs = [VM] * len(args)
    if scalars:
        specs[0] = SM
    return pl.pallas_call(
        body,
        out_shape=list(outs),
        in_specs=specs,
        out_specs=[VM] * len(outs),
        scratch_shapes=list(scratch),
        cost_estimate=pl.CostEstimate(flops=int(flops), bytes_accessed=int(moved), transcendentals=0),
    )(*args)


def on_device(
    tokens,
    attention_gain,
    query_weight,
    key_value_weight,
    query_gain,
    key_gain,
    output_weight,
    ffn_gain,
    gate_weight,
    up_weight,
    down_weight,
    cotangent,
):
    hw = query_gain.shape[0]
    pw = 2 * hw
    R = tokens.shape[1]
    W = tokens.shape[2]
    NT = lax.axis_size("tp")
    NC = lax.axis_size("ctx")
    N = lax.axis_size("dp") * NC
    B = R * NT
    C = query_weight.shape[1]
    F = gate_weight.shape[1]
    QH = C // hw
    KH = key_value_weight.shape[1] // pw
    assert QH == 2 * KH
    H = W // 2
    blk = W // N
    scale = 1.0 / math.sqrt(hw)
    c2 = scale * log2e
    masks = list(range(0, N, 2)) + list(range(1, N, 2))
    me = lax.axis_index("dp") * NC + lax.axis_index("ctx")
    ctx = lax.axis_index("ctx")
    z = lax.axis_index("tp")
    where = jnp.stack([me, ctx, z]).astype(jnp.int32)
    aligned = blk % 128 == 0

    def plane(v, mask):
        return lax.ppermute(v, ("dp", "ctx"), [(i, i ^ mask) for i in range(N)])

    def column(v, mask):
        return lax.ppermute(v, "tp", [(i, i ^ mask) for i in range(NT)])

    def along(v, mask, keep):
        pairs = [(i, i ^ mask) for i in range(NC) if keep(i, i ^ mask)]
        return lax.ppermute(v, "ctx", pairs)

    def after(v, *deps):
        return lax.optimization_barrier((v,) + deps)[0]

    def gather_near(own):
        return [own] + [plane(own, r) for r in range(2, N, 2)]

    def gather_core(near):
        mine = jnp.concatenate(near, axis=1)
        return mine, plane(mine, 1)

    def share_out(refs, total, k):
        m = total.shape[0] * 2 // N
        for i, ref in enumerate(refs):
            ref[k] = total[i * m : (i + 1) * m].astype(ref.dtype)

    def share_shapes(kinds, cols):
        shape = (kinds, H * 2 // N, cols)
        return [sds(shape, f32)] + [sds(shape, bf16)] * (N // 2 - 1)

    def close_sum(own, parts):
        kinds, m, cols = own.shape
        part = 384 if cols % 384 == 0 else cols
        n_parts = len(parts)

        def body(first, *refs):
            for k, out in enumerate(refs[n_parts:]):
                total = first[k]
                for p in refs[:n_parts]:
                    total = total + p[k].astype(f32)
                out[...] = total if k < kinds - 1 else total.T

        block = pl.BlockSpec((kinds, m, part), lambda i: (0, 0, i))
        return pl.pallas_call(
            body,
            grid=(cols // part,),
            out_shape=[sds((m, cols), f32)] * (kinds - 1) + [sds((cols, m), f32)],
            in_specs=[block] * (1 + n_parts),
            out_specs=[pl.BlockSpec((m, part), lambda i: (0, i))] * (kinds - 1)
            + [pl.BlockSpec((part, m), lambda i: (i, 0))],
            cost_estimate=pl.CostEstimate(
                flops=own.size * N, bytes_accessed=own.size * 14, transcendentals=0
            ),
        )(own, *parts)

    def gather_column(own):
        return [own] + [column(own, k) for k in range(1, NT)]

    def spread_column(pieces):
        return [pieces[0]] + [column(pieces[k], k) for k in range(1, NT)]

    def put_slots(refs, value):
        for k, ref in enumerate(refs):
            ref[...] = value[k * R : (k + 1) * R].astype(ref.dtype)

    def join_slots(refs):
        return jnp.concatenate([ref[...] for ref in refs], axis=0)

    def take_cols(v, index, size, order):
        picks = index ^ jnp.array(order, jnp.int32)
        return jnp.take(v.reshape(v.shape[0], -1, size), picks, axis=1).reshape(v.shape)

    own_qkv = jnp.stack([query_weight, key_value_weight])

    def pre_body(s_ref, t_ref, c_ref, ga_ref, gf_ref, o_ref, n_ref, t_out, c_out, g_out, ot_out):
        index = s_ref[0]
        for s, mask in enumerate(masks):
            if aligned:
                src = pl.ds(pl.multiple_of((index ^ mask) * blk, blk), blk)
            else:
                src = slice(s * blk, (s + 1) * blk)
            dst = slice(s * blk, (s + 1) * blk)
            t_out[:, dst] = t_ref[:, src]
            c_out[:, dst] = c_ref[:, src]
            g_out[0:1, dst] = ga_ref[:, src]
            g_out[1:2, dst] = gf_ref[:, src]
        x = t_out[...].astype(f32)
        inv = lax.rsqrt(jnp.mean(x * x, axis=-1, keepdims=True) + epsilon)
        n_ref[...] = (x * inv * g_out[0:1, :]).astype(bf16)
        ot_out[...] = o_ref[...].T

    t_in, c_in = tokens[0], cotangent[0]
    ga_in, gf_in = attention_gain.reshape(1, W), ffn_gain.reshape(1, W)
    if not aligned:
        t_in, c_in, ga_in, gf_in = (
            take_cols(v, me, blk, masks) for v in (t_in, c_in, ga_in, gf_in)
        )
    normed, tok, cot, gain2, own_out = whole_call(
        pre_body,
        [sds((R, W), bf16)] * 3 + [sds((2, W), f32), sds((blk, C), bf16)],
        (where, t_in, c_in, ga_in, gf_in, output_weight),
        R * W * 8,
    )
    first_pieces = gather_column(normed)
    qkv_near = gather_near(after(own_qkv, normed))
    qkv_m, qkv_o = gather_core(qkv_near)
    own_ffn = jnp.stack([gate_weight, up_weight, down_weight.T])
    ffn_near = gather_near(after(own_ffn, normed))
    out_cols = jnp.concatenate(gather_column(own_out), axis=1)[None]
    out_near = gather_near(out_cols)
    cot_pieces = gather_column(cot)

    half_width = hw // 2
    freq = jnp.exp(jnp.arange(half_width, dtype=f32) * (-2.0 * math.log(rope_base) / hw))
    positions = ctx * B + (jnp.arange(B, dtype=jnp.int32) ^ (z * R))
    angle = positions.astype(f32)[:, None] * freq[None, :]
    cos_h, sin_h = jnp.cos(angle), jnp.sin(angle)
    cosine = jnp.tile(cos_h, (1, 2 * QH))
    sine = jnp.tile(jnp.concatenate([-sin_h, sin_h], -1), (1, QH))
    qg = jnp.tile(query_gain, QH)[None]
    kg = jnp.tile(jnp.concatenate([key_gain, jnp.ones_like(key_gain)]), KH)[None]

    def three_terms(x):
        high = x.astype(bf16)
        rest = x - high.astype(f32)
        low = rest.astype(bf16)
        return high, low, (rest - low.astype(f32)).astype(bf16)

    def head_mean(x):
        n = x.shape[1]
        same = rows_of((n, n)) // hw == lanes((n, n)) // hw
        ones = jnp.where(same, 1.0 / hw, 0.0).astype(bf16)
        return sum(mm(term, ones) for term in three_terms(x))

    def swap_halves(x):
        first = lanes(x.shape) % hw < half_width
        return jnp.where(
            first, pltpu.roll(x, x.shape[1] - half_width, 1), pltpu.roll(x, half_width, 1)
        )

    def qkv_body(*refs):
        wm, wo, cs, sn, qg_ref, kg_ref, rq, pr, q_raw, p_raw = refs[NT:]
        rows = join_slots(refs[:NT])
        left, right = rows[:, :H], rows[:, H:]
        q = mm(left, wm[0]) + mm(right, wo[0])
        p = mm(left, wm[1]) + mm(right, wo[1])
        q_raw[...] = q
        p_raw[...] = p
        qn = q * lax.rsqrt(head_mean(q * q) + epsilon) * qg_ref[...]
        rq[...] = (qn * cs[...] + swap_halves(qn) * sn[...]).astype(bf16)
        kn = p * lax.rsqrt(head_mean(p * p) + epsilon) * kg_ref[...]
        kr = kn * cs[...] + swap_halves(kn) * sn[...]
        pr[...] = jnp.where(lanes(p.shape) % pw < hw, kr, p).astype(bf16)

    rot_q, pair, q_raw, p_raw = whole_call(
        qkv_body,
        [sds((B, C), bf16), sds((B, C), bf16), sds((B, C), f32), sds((B, C), f32)],
        (*first_pieces, qkv_m, qkv_o, cosine, sine, qg, kg),
        4 * B * W * C,
        scalars=False,
    )

    earlier = lambda i, j: i < j
    kv_even = [pair] + [along(pair, r, earlier) for r in range(2, NC, 2)]
    kv_odd = [along(pair, 1, earlier)]
    for r in range(2, NC, 2):
        kv_odd.append(along(kv_even[r // 2], 1, lambda i, j: (i ^ r) < i))
    kv_pieces = [v for pq in zip(kv_even, kv_odd) for v in pq]
    out_m, out_o = gather_core(out_near)

    def widen(x, part):
        moved = x if part == 0 else pltpu.roll(x, hw, 1)
        return jnp.where(lanes(x.shape) < hw, moved, 0.0)

    def widen_high(x, part):
        moved = x if part == 1 else pltpu.roll(x, hw, 1)
        return jnp.where(lanes(x.shape) >= hw, moved, 0.0)

    def causal(zz):
        key = rows_of((B, B)) ^ zz
        qry = lanes((B, B)) ^ zz
        return key <= qry

    def fwd_body(s_ref, q_ref, *refs):
        kv_in, slot_refs = refs[:NC], refs[NC : NC + NT]
        att_ref, lse_ref, qz, acc, tot, kv_ref = refs[NC + NT :]
        r, h = pl.program_id(0), pl.program_id(1)
        here = s_ref[1]

        @pl.when((r == 0) & (h == 0))
        def _():
            for hd in range(QH):
                x = q_ref[:, (hd // 2) * pw : (hd // 2 + 1) * pw].astype(f32)
                qz[hd] = widen(x, hd % 2).astype(bf16)
            for k in range(NC):
                kv_ref[k] = kv_in[k][...]

        def step(masked):
            kv = kv_ref[r, :, pl.ds(pl.multiple_of(h * pw, pw), pw)]
            kvt = kv.astype(f32).T.astype(bf16)
            for g in range(2):
                hd = 2 * h + g
                e = jnp.exp2(mm_nt(kv, qz[hd]) * c2)
                if masked:
                    e = jnp.where(causal(s_ref[2] * R), e, 0.0)
                part = jnp.sum(e, axis=0, keepdims=True)
                o = mm(kvt, e.astype(bf16))
                if masked:
                    tot[hd] = jnp.broadcast_to(part, (8, B))
                    acc[hd] = o
                else:
                    tot[hd] += jnp.broadcast_to(part, (8, B))
                    acc[hd] += o

        @pl.when(r == 0)
        def _():
            step(True)

        @pl.when((here ^ r) < here)
        def _():
            step(False)

        @pl.when((r == NC - 1) & (h == KH - 1))
        def _():
            outs = [acc[hd][hw:] / tot[hd][0:1] for hd in range(QH)]
            att = jnp.concatenate(outs, axis=0).T.astype(bf16)
            att_ref[...] = att
            put_slots(slot_refs, att)
            for hd in range(QH):
                lse_ref[hd] = jnp.log(tot[hd][0:1])

    fixed = lambda shape: pl.BlockSpec(shape, lambda r, h: (0,) * len(shape))
    *att_slots, attended, lse = pl.pallas_call(
        fwd_body,
        grid=(NC, KH),
        out_shape=[sds((R, C), bf16)] * NT + [sds((B, C), bf16), sds((QH, 1, B), f32)],
        in_specs=[SM] + [fixed((B, C))] * (1 + NC),
        out_specs=[fixed((R, C))] * NT + [fixed((B, C)), fixed((QH, 1, B))],
        scratch_shapes=[
            pltpu.VMEM((QH, B, pw), bf16),
            pltpu.VMEM((QH, pw, B), f32),
            pltpu.VMEM((QH, 8, B), f32),
            pltpu.VMEM((NC, B, C), bf16),
        ],
        cost_estimate=pl.CostEstimate(
            flops=16 * QH * B * B * pw, bytes_accessed=4 * B * C * 2, transcendentals=4 * QH * B * B
        ),
        name="attention_forward",
    )(where, rot_q, *kv_pieces)

    att_pieces = spread_column(att_slots)
    ffn_m, ffn_o = gather_core(ffn_near)

    def out_body(*refs):
        pieces, (om, oo, t_ref, g_ref, res, nrm) = refs[:NT], refs[NT:]
        a = jnp.concatenate([p[...] for p in pieces], axis=1)
        x = t_ref[...].astype(f32) + jnp.concatenate([mm_nt(a, om[0]), mm_nt(a, oo[0])], axis=1)
        res[...] = x
        inv = lax.rsqrt(jnp.mean(x * x, axis=-1, keepdims=True) + epsilon)
        nrm[...] = (x * inv * g_ref[1:2, :]).astype(bf16)

    resid, normed_f = whole_call(
        out_body,
        [sds((R, W), f32), sds((R, W), bf16)],
        (*att_pieces, out_m, out_o, tok, gain2),
        2 * R * W * W,
        scalars=False,
    )
    second_pieces = gather_column(normed_f)

    chunks = [slice(i, min(i + 256, F)) for i in range(0, F, 256)]

    def hidden_body(*refs):
        wm, wo, out = refs[NT:]
        c = join_slots(refs[:NT])
        for cols in chunks:
            out[:, cols] = mm(c[:, :H], wm[0, :, cols]) + mm(c[:, H:], wo[0, :, cols])

    down_spec = pl.BlockSpec((1, H, F), lambda k: (2, 0, 0))
    grad_mid = pl.pallas_call(
        hidden_body,
        grid=(1,),
        out_shape=sds((B, F), f32),
        in_specs=[pl.BlockSpec((R, W), lambda k: (0, 0))] * NT + [down_spec] * 2,
        out_specs=pl.BlockSpec((B, F), lambda k: (0, 0)),
        cost_estimate=pl.CostEstimate(
            flops=2 * B * W * F, bytes_accessed=2 * W * F + 6 * B * F, transcendentals=0
        ),
        name="hidden_back",
    )(*cot_pieces, ffn_m, ffn_o)

    lse_out = jnp.take(
        lse.reshape(QH, NT, R), z ^ jnp.arange(NT, dtype=jnp.int32), axis=1
    ).reshape(1, QH, B)
    grad_mid, lse_out = lax.optimization_barrier((grad_mid, lse_out))

    def ffn_body(*refs):
        wm, wo, gmid_r, hid = refs[NT : NT + 4]
        gnfs = refs[NT + 4 :]
        r = join_slots(refs[:NT])
        rl, rr = r[:, :H], r[:, H:]
        for cols in chunks:
            gate = mm(rl, wm[0, :, cols]) + mm(rr, wo[0, :, cols])
            up = mm(rl, wm[1, :, cols]) + mm(rr, wo[1, :, cols])
            gmid = gmid_r[:, cols]
            sig = jax.nn.sigmoid(gate)
            act = gate * sig
            hid[0, :, cols] = (gmid * up * sig * (1.0 + gate * (1.0 - sig))).astype(bf16)
            hid[1, :, cols] = (gmid * act).astype(bf16)
            hid[2, :, cols] = (act * up).astype(bf16)
        for w, cols in ((wm, slice(0, H)), (wo, slice(H, W))):
            g = mm_nt(hid[0], w[0]) + mm_nt(hid[1], w[1])
            for k, ref in enumerate(gnfs):
                ref[:, cols] = g[k * R : (k + 1) * R].astype(bf16)

    hidden, *gnf_slots = whole_call(
        ffn_body,
        [sds((3, B, F), bf16)] + [sds((R, W), bf16)] * NT,
        (*second_pieces, ffn_m, ffn_o, grad_mid),
        8 * B * W * F,
        scalars=False,
    )
    gnf_pieces = spread_column(gnf_slots)

    one = lambda shape: pl.BlockSpec(shape, lambda k: (0,) * len(shape))
    kind = lambda rows: pl.BlockSpec((1, rows, F), lambda k: (k, 0, 0))

    def dw_body(cols, *refs):
        r_in, c_in, (h_ref, *rest) = refs[:NT], refs[NT : 2 * NT], refs[2 * NT :]
        lt = rest[-1]
        k = pl.program_id(0)

        @pl.when(k == 0)
        def _():
            lt[0] = jnp.concatenate([ref[:, cols] for ref in r_in], axis=0).T
            lt[1] = jnp.concatenate([ref[:, cols] for ref in c_in], axis=0).T

        total = mm(lt[k // 2], h_ref[0])
        if len(rest) == 2:
            rest[0][0] = total.astype(bf16)
        else:
            share_out(rest[1:-1], total + rest[0][0].astype(f32), 0)

    def half_weights(cols, hid, got):
        outs = share_shapes(3, F) if got else [sds((3, H, F), bf16)]
        return pl.pallas_call(
            functools.partial(dw_body, cols),
            grid=(3,),
            out_shape=outs,
            in_specs=[one((R, W))] * (2 * NT) + [kind(B)] + [kind(H)] * len(got),
            out_specs=[kind(o.shape[1]) for o in outs],
            scratch_shapes=[pltpu.VMEM((2, H, B), bf16)],
            cost_estimate=pl.CostEstimate(
                flops=3 * B * W * F, bytes_accessed=3 * W * F + 6 * B * F, transcendentals=0
            ),
        )(*second_pieces, *cot_pieces, hid, *got)

    (dwf_o,) = half_weights(slice(H, W), hidden, [])
    dwf_got = plane(dwf_o, 1)

    def out_part_body(h_ref, wm, wo, *outs):
        for w, cols in ((wm, slice(0, H)), (wo, slice(H, W))):
            o = mm_nt(h_ref[0], w[0])
            for k, ref in enumerate(outs):
                ref[:, cols] = o[k * R : (k + 1) * R].astype(bf16)

    third = lambda rows: pl.BlockSpec((1, rows, F), lambda k: (2, 0, 0))
    ffn_slots = pl.pallas_call(
        out_part_body,
        grid=(1,),
        out_shape=[sds((R, W), bf16)] * NT,
        in_specs=[third(B), third(H), third(H)],
        out_specs=[one((R, W))] * NT,
        cost_estimate=pl.CostEstimate(
            flops=2 * B * W * F, bytes_accessed=2 * W * F + 2 * B * F, transcendentals=0
        ),
        name="ffn_out",
    )(after(hidden, dwf_o), ffn_m, ffn_o)
    ffn_own, *ffn_sends = half_weights(slice(0, H), hidden, [dwf_got])
    gnf_pieces, ffn_own, ffn_sends, ffn_slots = lax.optimization_barrier(
        (gnf_pieces, ffn_own, ffn_sends, ffn_slots)
    )
    ffn_got = [plane(v, 2 * (i + 1)) for i, v in enumerate(ffn_sends)]

    def back_body(*refs):
        pieces, (res, c_ref, g_ref, om, oo, gres, gg, rg, *gas) = refs[:NT], refs[NT:]
        grad = sum(p[...].astype(f32) for p in pieces)
        x = res[...]
        inv = lax.rsqrt(jnp.mean(x * x, axis=-1, keepdims=True) + epsilon)
        hat = x * inv
        gg[...] = jnp.sum(grad * hat, axis=0, keepdims=True)
        scaled = grad * g_ref[1:2, :]
        through = inv * (scaled - hat * jnp.mean(scaled * hat, axis=-1, keepdims=True))
        total = c_ref[...].astype(f32) + through
        gres[...] = total
        half = total.astype(bf16)
        rg[...] = half
        ga = (mm(half[:, :H], om[0]) + mm(half[:, H:], oo[0])).astype(bf16)
        for k, ref in enumerate(gas):
            ref[...] = ga[:, k * C : (k + 1) * C]

    grad_resid, ffn_gain_part, rg16, *ga_slots = whole_call(
        back_body,
        [sds((R, W), f32), sds((1, W), f32), sds((R, W), bf16)] + [sds((R, C), bf16)] * NT,
        (*gnf_pieces, resid, cot, gain2, out_m, out_o),
        2 * R * W * W,
        scalars=False,
    )
    ga_pieces = spread_column(ga_slots)
    ffn_pieces = spread_column(ffn_slots)

    def dwo_body(cols, g_ref, *refs):
        g = g_ref[:, cols].T
        a = jnp.concatenate([ref[...] for ref in refs[:NT]], axis=1)
        total = mm(g, a)
        rest = refs[NT:]
        if len(rest) == 1:
            rest[0][0] = total.astype(bf16)
        else:
            share_out(rest[1:], total + rest[0][0].astype(f32), 0)

    def half_out(cols, got):
        return whole_call(
            functools.partial(dwo_body, cols),
            share_shapes(1, NT * C) if got else [sds((1, H, NT * C), bf16)],
            (rg16, *att_pieces, *got),
            R * W * NT * C,
            scalars=False,
        )

    (dwo_o,) = half_out(slice(H, W), [])
    out_own, *out_sends = half_out(slice(0, H), [plane(dwo_o, 1)])
    out_got = [plane(v, 2 * (i + 1)) for i, v in enumerate(out_sends)]

    def bwd_body(s_ref, q_ref, a_ref, l_ref, *refs):
        d_in, kv_in = refs[:NT], refs[NT : NT + NC]
        dq_ref, even, odd, qz, dz, acc, dl, kv_ref = refs[NT + NC :]
        r, h = pl.program_id(0), pl.program_id(1)
        here = s_ref[1]

        @pl.when((r == 0) & (h == 0))
        def _():
            d_all = join_slots(d_in).astype(f32)
            for hd in range(QH):
                cols = slice((hd // 2) * pw, (hd // 2 + 1) * pw)
                qz[hd] = widen(q_ref[:, cols].astype(f32), hd % 2).astype(bf16)
                dz[hd] = widen_high(d_all[:, cols], hd % 2).astype(bf16)
            for k in range(NC):
                kv_ref[k] = kv_in[k][...]
            prod = d_all * a_ref[...].astype(f32)
            pick = jnp.where(lanes((8, C)) // hw == rows_of((8, C)), 1.0, 0.0).astype(bf16)
            sums = sum(mm_nt(pick, term) for term in three_terms(prod))
            for hd in range(QH):
                dl[hd] = jnp.broadcast_to(sums[hd : hd + 1], (8, B))

        here_cols = pl.ds(pl.multiple_of(h * pw, pw), pw)

        def put(value):
            @pl.when(r % 2 == 0)
            def _():
                even[r // 2, :, here_cols] = value

            @pl.when(r % 2 == 1)
            def _():
                odd[r // 2, :, here_cols] = value

        def step(masked):
            kv = kv_ref[r, :, here_cols]
            kvt = kv.astype(f32).T.astype(bf16)
            total = None
            for g in range(2):
                hd = 2 * h + g
                q, d = qz[hd], dz[hd]
                shift = l_ref[hd] * log2e
                p = jnp.exp2(mm_nt(kv, q) * c2 - shift)
                if masked:
                    p = jnp.where(causal(s_ref[2] * R), p, 0.0)
                ds = (p * (mm_nt(kv, d) - dl[hd][0:1])).astype(bf16)
                t = jnp.where(lanes((B, pw)) < hw, mm(ds, q) * scale, mm(p.astype(bf16), d))
                total = t if total is None else total + t
                o = mm(kvt, ds)
                if masked:
                    acc[hd] = o
                else:
                    acc[hd] += o
            put(total.astype(bf16))

        @pl.when(r == 0)
        def _():
            step(True)

        @pl.when((here ^ r) < here)
        def _():
            step(False)

        @pl.when((here ^ r) > here)
        def _():
            put(jnp.zeros((B, pw), bf16))

        @pl.when((r == NC - 1) & (h == KH - 1))
        def _():
            outs = [acc[hd][:hw] for hd in range(QH)]
            dq_ref[...] = jnp.concatenate(outs, axis=0).T * scale

    grad_rot_q, dkv_even, dkv_odd = pl.pallas_call(
        bwd_body,
        grid=(NC, KH),
        out_shape=[sds((B, C), f32)] + [sds((NC // 2, B, C), bf16)] * 2,
        in_specs=[SM, fixed((B, C)), fixed((B, C)), fixed((QH, 1, B))]
        + [fixed((R, C))] * NT
        + [fixed((B, C))] * NC,
        out_specs=[fixed((B, C))] + [fixed((NC // 2, B, C))] * 2,
        scratch_shapes=[
            pltpu.VMEM((QH, B, pw), bf16),
            pltpu.VMEM((QH, B, pw), bf16),
            pltpu.VMEM((QH, pw, B), f32),
            pltpu.VMEM((QH, 8, B), f32),
            pltpu.VMEM((NC, B, C), bf16),
        ],
        cost_estimate=pl.CostEstimate(
            flops=40 * QH * B * B * pw, bytes_accessed=8 * B * C * 2, transcendentals=4 * QH * B * B
        ),
        name="attention_backward",
    )(where, rot_q, attended, lse, *ga_pieces, *kv_pieces)

    odd = lax.ppermute(dkv_odd, "ctx", [(i, i ^ 1) for i in range(NC)])
    pair_parts = []
    for k in range(1, NC // 2):
        part = (dkv_even[k].astype(f32) + odd[k].astype(f32)).astype(bf16)
        pair_parts.append(along(part, 2 * k, lambda i, j: i // 2 > j // 2))

    def qk_body(s_ref, dq, even, odd_ref, q_raw_r, p_raw_r, cs, sn, qg_ref, kg_ref, wm, wo, g_ref, fg_ref, *refs):
        index = s_ref[0]
        n_parts = len(pair_parts)
        parts, r_in, gnas = refs[:n_parts], refs[n_parts : n_parts + NT], refs[n_parts + NT : n_parts + 2 * NT]
        both_ref, pack = refs[n_parts + 2 * NT :]
        r_all = join_slots(r_in)

        def back(grad, raw, gain, live):
            turned = grad * cs[...] - swap_halves(grad) * sn[...]
            inv = lax.rsqrt(head_mean(raw * raw) + epsilon)
            hat = raw * inv
            scaled = turned * gain
            out = inv * (scaled - hat * head_mean(scaled * hat))
            gg = jnp.sum(turned * hat, axis=0, keepdims=True)
            if live is not None:
                out = jnp.where(live, out, grad)
            return out.astype(bf16), gg

        dp = even[0].astype(f32) + odd_ref[0].astype(f32)
        for p in parts:
            dp = dp + p[...].astype(f32)
        gq, qsum = back(dq[...], q_raw_r[...], qg_ref[...], None)
        live = lanes((B, C)) % pw < hw
        gp, ksum = back(dp, p_raw_r[...], kg_ref[...], live)
        both_ref[...] = jnp.concatenate([gq, gp], axis=1)
        pack[...] = jnp.zeros_like(pack)
        for w, cols, first in ((wm, slice(0, H), 0), (wo, slice(H, W), N // 2)):
            part = mm_nt(gq, w[0]) + mm_nt(gp, w[1])
            for k, ref in enumerate(gnas):
                ref[:, cols] = part[k * R : (k + 1) * R].astype(bf16)
            agg = jnp.sum(part * r_all[:, cols].astype(f32), axis=0, keepdims=True) / g_ref[0:1, cols]
            for i in range(N // 2):
                to = index ^ masks[first + i]
                pack[pl.ds(to, 1), :] = agg[:, i * blk : (i + 1) * blk]
                pack[pl.ds(N + to, 1), :] = fg_ref[:, (first + i) * blk : (first + i + 1) * blk]
        heads_q = sum(qsum[:, i * pw : (i + 1) * pw] for i in range(KH))
        heads_q = heads_q + pltpu.roll(heads_q, hw, 1)
        heads_k = sum(ksum[:, i * pw : (i + 1) * pw] for i in range(KH))
        pack[2 * N : 2 * N + 1, :hw] = heads_q[:, :hw]
        pack[2 * N + 1 : 2 * N + 2, :hw] = heads_k[:, :hw]

    *gna_slots, both16, packed = whole_call(
        qk_body,
        [sds((R, W), bf16)] * NT + [sds((B, 2 * C), bf16), sds((2 * N + 8, blk), f32)],
        (
            where, grad_rot_q, dkv_even, odd, q_raw, p_raw, cosine, sine, qg, kg,
            qkv_m, qkv_o, gain2, ffn_gain_part, *pair_parts, *first_pieces,
        ),
        4 * B * W * C,
    )
    gna_pieces = spread_column(gna_slots)

    G = 2 * N + 8
    X = -(-G // 16) * 16
    gain_pieces = gather_column(packed)

    def put_gains(ref, at, gains):
        high = gains.astype(bf16)
        low = (gains - high.astype(f32)).astype(bf16)
        for k, part in enumerate((high, low)):
            ref[k, at : at + X] = jnp.zeros((X, C), bf16)
            ref[k, at : at + G, :blk] = part

    def read_gains(ref, at):
        return sum(ref[k, at : at + G, :blk].astype(f32) for k in range(2))

    def proj_body(cols, *refs):
        gains = sum(ref[...] for ref in refs[NT : 2 * NT])
        b_ref, *rest = refs[2 * NT :]
        rt = jnp.concatenate([ref[:, cols] for ref in refs[:NT]], axis=0).T
        full = mm(rt, b_ref[...])
        if len(rest) == 1:
            for k in range(2):
                rest[0][k, :H] = full[:, k * C : (k + 1) * C].astype(bf16)
            put_gains(rest[0], H, gains)
            return
        got, total_gains, own, *sends = rest
        gains = gains + read_gains(got, H)
        total_gains[...] = gains
        for k in range(2):
            part = full[:, k * C : (k + 1) * C] + got[k, :H].astype(f32)
            own[k] = part[:blk]
            for i, ref in enumerate(sends):
                ref[k, :blk] = part[(i + 1) * blk : (i + 2) * blk].astype(bf16)
        for ref in sends:
            put_gains(ref, blk, gains)

    def half_proj(cols, outs, got):
        return whole_call(
            functools.partial(proj_body, cols),
            outs,
            (*first_pieces, *gain_pieces, both16, *got),
            2 * B * W * C,
            scalars=False,
        )

    (proj_o,) = half_proj(slice(H, W), [sds((2, H + X, C), bf16)], [])
    plane_gains, att_own, *att_sends = half_proj(
        slice(0, H),
        [sds((G, blk), f32), sds((2, blk, C), f32)] + [sds((2, blk + X, C), bf16)] * (N // 2 - 1),
        [plane(proj_o, 1)],
    )
    att_got = [plane(v, 2 * (i + 1)) for i, v in enumerate(att_sends)]

    def att_close_body(gains, own, *refs):
        parts, (out_q, out_p, *out_g) = refs[: len(att_got)], refs[len(att_got) :]
        for k, ref in enumerate((out_q, out_p)):
            total = own[k]
            for p in parts:
                total = total + p[k, :blk].astype(f32)
            ref[...] = total
        total = gains[...] + sum(read_gains(p, blk) for p in parts)
        out_g[0][...] = total[:N]
        out_g[1][...] = total[N : 2 * N]
        out_g[2][...] = total[2 * N : 2 * N + 1, :hw]
        out_g[3][...] = total[2 * N + 1 : 2 * N + 2, :hw]

    grad_query, grad_pairs, *gain_sums = whole_call(
        att_close_body,
        [sds((blk, C), f32)] * 2 + [sds((N, blk), f32)] * 2 + [sds((1, hw), f32)] * 2,
        (plane_gains, att_own, *att_got),
        blk * C * 8,
        scalars=False,
    )

    def out_sum_body(first, *refs):
        parts, outs = refs[: len(out_got)], refs[len(out_got) :]
        total = first[0]
        for p in parts:
            total = total + p[0].astype(f32)
        for k, ref in enumerate(outs):
            ref[...] = total[:, k * C : (k + 1) * C].astype(bf16)

    out_slots = whole_call(
        out_sum_body,
        [sds((blk, C), bf16)] * NT,
        (out_own, *out_got),
        blk * NT * C * 4,
        scalars=False,
    )
    out_pieces = spread_column(out_slots)

    def out_close_body(*refs):
        total = refs[0][...].astype(f32)
        for ref in refs[1:NT]:
            total = total + ref[...].astype(f32)
        refs[NT][...] = total.T

    (grad_output,) = whole_call(
        out_close_body, [sds((C, blk), f32)], out_pieces, blk * C * 4, scalars=False
    )

    def block_body(*refs):
        index = refs[0][0]
        fp, (res, bo) = refs[1 : NT + 1], refs[NT + 1 :]
        block = (res[...] + sum(p[...].astype(f32) for p in fp)).astype(bf16)
        for s, mask in enumerate(masks):
            src = slice(s * blk, (s + 1) * blk)
            if aligned:
                dst = pl.ds(pl.multiple_of((index ^ mask) * blk, blk), blk)
            else:
                dst = src
            bo[:, dst] = block[:, src]

    (block_out,) = whole_call(
        block_body, [sds((R, W), bf16)], (where, *ffn_pieces, resid), R * W * 8
    )

    grad_gate, grad_up, grad_down = close_sum(ffn_own, ffn_got)

    def end_body(*refs):
        s_ref, rest = refs[0], refs[1:]
        gp, (t_ref, gres, g_ref, gt) = rest[:NT], rest[NT:]
        index = s_ref[0]
        grad = sum(p[...].astype(f32) for p in gp)
        x = t_ref[...].astype(f32)
        inv = lax.rsqrt(jnp.mean(x * x, axis=-1, keepdims=True) + epsilon)
        hat = x * inv
        scaled = grad * g_ref[0:1, :]
        total = gres[...] + inv * (scaled - hat * jnp.mean(scaled * hat, axis=-1, keepdims=True))
        for s, mask in enumerate(masks):
            src = slice(s * blk, (s + 1) * blk)
            if aligned:
                dst = pl.ds(pl.multiple_of((index ^ mask) * blk, blk), blk)
            else:
                dst = src
            gt[:, dst] = total[:, src]

    gain_sums = [gain_sums[0].reshape(W), gain_sums[1].reshape(W)] + [
        v.reshape(hw) for v in gain_sums[2:]
    ]
    gna_pieces, gain_sums, grad_down, grad_output, block_out = lax.optimization_barrier(
        (gna_pieces, gain_sums, grad_down, grad_output, block_out)
    )
    (grad_tokens,) = whole_call(
        end_body, [sds((R, W), f32)], (where, *gna_pieces, tok, grad_resid, gain2), R * W * 16
    )
    if not aligned:
        inverse = [masks.index(m) for m in range(N)]
        slot_of = jnp.take(jnp.array(inverse), me ^ jnp.arange(N, dtype=jnp.int32))
        back_cols = lambda v: jnp.take(
            v.reshape(R, N, blk), slot_of, axis=1
        ).reshape(R, W)
        grad_tokens, block_out = back_cols(grad_tokens), back_cols(block_out)

    return (
        block_out[None],
        grad_tokens[None],
        lse_out,
        gain_sums[0],
        grad_query,
        grad_pairs,
        gain_sums[2],
        gain_sums[3],
        grad_output,
        gain_sums[1],
        grad_gate,
        grad_up,
        grad_down,
    )


def solution(mesh):
    in_specs = (
        P("dp", ("ctx", "tp"), None),
        P(),
        P(("dp", "ctx"), "tp"),
        P(("dp", "ctx"), "tp"),
        P(),
        P(),
        P("tp", ("dp", "ctx")),
        P(),
        P(("dp", "ctx"), "tp"),
        P(("dp", "ctx"), "tp"),
        P("tp", ("dp", "ctx")),
        P("dp", ("ctx", "tp"), None),
    )
    out_specs = (
        P("dp", ("ctx", "tp"), None),
        P("dp", ("ctx", "tp"), None),
        P("dp", "tp", "ctx"),
        P(),
        P(("dp", "ctx"), "tp"),
        P(("dp", "ctx"), "tp"),
        P(),
        P(),
        P("tp", ("dp", "ctx")),
        P(),
        P(("dp", "ctx"), "tp"),
        P(("dp", "ctx"), "tp"),
        P("tp", ("dp", "ctx")),
    )

    return jax.shard_map(
        on_device, mesh=mesh, in_specs=in_specs, out_specs=out_specs, check_vma=False
    )
```
